256 devices in a mesh: seq: 32 (over z, x), head: 8 (over y, core).
Axes of the slice: x: 4, y: 4, z: 8, core: 2. Of those that a mesh axis runs over, the one named last changes fastest.
Arguments:
- tokens: bfloat16 [4096, 2048], P('seq'), may hold values from -6.5 to 6.5
- w_query: bfloat16 [2048, 2048], P(None, 'head'), may hold values from -0.125 to 0.125
- w_key: bfloat16 [2048, 4096], P(None, 'head'), may hold values from -0.125 to 0.125
- w_value: bfloat16 [2048, 4096], P(None, 'head'), may hold values from -0.125 to 0.125
- w_beta: bfloat16 [2048, 32], P(None, 'head'), may hold values from -0.150160646 to 0.150160646
- grad_out: bfloat16 [4096, 2048], P('seq', 'head'), may hold values from -6 to 6
Outputs:
- grad_tokens: bfloat16 [4096, 2048], P('seq', 'head')
- grad_w_query: float32 [2048, 2048], P('seq', 'head')
- grad_w_key: float32 [2048, 4096], P('seq', 'head')
- grad_w_value: float32 [2048, 4096], P('seq', 'head')
- grad_w_beta: float32 [2048, 32], P('seq', 'head')
The draws below stay inside these ranges and needn't reach their ends.
All inputs are finite; a program needn't handle non-finite values.
Results may differ from the reference program's by a relative error of at most 0.015.
Values may be sent and summed in bfloat16 or wider, within the bound.
A program may use at most 64 MiB of HBM per device.

```python
import jax
import jax.numpy as jnp
from jax import lax

D = 2048
H = 16
HEAD_SIZE = 128
NH = 2
SPAN = 64
TOKEN_COUNT = 4096


def common_pattern(key):
    signs = jax.random.bernoulli(jax.random.fold_in(key, 7), 0.5, (D,))
    return jnp.where(signs, 1.0, -1.0).astype(jnp.float32)


def draw_tokens(key, part):
    pattern = common_pattern(key)
    noise_key = jax.random.fold_in(key, 11)
    noise = jnp.clip(jax.random.normal(noise_key, (TOKEN_COUNT, D), jnp.float32), -6.0, 6.0)
    along = jnp.dot(noise, pattern, precision=lax.Precision.HIGHEST)
    noise = noise - along[:, None] * pattern[None, :] / D
    segment_length = HEAD_SIZE // 2
    midpoint = TOKEN_COUNT // 2
    leading_segment = jax.random.randint(jax.random.fold_in(key, 13), (), 0, midpoint - segment_length + 1)
    trailing_segment = jax.random.randint(jax.random.fold_in(key, 17), (), midpoint, TOKEN_COUNT - segment_length + 1)
    token_position = jnp.arange(TOKEN_COUNT, dtype=jnp.int32)
    within_segment = (token_position >= leading_segment) & (token_position < leading_segment + segment_length) | (token_position >= trailing_segment) & (token_position < trailing_segment + segment_length)
    strength = jnp.where(within_segment, 0.0, 0.25).astype(jnp.float32)
    return jnp.clip(noise + strength[:, None] * pattern[None, :], -6.5, 6.5).astype(jnp.bfloat16)


def draw_w_beta(key, part):
    pattern = common_pattern(key)
    chance = 0.5
    flagged = jax.random.bernoulli(jax.random.fold_in(key, 23), chance, (H,))
    chosen_head = jax.random.randint(jax.random.fold_in(key, 29), (), 0, H)
    lasting = flagged | (jnp.arange(H, dtype=jnp.int32) == chosen_head)
    factor = jnp.exp(jax.random.uniform(jax.random.fold_in(key, 37), (H,), jnp.float32, jnp.log(0.2), jnp.log(1.0)))
    target = factor * HEAD_SIZE / (NH * TOKEN_COUNT)
    offset = jnp.log(2.0 / target - 1.0)
    lasting_cols = jnp.repeat(lasting, NH)
    offset_cols = jnp.repeat(offset, NH)
    noise = jnp.clip(jax.random.normal(jax.random.fold_in(key, 31), (D, H * NH), jnp.float32), -4.0, 4.0)
    lasting_weight = -offset_cols[None, :] * pattern[:, None] / (0.25 * D) + 0.5 * noise / D ** 0.5
    drawn_weight = noise / D ** 0.5
    weight = jnp.where(lasting_cols[None, :], lasting_weight, drawn_weight)
    limit = (36.0 + 6.0 * D ** 0.5) / D
    return jnp.clip(weight, -limit, limit).astype(jnp.bfloat16)


def steps_of(stream_key, dims, cuts, smallest, high):
    gain = 1.0
    for axis_at, parts in cuts:
        draws = jax.random.uniform(jax.random.fold_in(jax.random.fold_in(stream_key, 6), axis_at), (parts,), jnp.float32, smallest / len(cuts), high / len(cuts))
        gain = gain * jnp.repeat(jnp.exp(draws), dims[axis_at] // parts).reshape((-1,) + (1,) * (len(dims) - 1 - axis_at))
    return gain


def scatter_about(stream_key, dims, width, bound, cuts=(), kind=jnp.bfloat16):
    result = width * jax.random.normal(stream_key, dims, jnp.float32)
    if cuts:
        result = result * steps_of(stream_key, dims, cuts, -0.22, 0.18)
    return jnp.clip(result, -bound, bound).astype(kind)


def setup_inputs(seed: int = 0) -> dict:
    arg_keys = jax.random.split(jax.random.key(seed), 7)
    return {
        "tokens": draw_tokens(jax.random.fold_in(arg_keys[6], 71), 0),
        "w_query": scatter_about(arg_keys[1], (D, H * HEAD_SIZE), D ** -0.5, 0.125, ((1, 8),)),
        "w_key": scatter_about(arg_keys[2], (D, H * NH * HEAD_SIZE), D ** -0.5, 0.125, ((1, 8),)),
        "w_value": scatter_about(arg_keys[3], (D, H * NH * HEAD_SIZE), D ** -0.5, 0.125, ((1, 8),)),
        "w_beta": draw_w_beta(jax.random.fold_in(arg_keys[6], 71), 0),
        "grad_out": scatter_about(arg_keys[5], (TOKEN_COUNT, H * HEAD_SIZE), 1.0, 6.0, ((0, 32), (1, 8))),
    }


highest = lax.Precision.HIGHEST
epsilon = 1e-06

def product(left, right):
    return jnp.matmul(left, right, precision=highest)

def normalize(matrix):
    return matrix * lax.rsqrt(lax.optimization_barrier(jnp.sum(matrix * matrix, axis=-1, keepdims=True)) + epsilon)

def span_update(carry_state, pieces):
    query_rows, key_rows, value_rows, beta_rows = pieces
    step_count = key_rows.shape[0]
    row_count = query_rows.shape[0]
    key_gram = beta_rows[:, None] * product(key_rows, key_rows.T)
    system = jnp.eye(step_count, dtype=key_gram.dtype) + jnp.tril(key_gram, -1)
    weighting = lax.linalg.triangular_solve(system, jnp.diag(beta_rows), left_side=True, lower=True, unit_diagonal=True)
    w_rows = product(weighting, key_rows)
    new_values = product(weighting, value_rows) - product(w_rows, carry_state)
    column_token = lax.broadcasted_iota(jnp.int32, (row_count, step_count), 1) // (step_count // row_count)
    row_token = lax.broadcasted_iota(jnp.int32, (row_count, step_count), 0)
    scores = jnp.where(column_token <= row_token, product(query_rows, key_rows.T), 0.0)
    outputs = product(query_rows, carry_state) + product(scores, new_values)
    return (carry_state + product(key_rows.T, new_values), outputs)

def head_run(start_state, query_rows, key_rows, value_rows, beta_rows):
    blocks = query_rows.shape[0] // SPAN
    pieces = (query_rows.reshape(blocks, SPAN, HEAD_SIZE), key_rows.reshape(blocks, SPAN * NH, HEAD_SIZE), value_rows.reshape(blocks, SPAN * NH, HEAD_SIZE), beta_rows.reshape(blocks, SPAN * NH))
    end_state, outputs = lax.scan(span_update, start_state, pieces)
    return (end_state, outputs.reshape(blocks * SPAN, HEAD_SIZE))

def recurrence(proj_query, proj_key, proj_value, proj_beta, start_state):
    head_count = start_state.shape[0]
    row_count = proj_query.shape[0]
    queries = normalize(proj_query.reshape(row_count, head_count, HEAD_SIZE)).transpose(1, 0, 2)
    key_rows = normalize(proj_key.reshape(row_count, head_count, NH, HEAD_SIZE)).transpose(1, 0, 2, 3).reshape(head_count, row_count * NH, HEAD_SIZE)
    value_rows = proj_value.reshape(row_count, head_count, NH, HEAD_SIZE).transpose(1, 0, 2, 3).reshape(head_count, row_count * NH, HEAD_SIZE)
    beta_rows = (2.0 * jax.nn.sigmoid(proj_beta)).reshape(row_count, head_count, NH).transpose(1, 0, 2).reshape(head_count, row_count * NH)
    end_states, outputs = jax.vmap(head_run)(start_state, queries, key_rows, value_rows, beta_rows)
    return (outputs.transpose(1, 0, 2).reshape(row_count, head_count * HEAD_SIZE), end_states)

def reference(tokens, w_query, w_key, w_value, w_beta, grad_out):
    weights = (w_query, w_key, w_value, w_beta)
    projected = tuple((jnp.dot(tokens.astype(jnp.float32), matrix.astype(jnp.float32), preferred_element_type=jnp.float32) for matrix in weights))
    zero_state = jnp.zeros((H, HEAD_SIZE, HEAD_SIZE), jnp.float32)

    def forward(proj_query, proj_key, proj_value, proj_beta):
        return recurrence(proj_query, proj_key, proj_value, proj_beta, zero_state)[0]
    outputs, pullback = jax.vjp(forward, projected[0], projected[1], projected[2], projected[3])
    gradients = pullback(grad_out.astype(jnp.float32))
    rounded = tuple((gradient.astype(jnp.bfloat16) for gradient in gradients))
    weight_grads = tuple((lax.dot_general(tokens.astype(jnp.float32), gradient.astype(jnp.float32), (((0,), (0,)), ((), ())), preferred_element_type=jnp.float32) for gradient in rounded))
    input_term = lax.dot_general(rounded[0].astype(jnp.float32), w_query.astype(jnp.float32), (((1,), (1,)), ((), ())), preferred_element_type=jnp.float32)
    input_term = input_term + lax.dot_general(rounded[1].astype(jnp.float32), w_key.astype(jnp.float32), (((1,), (1,)), ((), ())), preferred_element_type=jnp.float32)
    input_term = input_term + lax.dot_general(rounded[2].astype(jnp.float32), w_value.astype(jnp.float32), (((1,), (1,)), ((), ())), preferred_element_type=jnp.float32)
    input_term = input_term + lax.dot_general(rounded[3].astype(jnp.float32), w_beta.astype(jnp.float32), (((1,), (1,)), ((), ())), preferred_element_type=jnp.float32)
    return (input_term.astype(jnp.bfloat16), weight_grads[0], weight_grads[1], weight_grads[2], weight_grads[3])
```

```python
import functools

import jax
import jax.numpy as jnp
from jax import lax
from jax.experimental import pallas as pl
from jax.experimental.pallas import tpu as pltpu
from jax.sharding import PartitionSpec as P

HEAD_SIZE = 128
NH = 2
XN = 4
EPS = 1e-6
MESH = pl.DeviceIdType.MESH
F32 = jnp.float32
BF16 = jnp.bfloat16

NN = ((1,), (0,))
NT = ((1,), (1,))
TN = ((0,), (0,))


def dg(left, right, dims):
    return lax.dot_general(left, right, (dims, ((), ())), preferred_element_type=F32)


def parts(array):
    if isinstance(array, tuple):
        return array
    if array.dtype == BF16:
        return (array,)
    high = array.astype(BF16)
    return (high, (array - high.astype(F32)).astype(BF16))


def mm(left, right, dims=NN):
    left, right = parts(left), parts(right)
    total = dg(left[0], right[0], dims)
    if len(right) > 1:
        total = total + dg(left[0], right[1], dims)
    if len(left) > 1:
        total = total + dg(left[1], right[0], dims)
    return total


def order_masks(tokens):
    rows = NH * tokens
    row = lax.broadcasted_iota(jnp.int32, (rows, rows), 0)
    col = lax.broadcasted_iota(jnp.int32, (rows, rows), 1)
    row_token, col_token = row & (tokens - 1), col & (tokens - 1)
    row_step, col_step = row >= tokens, col >= tokens
    return row, col, row_token, col_token, row_step, col_step


def score_mask(tokens):
    row = lax.broadcasted_iota(jnp.int32, (tokens, NH * tokens), 0)
    col = lax.broadcasted_iota(jnp.int32, (tokens, NH * tokens), 1)
    return (col & (tokens - 1)) <= row


def unit(matrix):
    scale = lax.rsqrt(jnp.sum(matrix * matrix, axis=-1, keepdims=True) + EPS)
    return matrix * scale, scale


def front_kernel(
    heads,
    tokens_ref,
    wq_ref,
    wk_ref,
    wv_ref,
    wb_ref,
    go_ref,
    a_ref,
    bt_ref,
    lt_ref,
    q_ref,
    k_ref,
    v_ref,
    u_ref,
    w_ref,
    x_ref,
    pg_ref,
    col_ref,
):
    size = HEAD_SIZE
    tok = tokens_ref[...]
    count = tok.shape[0]
    pq = dg(tok, wq_ref[...], NN)
    pk = dg(tok, wk_ref[...], NN)
    pv = dg(tok, wv_ref[...], NN)
    pb = dg(tok, wb_ref[...], NN)
    beta_all = 2.0 * jax.nn.sigmoid(pb)
    row, col, row_token, col_token, row_step, col_step = order_masks(count)
    strict = (col_token < row_token) | ((col_token == row_token) & row_step & ~col_step)
    smask = score_mask(count)
    eye = jnp.where(row == col, 1.0, 0.0)
    keys, values, betas, systems, inverses = [], [], [], [], []
    for h in range(heads):
        base = h * NH * size
        both = jnp.concatenate([pk[:, base : base + size], pk[:, base + size : base + 2 * size]], axis=0)
        key, key_scale = unit(both)
        value = jnp.concatenate([pv[:, base : base + size], pv[:, base + size : base + 2 * size]], axis=0)
        beta = jnp.concatenate([beta_all[:, 2 * h : 2 * h + 1], beta_all[:, 2 * h + 1 : 2 * h + 2]], axis=0)
        k_ref[h] = key
        v_ref[h] = value
        col_ref[h, :, 0:1] = beta
        col_ref[h, :, 1:2] = key_scale
        gram = mm(key, key, NT)
        system = jnp.where(strict, beta * gram, 0.0)
        keys.append(key)
        values.append(value)
        betas.append(beta)
        systems.append(system)
        inverses.append(eye - jnp.where(col_token == row_token, system, 0.0))
    level = 1
    while level < count:
        pick = ((row_token & (2 * level - 1)) >= level) & ((col_token | (2 * level - 1)) == (row_token | (2 * level - 1))) & (
            (col_token & (2 * level - 1)) < level
        )
        for h in range(heads):
            inverse = parts(inverses[h])
            inner = mm(jnp.where(pick, systems[h], 0.0), inverse)
            inverses[h] = inverses[h] - mm(inverse, inner)
        level *= 2
    small = jnp.where(
        lax.broadcasted_iota(jnp.int32, (size, size), 0) == lax.broadcasted_iota(jnp.int32, (size, size), 1), 1.0, 0.0
    )
    for h in range(heads):
        key, value, beta, inverse = keys[h], values[h], betas[h], inverses[h]
        x_ref[h] = inverse
        inverse = parts(inverse)
        w_rows = mm(inverse, beta * key)
        u_rows = mm(inverse, beta * value)
        query, query_scale = unit(pq[:, h * size : (h + 1) * size])
        go = go_ref[:, h * size : (h + 1) * size]
        key = parts(key)
        scores = jnp.where(smask, mm(query, key, NT), 0.0)
        pulled = mm(scores, go, TN)
        w_parts = parts(w_rows)
        a_ref[h] = small - mm(key, w_parts, TN)
        bt_ref[h] = mm(u_rows, key, TN)
        lt_ref[h] = mm(go, query, TN) - mm(pulled, w_parts, TN)
        q_ref[h] = query
        u_ref[h] = u_rows
        w_ref[h] = w_rows
        pg_ref[h] = pulled
        col_ref[h, 0:count, 2:3] = query_scale


def scan_kernel(
    zn,
    a_ref,
    bt_ref,
    lt_ref,
    s0_ref,
    d0_ref,
    abuf,
    bbuf,
    lbuf,
    s_in,
    d_in,
    s_out,
    d_out,
    s_put,
    d_put,
    s_got,
    d_got,
    pre,
    xsend,
    xrecv,
    zsend,
    zrecv,
    psend,
    precv,
):
    seq, head = lax.axis_index("seq"), lax.axis_index("head")
    z, x = lax.div(seq, XN), lax.rem(seq, XN)
    heads, size = a_ref.shape[0], a_ref.shape[1]
    quarter = size // XN
    peers = [lax.rem(x + d, XN) for d in range(1, XN)]
    above = lax.rem(z + 1, zn)
    below = lax.rem(z + zn - 1, zn)

    def at(zz, xx):
        return (zz * XN + xx, head)

    barrier = pltpu.get_barrier_semaphore()
    for peer in peers:
        pl.semaphore_signal(barrier, inc=1, device_id=at(z, peer), device_id_type=MESH)
    for other in (above, below):
        pl.semaphore_signal(barrier, inc=1, device_id=at(other, x), device_id_type=MESH)
    pl.semaphore_wait(barrier, XN + 1)

    copies = []
    for i, peer in enumerate(peers):
        rows = pl.ds(pl.multiple_of(peer * quarter, quarter), quarter)
        for kind, (src, dst) in enumerate(
            ((a_ref, abuf.at[x]), (bt_ref.at[:, rows, :], bbuf.at[x]), (lt_ref.at[:, rows, :], lbuf.at[x]))
        ):
            copy = pltpu.make_async_remote_copy(
                src_ref=src,
                dst_ref=dst,
                send_sem=xsend.at[i, kind],
                recv_sem=xrecv.at[i, kind],
                device_id=at(z, peer),
                device_id_type=MESH,
            )
            copy.start()
            copies.append(copy)
    mine = pl.ds(pl.multiple_of(x * quarter, quarter), quarter)
    abuf[x] = a_ref[...]
    bbuf[x] = bt_ref[:, mine, :]
    lbuf[x] = lt_ref[:, mine, :]

    @pl.when(z == 0)
    def _():
        s_in[...] = jnp.zeros_like(s_in)

    @pl.when(z == zn - 1)
    def _():
        d_in[...] = jnp.zeros_like(d_in)

    for copy in copies:
        copy.wait()

    for h in range(heads):
        maps = [parts(abuf[j, h]) for j in range(XN)]
        p10 = mm(maps[1], maps[0])
        p32 = mm(maps[3], maps[2])
        p10s, p32s = parts(p10), parts(p32)
        p210 = mm(maps[2], p10s)
        p321 = mm(p32s, maps[1])
        total = mm(p32s, p10s)
        pre[h, 0] = abuf[0, h]
        pre[h, 1] = p10
        pre[h, 2] = p210
        pre[h, 3] = total
        pre[h, 4] = abuf[3, h]
        pre[h, 5] = p32
        pre[h, 6] = p321
        off = bbuf[0, h]
        s_put[1, h] = off
        for j in range(1, XN):
            off = mm(off, maps[j], NT) + bbuf[j, h]
            if j + 1 < XN:
                s_put[j + 1, h] = off
            else:
                s_out[h] = off
        off = lbuf[XN - 1, h]
        d_put[XN - 2, h] = off
        for j in range(XN - 2, -1, -1):
            off = mm(off, maps[j], NN) + lbuf[j, h]
            if j > 0:
                d_put[j - 1, h] = off
            else:
                d_out[h] = off

    s_hop = pltpu.make_async_remote_copy(
        src_ref=s_out, dst_ref=s_in, send_sem=zsend.at[0], recv_sem=zrecv.at[0], device_id=at(above, x), device_id_type=MESH
    )
    d_hop = pltpu.make_async_remote_copy(
        src_ref=d_out, dst_ref=d_in, send_sem=zsend.at[1], recv_sem=zrecv.at[1], device_id=at(below, x), device_id_type=MESH
    )

    def hand_out(put, got, kind):
        for i, peer in enumerate(peers):
            pltpu.make_async_remote_copy(
                src_ref=put.at[peer],
                dst_ref=got.at[x],
                send_sem=psend.at[i, kind],
                recv_sem=precv.at[i, kind],
                device_id=at(z, peer),
                device_id_type=MESH,
            ).start()
        got[x] = put[x]

    def forward():
        @pl.when(z > 0)
        def _():
            s_hop.wait_recv()

        @pl.when(z < zn - 1)
        def _():
            for h in range(heads):
                s_out[h] = s_out[h] + mm(s_in[h], pre[h, 3], NT)
            s_hop.start()

        for h in range(heads):
            state = s_in[h]
            pieces = parts(state)
            s_put[0, h] = state
            for j in range(1, XN):
                s_put[j, h] = s_put[j, h] + mm(pieces, pre[h, j - 1], NT)
        hand_out(s_put, s_got, 0)

    def backward():
        @pl.when(z < zn - 1)
        def _():
            d_hop.wait_recv()

        @pl.when(z > 0)
        def _():
            for h in range(heads):
                d_out[h] = d_out[h] + mm(d_in[h], pre[h, 3], NN)
            d_hop.start()

        for h in range(heads):
            state = d_in[h]
            pieces = parts(state)
            d_put[XN - 1, h] = state
            for j in range(XN - 1):
                d_put[j, h] = d_put[j, h] + mm(pieces, pre[h, 6 - j], NN)
        hand_out(d_put, d_got, 1)

    @pl.when(z < zn // 2)
    def _():
        forward()
        backward()

    @pl.when(z >= zn // 2)
    def _():
        backward()
        forward()

    @pl.when(z < zn - 1)
    def _():
        s_hop.wait_send()

    @pl.when(z > 0)
    def _():
        d_hop.wait_send()

    for kind, (put, got) in enumerate(((s_put, s_got), (d_put, d_got))):
        for i, peer in enumerate(peers):
            pltpu.make_async_remote_copy(
                src_ref=put.at[peer],
                dst_ref=got.at[x],
                send_sem=psend.at[i, kind],
                recv_sem=precv.at[i, kind],
                device_id=at(z, peer),
                device_id_type=MESH,
            ).wait()
    for j in range(XN):
        for h in range(heads):
            s0_ref[h, j * quarter : (j + 1) * quarter, :] = s_got[j, h]
            d0_ref[h, j * quarter : (j + 1) * quarter, :] = d_got[j, h]


def back_kernel(heads, q_ref, k_ref, v_ref, u_ref, w_ref, x_ref, pg_ref, col_ref, go_ref, s0_ref, d0_ref, gq_ref, gk_ref, gv_ref, gb_ref):
    size = HEAD_SIZE
    count = q_ref.shape[1]
    row, col, row_token, col_token, row_step, col_step = order_masks(count)
    strict = (col_token < row_token) | ((col_token == row_token) & row_step & ~col_step)
    smask = score_mask(count)
    for h in range(heads):
        query, key, value = q_ref[h], k_ref[h], v_ref[h]
        beta, key_scale = col_ref[h, :, 0:1], col_ref[h, :, 1:2]
        query_scale = col_ref[h, 0:count, 2:3]
        go = go_ref[:, h * size : (h + 1) * size]
        state, adjoint = parts(s0_ref[h]), parts(d0_ref[h])
        keys = parts(key)
        fresh = u_ref[h] - mm(w_ref[h], state, NT)
        rest = value - mm(keys, state, NT)
        d_fresh = pg_ref[h] + mm(keys, adjoint, NT)
        solved = mm(x_ref[h], d_fresh, TN)
        fresh_parts = parts(fresh)
        d_scores = parts(jnp.where(smask, mm(go, fresh_parts, NT), 0.0))
        d_system = jnp.where(strict, -mm(solved, fresh_parts, NT), 0.0)
        d_rest = beta * solved
        gram = mm(keys, keys, NT)
        d_beta = jnp.sum(solved * rest, axis=-1, keepdims=True) + jnp.sum(d_system * gram, axis=-1, keepdims=True)
        d_gram = parts(beta * d_system)
        d_query = mm(go, state) + mm(d_scores, keys)
        d_key = (
            mm(d_scores, query, TN)
            + mm(fresh_parts, adjoint)
            - mm(d_rest, state)
            + mm(d_gram, keys)
            + mm(d_gram, keys, TN)
        )
        d_query = query_scale * (d_query - query * jnp.sum(query * d_query, axis=-1, keepdims=True))
        d_key = key_scale * (d_key - key * jnp.sum(key * d_key, axis=-1, keepdims=True))
        d_logit = d_beta * beta * (1.0 - 0.5 * beta)
        gq_ref[:, h * size : (h + 1) * size] = d_query.astype(BF16)
        for j in range(NH):
            at = (h * NH + j) * size
            gk_ref[:, at : at + size] = d_key[j * count : (j + 1) * count].astype(BF16)
            gv_ref[:, at : at + size] = d_rest[j * count : (j + 1) * count].astype(BF16)
            gb_ref[:, h * NH + j : h * NH + j + 1] = d_logit[j * count : (j + 1) * count].astype(BF16)


def vmem(count):
    return [pl.BlockSpec(memory_space=pltpu.VMEM)] * count


def per_device(tokens, w_query, w_key, w_value, w_beta, grad_out):
    count = tokens.shape[0]
    size = HEAD_SIZE
    heads = w_query.shape[1] // size
    rows = NH * count
    quarter = size // XN
    zn = lax.axis_size("seq") // XN
    f32 = lambda *shape: jax.ShapeDtypeStruct(shape, F32)
    bf16 = lambda *shape: jax.ShapeDtypeStruct(shape, BF16)
    square = f32(heads, size, size)
    steps = f32(heads, rows, size)
    a, bt, lt, q, k, v, u, w, x, pg, cols = pl.pallas_call(
        functools.partial(front_kernel, heads),
        out_shape=(
            square,
            square,
            square,
            f32(heads, count, size),
            steps,
            steps,
            steps,
            steps,
            f32(heads, rows, rows),
            steps,
            f32(heads, rows, 8),
        ),
        in_specs=vmem(6),
        out_specs=tuple(vmem(11)),
        name="front",
    )(tokens, w_query, w_key, w_value, w_beta, grad_out)
    s0, d0 = pl.pallas_call(
        functools.partial(scan_kernel, zn),
        out_shape=(square, square),
        in_specs=vmem(3),
        out_specs=tuple(vmem(2)),
        scratch_shapes=[
            pltpu.VMEM((XN, heads, size, size), F32),
            pltpu.VMEM((XN, heads, quarter, size), F32),
            pltpu.VMEM((XN, heads, quarter, size), F32),
            pltpu.VMEM((heads, quarter, size), F32),
            pltpu.VMEM((heads, quarter, size), F32),
            pltpu.VMEM((heads, quarter, size), F32),
            pltpu.VMEM((heads, quarter, size), F32),
            pltpu.VMEM((XN, heads, quarter, size), F32),
            pltpu.VMEM((XN, heads, quarter, size), F32),
            pltpu.VMEM((XN, heads, quarter, size), F32),
            pltpu.VMEM((XN, heads, quarter, size), F32),
            pltpu.VMEM((heads, 7, size, size), F32),
            pltpu.SemaphoreType.DMA((XN - 1, 3)),
            pltpu.SemaphoreType.DMA((XN - 1, 3)),
            pltpu.SemaphoreType.DMA((2,)),
            pltpu.SemaphoreType.DMA((2,)),
            pltpu.SemaphoreType.DMA((XN - 1, 2)),
            pltpu.SemaphoreType.DMA((XN - 1, 2)),
        ],
        compiler_params=pltpu.CompilerParams(collective_id=0, has_side_effects=True),
        name="scan",
    )(a, bt, lt)
    gq, gk, gv, gb = pl.pallas_call(
        functools.partial(back_kernel, heads),
        out_shape=(
            bf16(count, heads * size),
            bf16(count, heads * NH * size),
            bf16(count, heads * NH * size),
            bf16(count, heads * NH),
        ),
        in_specs=vmem(11),
        out_specs=tuple(vmem(4)),
        name="back",
    )(q, k, v, u, w, x, pg, cols, grad_out, s0, d0)

    rounded = (gq, gk, gv, gb)
    weights = (w_query, w_key, w_value, w_beta)
    grad_all = jnp.concatenate(rounded, axis=1)
    summed = lax.psum_scatter(
        lax.dot_general(tokens, grad_all, (((0,), (0,)), ((), ())), preferred_element_type=F32).astype(BF16),
        "seq",
        scatter_dimension=0,
        tiled=True,
    ).astype(F32)
    first = gq.shape[1]
    second = first + gk.shape[1]
    third = second + gv.shape[1]
    input_term = sum(dg(g, wt, NT) for g, wt in zip(rounded, weights))
    grad_tokens = lax.psum_scatter(input_term.astype(BF16), "head", scatter_dimension=1, tiled=True)
    return (grad_tokens, summed[:, :first], summed[:, first:second], summed[:, second:third], summed[:, third:])


def solution(mesh):
    in_specs = (
        P("seq", None),
        P(None, "head"),
        P(None, "head"),
        P(None, "head"),
        P(None, "head"),
        P("seq", "head"),
    )
    return jax.shard_map(
        per_device, mesh=mesh, in_specs=in_specs, out_specs=(P("seq", "head"),) * 5, check_vma=False
    )
```

```python
import functools

import jax
import jax.numpy as jnp
from jax import lax
from jax.experimental import pallas as pl
from jax.experimental.pallas import tpu as pltpu
from jax.sharding import PartitionSpec as P

HEAD_SIZE = 128
NH = 2
XN = 4
EPS = 1e-6
MESH = pl.DeviceIdType.MESH
F32 = jnp.float32
BF16 = jnp.bfloat16

NN = ((1,), (0,))
NT = ((1,), (1,))
TN = ((0,), (0,))


def dg(left, right, dims):
    return lax.dot_general(left, right, (dims, ((), ())), preferred_element_type=F32)


def parts(array):
    if isinstance(array, tuple):
        return array
    if array.dtype == BF16:
        return (array,)
    high = array.astype(BF16)
    return (high, (array - high.astype(F32)).astype(BF16))


def mm(left, right, dims=NN):
    left, right = parts(left), parts(right)
    total = dg(left[0], right[0], dims)
    if len(right) > 1:
        total = total + dg(left[0], right[1], dims)
    if len(left) > 1:
        total = total + dg(left[1], right[0], dims)
    return total


def order_masks(tokens):
    rows = NH * tokens
    row = lax.broadcasted_iota(jnp.int32, (rows, rows), 0)
    col = lax.broadcasted_iota(jnp.int32, (rows, rows), 1)
    row_token, col_token = row & (tokens - 1), col & (tokens - 1)
    row_step, col_step = row >= tokens, col >= tokens
    return row, col, row_token, col_token, row_step, col_step


def score_mask(tokens):
    row = lax.broadcasted_iota(jnp.int32, (tokens, NH * tokens), 0)
    col = lax.broadcasted_iota(jnp.int32, (tokens, NH * tokens), 1)
    return (col & (tokens - 1)) <= row


def unit(matrix):
    scale = lax.rsqrt(jnp.sum(matrix * matrix, axis=-1, keepdims=True) + EPS)
    return matrix * scale, scale


def front_kernel(
    heads,
    tokens_ref,
    wq_ref,
    wk_ref,
    wv_ref,
    wb_ref,
    go_ref,
    a_ref,
    bt_ref,
    lt_ref,
    q_ref,
    k_ref,
    v_ref,
    u_ref,
    w_ref,
    x_ref,
    pg_ref,
    col_ref,
):
    size = HEAD_SIZE
    tok = tokens_ref[...]
    count = tok.shape[0]
    pq = dg(tok, wq_ref[...], NN)
    pk = dg(tok, wk_ref[...], NN)
    pv = dg(tok, wv_ref[...], NN)
    pb = dg(tok, wb_ref[...], NT)
    beta_all = 2.0 * jax.nn.sigmoid(pb)
    row, col, row_token, col_token, row_step, col_step = order_masks(count)
    strict = (col_token < row_token) | ((col_token == row_token) & row_step & ~col_step)
    smask = score_mask(count)
    eye = jnp.where(row == col, 1.0, 0.0)
    keys, values, betas, systems, inverses = [], [], [], [], []
    for h in range(heads):
        base = h * NH * size
        both = jnp.concatenate([pk[:, base : base + size], pk[:, base + size : base + 2 * size]], axis=0)
        key, key_scale = unit(both)
        value = jnp.concatenate([pv[:, base : base + size], pv[:, base + size : base + 2 * size]], axis=0)
        beta = jnp.concatenate([beta_all[:, 2 * h : 2 * h + 1], beta_all[:, 2 * h + 1 : 2 * h + 2]], axis=0)
        k_ref[h] = key
        v_ref[h] = value
        col_ref[h, :, 0:1] = beta
        col_ref[h, :, 1:2] = key_scale
        gram = mm(key, key, NT)
        system = jnp.where(strict, beta * gram, 0.0)
        keys.append(key)
        values.append(value)
        betas.append(beta)
        systems.append(system)
        inverses.append(eye - jnp.where(col_token == row_token, system, 0.0))
    level = 1
    while level < count:
        pick = ((row_token & (2 * level - 1)) >= level) & ((col_token | (2 * level - 1)) == (row_token | (2 * level - 1))) & (
            (col_token & (2 * level - 1)) < level
        )
        for h in range(heads):
            inverse = parts(inverses[h])
            inner = mm(jnp.where(pick, systems[h], 0.0), inverse)
            inverses[h] = inverses[h] - mm(inverse, inner)
        level *= 2
    small = jnp.where(
        lax.broadcasted_iota(jnp.int32, (size, size), 0) == lax.broadcasted_iota(jnp.int32, (size, size), 1), 1.0, 0.0
    )
    for h in range(heads):
        key, value, beta, inverse = keys[h], values[h], betas[h], inverses[h]
        x_ref[h] = inverse
        inverse = parts(inverse)
        w_rows = mm(inverse, beta * key)
        u_rows = mm(inverse, beta * value)
        query, query_scale = unit(pq[:, h * size : (h + 1) * size])
        go = go_ref[:, h * size : (h + 1) * size]
        key = parts(key)
        scores = jnp.where(smask, mm(query, key, NT), 0.0)
        pulled = mm(scores, go, TN)
        w_parts = parts(w_rows)
        a_ref[h] = small - mm(key, w_parts, TN)
        bt_ref[h] = mm(u_rows, key, TN)
        lt_ref[h] = mm(go, query, TN) - mm(pulled, w_parts, TN)
        q_ref[h] = query
        u_ref[h] = u_rows
        w_ref[h] = w_rows
        pg_ref[h] = pulled
        col_ref[h, 0:count, 2:3] = query_scale


def scan_kernel(
    zn,
    a_ref,
    bt_ref,
    lt_ref,
    tok_ref,
    s0_ref,
    d0_ref,
    tt_ref,
    abuf,
    bbuf,
    lbuf,
    s_in,
    d_in,
    s_out,
    d_out,
    s_put,
    d_put,
    s_got,
    d_got,
    pre,
    xsend,
    xrecv,
    zsend,
    zrecv,
    psend,
    precv,
    tokt,
    ttbuf,
    tsend,
    trecv,
):
    seq, head = lax.axis_index("seq"), lax.axis_index("head")
    z, x = lax.div(seq, XN), lax.rem(seq, XN)
    heads, size = a_ref.shape[0], a_ref.shape[1]
    quarter = size // XN
    peers = [lax.rem(x + d, XN) for d in range(1, XN)]
    above = lax.rem(z + 1, zn)
    below = lax.rem(z + zn - 1, zn)

    def at(zz, xx):
        return (zz * XN + xx, head)

    barrier = pltpu.get_barrier_semaphore()
    for peer in peers:
        pl.semaphore_signal(barrier, inc=1, device_id=at(z, peer), device_id_type=MESH)
    for other in (above, below):
        pl.semaphore_signal(barrier, inc=1, device_id=at(other, x), device_id_type=MESH)
    pl.semaphore_wait(barrier, XN + 1)

    copies = []
    for i, peer in enumerate(peers):
        rows = pl.ds(pl.multiple_of(peer * quarter, quarter), quarter)
        for kind, (src, dst) in enumerate(
            ((a_ref, abuf.at[x]), (bt_ref.at[:, rows, :], bbuf.at[x]), (lt_ref.at[:, rows, :], lbuf.at[x]))
        ):
            copy = pltpu.make_async_remote_copy(
                src_ref=src,
                dst_ref=dst,
                send_sem=xsend.at[i, kind],
                recv_sem=xrecv.at[i, kind],
                device_id=at(z, peer),
                device_id_type=MESH,
            )
            copy.start()
            copies.append(copy)
    mine = pl.ds(pl.multiple_of(x * quarter, quarter), quarter)
    abuf[x] = a_ref[...]
    bbuf[x] = bt_ref[:, mine, :]
    lbuf[x] = lt_ref[:, mine, :]

    @pl.when(z == 0)
    def _():
        s_in[...] = jnp.zeros_like(s_in)

    @pl.when(z == zn - 1)
    def _():
        d_in[...] = jnp.zeros_like(d_in)

    rows = tok_ref.shape[1] // (zn * XN)
    for zz in range(zn):
        block = tok_ref[:, zz * XN * rows : (zz + 1) * XN * rows]
        tokt[zz] = block.T.reshape(XN, rows, block.shape[0])

    for copy in copies:
        copy.wait()

    count = tok_ref.shape[0]
    lanes = pl.ds(pl.multiple_of(x * count, count), count)
    t_copies = []
    for i, peer in enumerate(peers):
        copy = pltpu.make_async_remote_copy(
            src_ref=tokt.at[:, peer],
            dst_ref=ttbuf.at[:, :, lanes],
            send_sem=tsend.at[i],
            recv_sem=trecv.at[i],
            device_id=at(z, peer),
            device_id_type=MESH,
        )
        copy.start()
        t_copies.append(copy)
    ttbuf[:, :, lanes] = tokt[:, x]

    for h in range(heads):
        maps = [parts(abuf[j, h]) for j in range(XN)]
        p10 = mm(maps[1], maps[0])
        p32 = mm(maps[3], maps[2])
        p10s, p32s = parts(p10), parts(p32)
        p210 = mm(maps[2], p10s)
        p321 = mm(p32s, maps[1])
        total = mm(p32s, p10s)
        pre[h, 0] = abuf[0, h]
        pre[h, 1] = p10
        pre[h, 2] = p210
        pre[h, 3] = total
        pre[h, 4] = abuf[3, h]
        pre[h, 5] = p32
        pre[h, 6] = p321
        off = bbuf[0, h]
        s_put[1, h] = off
        for j in range(1, XN):
            off = mm(off, maps[j], NT) + bbuf[j, h]
            if j + 1 < XN:
                s_put[j + 1, h] = off
            else:
                s_out[h] = off
        off = lbuf[XN - 1, h]
        d_put[XN - 2, h] = off
        for j in range(XN - 2, -1, -1):
            off = mm(off, maps[j], NN) + lbuf[j, h]
            if j > 0:
                d_put[j - 1, h] = off
            else:
                d_out[h] = off

    s_hop = pltpu.make_async_remote_copy(
        src_ref=s_out, dst_ref=s_in, send_sem=zsend.at[0], recv_sem=zrecv.at[0], device_id=at(above, x), device_id_type=MESH
    )
    d_hop = pltpu.make_async_remote_copy(
        src_ref=d_out, dst_ref=d_in, send_sem=zsend.at[1], recv_sem=zrecv.at[1], device_id=at(below, x), device_id_type=MESH
    )

    def hand_out(put, got, kind):
        for i, peer in enumerate(peers):
            pltpu.make_async_remote_copy(
                src_ref=put.at[peer],
                dst_ref=got.at[x],
                send_sem=psend.at[i, kind],
                recv_sem=precv.at[i, kind],
                device_id=at(z, peer),
                device_id_type=MESH,
            ).start()
        got[x] = put[x]

    def forward():
        @pl.when(z > 0)
        def _():
            s_hop.wait_recv()

        @pl.when(z < zn - 1)
        def _():
            for h in range(heads):
                s_out[h] = s_out[h] + mm(s_in[h], pre[h, 3], NT)
            s_hop.start()

        for h in range(heads):
            state = s_in[h]
            pieces = parts(state)
            s_put[0, h] = state
            for j in range(1, XN):
                s_put[j, h] = s_put[j, h] + mm(pieces, pre[h, j - 1], NT)
        hand_out(s_put, s_got, 0)

    def backward():
        @pl.when(z < zn - 1)
        def _():
            d_hop.wait_recv()

        @pl.when(z > 0)
        def _():
            for h in range(heads):
                d_out[h] = d_out[h] + mm(d_in[h], pre[h, 3], NN)
            d_hop.start()

        for h in range(heads):
            state = d_in[h]
            pieces = parts(state)
            d_put[XN - 1, h] = state
            for j in range(XN - 1):
                d_put[j, h] = d_put[j, h] + mm(pieces, pre[h, 6 - j], NN)
        hand_out(d_put, d_got, 1)

    @pl.when(z < zn // 2)
    def _():
        forward()
        backward()

    @pl.when(z >= zn // 2)
    def _():
        backward()
        forward()

    @pl.when(z < zn - 1)
    def _():
        s_hop.wait_send()

    @pl.when(z > 0)
    def _():
        d_hop.wait_send()

    for kind, (put, got) in enumerate(((s_put, s_got), (d_put, d_got))):
        for i, peer in enumerate(peers):
            pltpu.make_async_remote_copy(
                src_ref=put.at[peer],
                dst_ref=got.at[x],
                send_sem=psend.at[i, kind],
                recv_sem=precv.at[i, kind],
                device_id=at(z, peer),
                device_id_type=MESH,
            ).wait()
    for copy in t_copies:
        copy.wait()
    tt_ref[...] = ttbuf[...]
    for j in range(XN):
        for h in range(heads):
            s0_ref[h, j * quarter : (j + 1) * quarter, :] = s_got[j, h]
            d0_ref[h, j * quarter : (j + 1) * quarter, :] = d_got[j, h]


def back_kernel(heads, q_ref, k_ref, v_ref, u_ref, w_ref, x_ref, pg_ref, col_ref, go_ref, s0_ref, d0_ref, g_ref):
    size = HEAD_SIZE
    count = q_ref.shape[1]
    row, col, row_token, col_token, row_step, col_step = order_masks(count)
    strict = (col_token < row_token) | ((col_token == row_token) & row_step & ~col_step)
    smask = score_mask(count)
    logits = []
    for h in range(heads):
        query, key, value = q_ref[h], k_ref[h], v_ref[h]
        beta, key_scale = col_ref[h, :, 0:1], col_ref[h, :, 1:2]
        query_scale = col_ref[h, 0:count, 2:3]
        go = go_ref[:, h * size : (h + 1) * size]
        state, adjoint = parts(s0_ref[h]), parts(d0_ref[h])
        keys = parts(key)
        fresh = u_ref[h] - mm(w_ref[h], state, NT)
        rest = value - mm(keys, state, NT)
        d_fresh = pg_ref[h] + mm(keys, adjoint, NT)
        solved = mm(x_ref[h], d_fresh, TN)
        fresh_parts = parts(fresh)
        d_scores = parts(jnp.where(smask, mm(go, fresh_parts, NT), 0.0))
        d_system = jnp.where(strict, -mm(solved, fresh_parts, NT), 0.0)
        d_rest = beta * solved
        gram = mm(keys, keys, NT)
        d_beta = jnp.sum(solved * rest, axis=-1, keepdims=True) + jnp.sum(d_system * gram, axis=-1, keepdims=True)
        d_gram = parts(beta * d_system)
        d_query = mm(go, state) + mm(d_scores, keys)
        d_key = (
            mm(d_scores, query, TN)
            + mm(fresh_parts, adjoint)
            - mm(d_rest, state)
            + mm(d_gram, keys)
            + mm(d_gram, keys, TN)
        )
        d_query = query_scale * (d_query - query * jnp.sum(query * d_query, axis=-1, keepdims=True))
        d_key = key_scale * (d_key - key * jnp.sum(key * d_key, axis=-1, keepdims=True))
        d_logit = d_beta * beta * (1.0 - 0.5 * beta)
        g_ref[:, h * size : (h + 1) * size] = d_query.astype(BF16)
        for j in range(NH):
            at = (heads + h * NH + j) * size
            g_ref[:, at : at + size] = d_key[j * count : (j + 1) * count].astype(BF16)
            at += heads * NH * size
            g_ref[:, at : at + size] = d_rest[j * count : (j + 1) * count].astype(BF16)
            logits.append(d_logit[j * count : (j + 1) * count])
    pad = jnp.zeros((count, size - len(logits)), F32)
    g_ref[:, heads * (1 + 2 * NH) * size :] = jnp.concatenate(logits + [pad], axis=1).astype(BF16)


def tail_kernel(
    zn,
    yn,
    g_ref,
    tt_ref,
    wq_hbm,
    wk_hbm,
    wv_hbm,
    wb_hbm,
    gx_ref,
    gwq_ref,
    gwk_ref,
    gwv_ref,
    gwb_ref,
    wq,
    wk,
    wv,
    wb,
    gbuf,
    part,
    ring_a,
    ring_b,
    got_a,
    got_b,
    pair_put,
    pair_got,
    y_put,
    y_got,
    wsem,
    gsend,
    grecv,
    rsend,
    rrecv,
    csend,
    crecv,
    ysend,
    yrecv,
):
    seq, head = lax.axis_index("seq"), lax.axis_index("head")
    z, x = lax.div(seq, XN), lax.rem(seq, XN)
    y, core = lax.div(head, 2), lax.rem(head, 2)
    above, below = lax.rem(z + 1, zn), lax.rem(z + zn - 1, zn)
    right, left = lax.rem(x + 1, XN), lax.rem(x + XN - 1, XN)
    partner = head + 1 - 2 * core
    count, width = g_ref.shape
    q_wide, k_wide, v_wide = wq.shape[1], wk.shape[1], wv.shape[1]
    beta_at = q_wide + k_wide + v_wide
    betas = wb.shape[0]
    rows = part.shape[1]
    block = gx_ref.shape[1]

    loads = [
        pltpu.make_async_copy(src, dst, wsem.at[i])
        for i, (src, dst) in enumerate(((wq_hbm, wq), (wk_hbm, wk), (wv_hbm, wv), (wb_hbm, wb)))
    ]
    for load in loads:
        load.start()

    barrier = pltpu.get_barrier_semaphore()
    greeted = [(z * XN + right, head), (z * XN + left, head), (above * XN + x, head), (below * XN + x, head), (seq, partner)]
    greeted += [(seq, lax.rem(y + d, yn) * 2 + core) for d in range(1, yn)]
    for device in greeted:
        pl.semaphore_signal(barrier, inc=1, device_id=device, device_id_type=MESH)
    pl.semaphore_wait(barrier, len(greeted))

    half = q_wide + k_wide
    mid_a, mid_b = half // 2, half + 3 * 128
    pieces = ((0, mid_a, 0, 0), (half, mid_b, 1, 0), (mid_a, half, 0, mid_a), (mid_b, width, 1, mid_b - half))

    def block_rows(member):
        return pl.ds(pl.multiple_of(member * count, count), count)

    def own_copy(p, way):
        lo, hi = pieces[p][:2]
        return pltpu.make_async_remote_copy(
            src_ref=g_ref.at[:, lo:hi],
            dst_ref=gbuf.at[block_rows(x), lo:hi],
            send_sem=gsend.at[p, way],
            recv_sem=grecv.at[p, way],
            device_id=(z * XN + (right if way == 0 else left), head),
            device_id_type=MESH,
        )

    def onward_copy(p):
        lo, hi = pieces[p][:2]
        to_right = p < 2
        spot = gbuf.at[block_rows(left if to_right else right), lo:hi]
        return pltpu.make_async_remote_copy(
            src_ref=spot,
            dst_ref=spot,
            send_sem=gsend.at[p, 2],
            recv_sem=grecv.at[p, 2],
            device_id=(z * XN + (right if to_right else left), head),
            device_id_type=MESH,
        )

    def offer(p):
        own_copy(p, 0).start()
        own_copy(p, 1).start()

    def relay(p):
        own_copy(p, 0).wait_recv()
        own_copy(p, 1).wait_recv()
        onward_copy(p).start()

    offer(0)
    offer(1)
    gbuf[block_rows(x), :] = g_ref[...]
    for load in loads:
        load.wait()

    def input_term(d, side):
        lo = pl.multiple_of((lax.rem(y + d, yn) * 2 + side) * block, block)
        spot = pl.ds(lo, block)
        total = dg(g_ref[:, :q_wide], wq[spot, :], NT)
        total = total + dg(g_ref[:, q_wide:half], wk[spot, :], NT)
        total = total + dg(g_ref[:, half:beta_at], wv[spot, :], NT)
        return total + dg(g_ref[:, beta_at : beta_at + betas], wb[:, spot], NN)

    def pair_copy(d):
        return pltpu.make_async_remote_copy(
            src_ref=pair_put.at[d],
            dst_ref=pair_got.at[d],
            send_sem=csend.at[d],
            recv_sem=crecv.at[d],
            device_id=(seq, partner),
            device_id_type=MESH,
        )

    def y_copy(d):
        return pltpu.make_async_remote_copy(
            src_ref=y_put.at[d - 1],
            dst_ref=y_got.at[d - 1],
            send_sem=ysend.at[d - 1],
            recv_sem=yrecv.at[d - 1],
            device_id=(seq, lax.rem(y + d, yn) * 2 + core),
            device_id_type=MESH,
        )

    order = list(range(1, yn)) + [0]
    for d in order:
        pair_put[d] = input_term(d, 1 - core).astype(BF16)
        pair_copy(d).start()
    relay(0)
    offer(2)
    relay(1)
    offer(3)
    kept = None
    for d in order:
        term = input_term(d, core)
        pair_copy(d).wait_recv()
        term = term + pair_got[d].astype(F32)
        if d:
            y_put[d - 1] = term.astype(BF16)
            y_copy(d).start()
        else:
            gx_ref[...] = term

    rings = ((ring_a, got_a), (ring_b, got_b))

    def hop(p, step):
        lo, hi, way, at = pieces[p]
        put, got = rings[way]
        return pltpu.make_async_remote_copy(
            src_ref=put.at[step, :, at : at + hi - lo],
            dst_ref=got.at[step, :, at : at + hi - lo],
            send_sem=rsend.at[p, step],
            recv_sem=rrecv.at[p, step],
            device_id=((below if way else above) * XN + x, head),
            device_id_type=MESH,
        )

    def store(lo, value):
        for i in range(value.shape[1] // 128):
            at = lo + i * 128
            piece = value[:, i * 128 : (i + 1) * 128]
            if at < q_wide:
                gwq_ref[:, at : at + 128] = piece
            elif at < half:
                gwk_ref[:, at - q_wide : at - q_wide + 128] = piece
            elif at < beta_at:
                gwv_ref[:, at - half : at - half + 128] = piece
            else:
                gwb_ref[...] = piece[:, :betas]

    def ring_step(p, step):
        lo, hi, way, at = pieces[p]
        put, got = rings[way]
        if step == 0:
            onward_copy(p).wait_recv()
            part[:, :, lo:hi] = dg(tt_ref[...].reshape(zn * rows, XN * count), gbuf[:, lo:hi], NN).reshape(zn, rows, hi - lo)
        chunk = lax.rem(z + 1 + step, zn) if way else lax.rem(z + 2 * zn - 1 - step, zn)
        value = part[chunk, :, lo:hi]
        if step > 0:
            hop(p, step - 1).wait_recv()
            value = value + got[step - 1, :, at : at + hi - lo].astype(F32)
        if step < zn - 1:
            put[step, :, at : at + hi - lo] = value.astype(BF16)
            hop(p, step).start()
        else:
            store(lo, value)

    delay = (0, 0, 1, 1)
    for turn in range(zn + max(delay)):
        for p in range(len(pieces)):
            step = turn - delay[p]
            if step == 0 and p >= 2:
                relay(p)
            if 0 <= step < zn:
                ring_step(p, step)

    total = gx_ref[...]
    for d in range(1, yn):
        y_copy(d).wait_recv()
        total = total + y_got[d - 1].astype(F32)
    gx_ref[...] = total

    for p in range(len(pieces)):
        own_copy(p, 0).wait_send()
        own_copy(p, 1).wait_send()
        onward_copy(p).wait_send()
        for step in range(zn - 1):
            hop(p, step).wait_send()
    for d in range(yn):
        pair_copy(d).wait_send()
        if d:
            y_copy(d).wait_send()


def vmem(count):
    return [pl.BlockSpec(memory_space=pltpu.VMEM)] * count


def per_device(tokens, w_query, w_key, w_value, w_beta, grad_out):
    count = tokens.shape[0]
    size = HEAD_SIZE
    heads = w_query.shape[1] // size
    rows = NH * count
    quarter = size // XN
    w_beta_t = w_beta.T
    shard = tokens.shape[1] // lax.axis_size("seq")
    zn = lax.axis_size("seq") // XN
    f32 = lambda *shape: jax.ShapeDtypeStruct(shape, F32)
    bf16 = lambda *shape: jax.ShapeDtypeStruct(shape, BF16)
    square = f32(heads, size, size)
    steps = f32(heads, rows, size)
    a, bt, lt, q, k, v, u, w, x, pg, cols = pl.pallas_call(
        functools.partial(front_kernel, heads),
        out_shape=(
            square,
            square,
            square,
            f32(heads, count, size),
            steps,
            steps,
            steps,
            steps,
            f32(heads, rows, rows),
            steps,
            f32(heads, rows, 8),
        ),
        in_specs=vmem(6),
        out_specs=tuple(vmem(11)),
        name="front",
    )(tokens, w_query, w_key, w_value, w_beta_t, grad_out)
    s0, d0, tt = pl.pallas_call(
        functools.partial(scan_kernel, zn),
        out_shape=(square, square, bf16(zn, shard, XN * count)),
        in_specs=vmem(4),
        out_specs=tuple(vmem(3)),
        scratch_shapes=[
            pltpu.VMEM((XN, heads, size, size), F32),
            pltpu.VMEM((XN, heads, quarter, size), F32),
            pltpu.VMEM((XN, heads, quarter, size), F32),
            pltpu.VMEM((heads, quarter, size), F32),
            pltpu.VMEM((heads, quarter, size), F32),
            pltpu.VMEM((heads, quarter, size), F32),
            pltpu.VMEM((heads, quarter, size), F32),
            pltpu.VMEM((XN, heads, quarter, size), F32),
            pltpu.VMEM((XN, heads, quarter, size), F32),
            pltpu.VMEM((XN, heads, quarter, size), F32),
            pltpu.VMEM((XN, heads, quarter, size), F32),
            pltpu.VMEM((heads, 7, size, size), F32),
            pltpu.SemaphoreType.DMA((XN - 1, 3)),
            pltpu.SemaphoreType.DMA((XN - 1, 3)),
            pltpu.SemaphoreType.DMA((2,)),
            pltpu.SemaphoreType.DMA((2,)),
            pltpu.SemaphoreType.DMA((XN - 1, 2)),
            pltpu.SemaphoreType.DMA((XN - 1, 2)),
            pltpu.VMEM((zn, XN, shard, count), BF16),
            pltpu.VMEM((zn, shard, XN * count), BF16),
            pltpu.SemaphoreType.DMA((XN - 1,)),
            pltpu.SemaphoreType.DMA((XN - 1,)),
        ],
        compiler_params=pltpu.CompilerParams(collective_id=0, has_side_effects=True),
        name="scan",
    )(a, bt, lt, tokens)
    width = heads * (1 + 2 * NH) * size + 128
    grads = pl.pallas_call(
        functools.partial(back_kernel, heads),
        out_shape=bf16(count, width),
        in_specs=vmem(11),
        out_specs=pl.BlockSpec(memory_space=pltpu.VMEM),
        name="back",
    )(q, k, v, u, w, x, pg, cols, grad_out, s0, d0)

    yn = lax.axis_size("head") // 2
    block = tokens.shape[1] // (2 * yn)
    half = heads * (1 + NH) * size
    dma = pltpu.SemaphoreType.DMA
    gx, gwq, gwk, gwv, gwb = pl.pallas_call(
        functools.partial(tail_kernel, zn, yn),
        out_shape=(
            f32(count, block),
            f32(shard, w_query.shape[1]),
            f32(shard, w_key.shape[1]),
            f32(shard, w_value.shape[1]),
            f32(shard, w_beta.shape[1]),
        ),
        in_specs=vmem(2) + [pl.BlockSpec(memory_space=pl.ANY)] * 4,
        out_specs=tuple(vmem(5)),
        scratch_shapes=[
            pltpu.VMEM(w_query.shape, BF16),
            pltpu.VMEM(w_key.shape, BF16),
            pltpu.VMEM(w_value.shape, BF16),
            pltpu.VMEM(w_beta_t.shape, BF16),
            pltpu.VMEM((XN * count, width), BF16),
            pltpu.VMEM((zn, shard, width), F32),
            pltpu.VMEM((zn - 1, shard, half), BF16),
            pltpu.VMEM((zn - 1, shard, width - half), BF16),
            pltpu.VMEM((zn - 1, shard, half), BF16),
            pltpu.VMEM((zn - 1, shard, width - half), BF16),
            pltpu.VMEM((yn, count, block), BF16),
            pltpu.VMEM((yn, count, block), BF16),
            pltpu.VMEM((yn - 1, count, block), BF16),
            pltpu.VMEM((yn - 1, count, block), BF16),
            dma((4,)),
            dma((4, 3)),
            dma((4, 3)),
            dma((4, zn - 1)),
            dma((4, zn - 1)),
            dma((yn,)),
            dma((yn,)),
            dma((yn - 1,)),
            dma((yn - 1,)),
        ],
        compiler_params=pltpu.CompilerParams(collective_id=1, has_side_effects=True),
        name="tail",
    )(grads, tt, w_query, w_key, w_value, w_beta_t)
    return (gx.astype(BF16), gwq, gwk, gwv, gwb)


def solution(mesh):
    in_specs = (
        P("seq", None),
        P(None, "head"),
        P(None, "head"),
        P(None, "head"),
        P(None, "head"),
        P("seq", "head"),
    )
    return jax.shard_map(
        per_device, mesh=mesh, in_specs=in_specs, out_specs=(P("seq", "head"),) * 5, check_vma=False
    )
```

```python
import functools
from types import SimpleNamespace

import jax
import jax.numpy as jnp
from jax import lax
from jax.experimental import pallas as pl
from jax.experimental.pallas import tpu as pltpu
from jax.sharding import PartitionSpec as P

HEAD_SIZE = 128
NH = 2
XN = 4
EPS = 1e-6
MESH = pl.DeviceIdType.MESH
F32 = jnp.float32
BF16 = jnp.bfloat16

NN = ((1,), (0,))
NT = ((1,), (1,))
TN = ((0,), (0,))


def dg(left, right, dims):
    return lax.dot_general(left, right, (dims, ((), ())), preferred_element_type=F32)


def parts(array):
    if isinstance(array, tuple):
        return array
    if array.dtype == BF16:
        return (array,)
    high = array.astype(BF16)
    return (high, (array - high.astype(F32)).astype(BF16))


def mm(left, right, dims=NN):
    left, right = parts(left), parts(right)
    total = dg(left[0], right[0], dims)
    if len(right) > 1:
        total = total + dg(left[0], right[1], dims)
    if len(left) > 1:
        total = total + dg(left[1], right[0], dims)
    return total


def mm1(left, right, dims=NN):
    return dg(left.astype(BF16), right.astype(BF16), dims)


def order_masks(tokens):
    rows = NH * tokens
    row = lax.broadcasted_iota(jnp.int32, (rows, rows), 0)
    col = lax.broadcasted_iota(jnp.int32, (rows, rows), 1)
    row_token, col_token = row & (tokens - 1), col & (tokens - 1)
    row_step, col_step = row >= tokens, col >= tokens
    return row, col, row_token, col_token, row_step, col_step


def score_mask(tokens):
    row = lax.broadcasted_iota(jnp.int32, (tokens, NH * tokens), 0)
    col = lax.broadcasted_iota(jnp.int32, (tokens, NH * tokens), 1)
    return (col & (tokens - 1)) <= row


def unit(matrix):
    scale = lax.rsqrt(jnp.sum(matrix * matrix, axis=-1, keepdims=True) + EPS)
    return matrix * scale, scale


def layer_kernel(zn, yn, heads, names, *refs):
    r = SimpleNamespace(**dict(zip(names, refs)))
    size = HEAD_SIZE
    seq, head = lax.axis_index("seq"), lax.axis_index("head")
    z, x = lax.div(seq, XN), lax.rem(seq, XN)
    y, core = lax.div(head, 2), lax.rem(head, 2)
    above, below = lax.rem(z + 1, zn), lax.rem(z + zn - 1, zn)
    right, left, across = lax.rem(x + 1, XN), lax.rem(x + XN - 1, XN), lax.rem(x + 2, XN)
    peers = (right, left, across)
    partner = head + 1 - 2 * core
    quarter = size // XN
    count, depth = r.tok.shape
    rows = NH * count
    shard = depth // (zn * XN)
    block = r.gx.shape[1]
    width = r.g.shape[1]

    def row_device(member):
        return (z * XN + member, head)

    def remote(src, dst, send, recv, device):
        return pltpu.make_async_remote_copy(
            src_ref=src, dst_ref=dst, send_sem=send, recv_sem=recv, device_id=device, device_id_type=MESH
        )

    loads = {}
    for i, name in enumerate(("tok", "wk", "wb", "wv", "wq", "go")):
        loads[name] = pltpu.make_async_copy(getattr(r, name + "_hbm"), getattr(r, name), r.load_sem.at[i])
        loads[name].start()

    barrier = pltpu.get_barrier_semaphore()
    greeted = [row_device(peer) for peer in peers]
    greeted += [(above * XN + x, head), (below * XN + x, head), (seq, partner)]
    greeted += [(seq, lax.rem(y + d, yn) * 2 + core) for d in range(1, yn)]
    for device in greeted:
        pl.semaphore_signal(barrier, inc=1, device_id=device, device_id_type=MESH)

    loads["tok"].wait()
    for zz in range(zn):
        lanes = r.tok[:, zz * XN * shard : (zz + 1) * XN * shard]
        r.tokt[zz] = lanes.T.reshape(XN, shard, count)
    pl.semaphore_wait(barrier, len(greeted))
    own_lanes = pl.ds(pl.multiple_of(x * count, count), count)
    started = []

    def start(copy):
        copy.start()
        started.append(copy)
        return copy

    tok_copies = [
        start(remote(r.tokt.at[:, peer], r.tt.at[:, :, own_lanes], r.tsend.at[i], r.trecv.at[i], row_device(peer)))
        for i, peer in enumerate(peers)
    ]
    r.tt[:, :, own_lanes] = r.tokt[:, x]

    row, col, row_token, col_token, row_step, col_step = order_masks(count)
    strict = (col_token < row_token) | ((col_token == row_token) & row_step & ~col_step)
    smask = score_mask(count)
    loads["wk"].wait()
    loads["wb"].wait()
    tok = r.tok[...]
    pk = dg(tok, r.wk[...], NN)
    beta_all = 2.0 * jax.nn.sigmoid(dg(tok, r.wb[...], NT))
    eye = jnp.where(row == col, 1.0, 0.0)
    inverses = []
    for h in range(heads):
        base = h * NH * size
        key, key_scale = unit(jnp.concatenate([pk[:, base : base + size], pk[:, base + size : base + 2 * size]], axis=0))
        beta = jnp.concatenate([beta_all[:, 2 * h : 2 * h + 1], beta_all[:, 2 * h + 1 : 2 * h + 2]], axis=0)
        r.kr[h] = key
        r.cols[h, :, 0:1] = beta
        r.cols[h, :, 1:2] = key_scale
        system = jnp.where(strict, beta * mm(key, key, NT), 0.0)
        r.system[h] = system
        inverses.append(eye - jnp.where(col_token == row_token, system, 0.0))
    loads["wv"].wait()
    loads["wq"].wait()
    loads["go"].wait()
    pv = dg(tok, r.wv[...], NN)
    pq = dg(tok, r.wq[...], NN)
    for h in range(heads):
        base = h * NH * size
        r.vr[h] = jnp.concatenate([pv[:, base : base + size], pv[:, base + size : base + 2 * size]], axis=0)
        query, query_scale = unit(pq[:, h * size : (h + 1) * size])
        r.qr[h] = query
        r.cols[h, 0:count, 2:3] = query_scale
    level = 1
    while level < count:
        span = 2 * level - 1
        pick = ((row_token & span) >= level) & ((col_token | span) == (row_token | span)) & ((col_token & span) < level)
        for h in range(heads):
            inverse = parts(inverses[h])
            inner = mm(jnp.where(pick, r.system[h], 0.0), inverse)
            inverses[h] = inverses[h] - mm(inverse, inner)
        level *= 2
    for h in range(heads):
        key, beta = r.kr[h], r.cols[h, :, 0:1]
        query, go = r.qr[h], r.go[:, h * size : (h + 1) * size]
        inverse = parts(inverses[h])
        r.x_hi[h], r.x_lo[h] = inverse
        solved = mm(inverse, jnp.concatenate([beta * key, beta * r.vr[h]], axis=1))
        w_rows, u_rows = parts(solved[:, :size]), solved[:, size:]
        r.w_hi[h], r.w_lo[h] = w_rows
        r.ur[h] = u_rows
        key = parts(key)
        scores = jnp.where(smask, mm(query, key, NT), 0.0)
        pulled = mm(scores, go, TN)
        r.pg[h] = pulled
        r.e_own[h] = mm(key, w_rows, TN).astype(BF16)
        offset = mm(u_rows, key, TN)
        adjoint = mm(go, query, TN) - mm(pulled, w_rows, TN)
        for j in range(XN):
            r.bl_own[j, h, :quarter, :] = offset[j * quarter : (j + 1) * quarter].astype(BF16)
            r.bl_own[j, h, quarter:, :] = adjoint[j * quarter : (j + 1) * quarter].astype(BF16)

    e_right = start(remote(r.e_own, r.ebuf.at[x], r.esend.at[0], r.erecv.at[0], row_device(right)))
    e_left = start(remote(r.e_own, r.ebuf.at[x], r.esend.at[1], r.erecv.at[1], row_device(left)))
    bl_copies = [
        start(remote(r.bl_own.at[peer], r.blbuf.at[x], r.bsend.at[i], r.brecv.at[i], row_device(peer)))
        for i, peer in enumerate(peers)
    ]
    r.ebuf[x] = r.e_own[...]
    r.blbuf[x] = r.bl_own[x]

    @pl.when(z == 0)
    def _():
        r.s_in[...] = jnp.zeros_like(r.s_in)

    @pl.when(z == zn - 1)
    def _():
        r.d_in[...] = jnp.zeros_like(r.d_in)

    half = heads // 2
    e_right.wait_recv()
    spot = r.ebuf.at[left, :half]
    e_on_right = start(remote(spot, spot, r.esend.at[2], r.erecv.at[2], row_device(right)))
    e_left.wait_recv()
    spot = r.ebuf.at[right, half:]
    e_on_left = start(remote(spot, spot, r.esend.at[3], r.erecv.at[3], row_device(left)))
    for copy in bl_copies:
        copy.wait_recv()
    e_on_right.wait_recv()
    e_on_left.wait_recv()

    for h in range(heads):
        maps = [r.ebuf[j, h] for j in range(XN)]
        wide = [m.astype(F32) for m in maps]
        e10 = wide[1] + wide[0] - dg(maps[1], maps[0], NN)
        e32 = wide[3] + wide[2] - dg(maps[3], maps[2], NN)
        e10s, e32s = parts(e10), parts(e32)
        e210 = wide[2] + e10 - mm(maps[2], e10s)
        e321 = e32 + wide[1] - mm(e32s, maps[1])
        r.tot_hi[h], r.tot_lo[h] = parts(e32 + e10 - mm(e32s, e10s))
        for i, m in enumerate((maps[0], e10s[0], e210.astype(BF16))):
            r.e_pre[h, i * size : (i + 1) * size, :] = m
        for i, m in enumerate((maps[3], e32s[0], e321.astype(BF16))):
            r.e_suf[h, :, i * size : (i + 1) * size] = m
        off = r.blbuf[0, h, :quarter, :].astype(F32)
        for j in range(1, XN):
            r.s_off[j, h] = off
            off = off - mm(off, maps[j], NT) + r.blbuf[j, h, :quarter, :].astype(F32)
        r.s_off[0, h] = off
        off = r.blbuf[XN - 1, h, quarter:, :].astype(F32)
        for j in range(XN - 2, -1, -1):
            r.d_off[j, h] = off
            off = off - mm(off, maps[j], NN) + r.blbuf[j, h, quarter:, :].astype(F32)
        r.d_off[XN - 1, h] = off

    s_hop = remote(r.s_out, r.s_in, r.zsend.at[0], r.zrecv.at[0], (above * XN + x, head))
    d_hop = remote(r.d_out, r.d_in, r.zsend.at[1], r.zrecv.at[1], (below * XN + x, head))

    def hand_copy(put, got, kind, i):
        return remote(put.at[peers[i]], got.at[x], r.psend.at[i, kind], r.precv.at[i, kind], row_device(peers[i]))

    def hand_out(put, got, kind):
        for i in range(XN - 1):
            hand_copy(put, got, kind, i).start()
        got[x] = put[x]

    def forward():
        @pl.when(z > 0)
        def _():
            s_hop.wait_recv()

        @pl.when(z < zn - 1)
        def _():
            for h in range(heads):
                state = r.s_in[h]
                moved = dg(state, r.tot_hi[h], NT) + dg(state, r.tot_lo[h], NT)
                r.s_out[h] = (state.astype(F32) + r.s_off[0, h] - moved).astype(BF16)
            s_hop.start()

        for h in range(heads):
            state = r.s_in[h]
            moved = dg(state, r.e_pre[h], NT)
            r.s_put[0, h] = state
            for j in range(1, XN):
                value = state.astype(F32) + r.s_off[j, h] - moved[:, (j - 1) * size : j * size]
                r.s_put[j, h] = value.astype(BF16)
        hand_out(r.s_put, r.s_got, 0)

    def backward():
        @pl.when(z < zn - 1)
        def _():
            d_hop.wait_recv()

        @pl.when(z > 0)
        def _():
            for h in range(heads):
                state = r.d_in[h]
                moved = dg(state, r.tot_hi[h], NN) + dg(state, r.tot_lo[h], NN)
                r.d_out[h] = (state.astype(F32) + r.d_off[XN - 1, h] - moved).astype(BF16)
            d_hop.start()

        for h in range(heads):
            state = r.d_in[h]
            moved = dg(state, r.e_suf[h], NN)
            r.d_put[XN - 1, h] = state
            for j in range(XN - 1):
                i = XN - 2 - j
                value = state.astype(F32) + r.d_off[j, h] - moved[:, i * size : (i + 1) * size]
                r.d_put[j, h] = value.astype(BF16)
        hand_out(r.d_put, r.d_got, 1)

    @pl.when(z < zn // 2)
    def _():
        forward()
        backward()

    @pl.when(z >= zn // 2)
    def _():
        backward()
        forward()

    for i in range(XN - 1):
        hand_copy(r.s_put, r.s_got, 0, i).wait_recv()
        hand_copy(r.d_put, r.d_got, 1, i).wait_recv()

    two = NH * size
    value_wide = heads * two
    head_wide = size + two
    logit_at = value_wide + heads * head_wide
    cuts = [0]
    for h in range(heads):
        cuts.append(cuts[-1] + two)
    cuts += [value_wide + head_wide, value_wide + head_wide + two, width]
    cuts = list(zip(cuts[:-1], cuts[1:]))
    to_right = (True, False, True, False, False)

    def member_rows(member):
        return pl.ds(pl.multiple_of(member * count, count), count)

    def own_copy(p, way):
        lo, hi = cuts[p]
        device = row_device(left if way else right)
        src = r.g.at[:, lo:hi]
        return remote(src, r.gbuf.at[member_rows(x), lo:hi], r.gsend.at[p, way], r.grecv.at[p, way], device)

    def onward_copy(p):
        lo, hi = cuts[p]
        spot = r.gbuf.at[member_rows(left if to_right[p] else right), lo:hi]
        return remote(spot, spot, r.gsend.at[p, 2], r.grecv.at[p, 2], row_device(right if to_right[p] else left))

    def offer(p):
        lo, hi = cuts[p]
        own_copy(p, 0).start()
        own_copy(p, 1).start()
        r.gbuf[member_rows(x), lo:hi] = r.g[:, lo:hi]

    def relay(p):
        own_copy(p, 0).wait_recv()
        own_copy(p, 1).wait_recv()
        onward_copy(p).start()

    states = [jnp.concatenate([r.s_got[j, h] for j in range(XN)], axis=0) for h in range(heads)]
    adjoints = [jnp.concatenate([r.d_got[j, h] for j in range(XN)], axis=0) for h in range(heads)]
    for h in range(heads):
        keys = parts(r.kr[h])
        r.fresh[h] = r.ur[h] - mm((r.w_hi[h], r.w_lo[h]), states[h], NT)
        solved = mm((r.x_hi[h], r.x_lo[h]), r.pg[h] + mm(keys, adjoints[h], NT), TN)
        r.solved[h] = solved
        d_value = r.cols[h, :, 0:1] * solved
        for j in range(NH):
            at = h * two + j * size
            r.g[:, at : at + size] = d_value[j * count : (j + 1) * count].astype(BF16)
        offer(h)

    logits = []
    for h in range(heads):
        query, key = r.qr[h], r.kr[h]
        beta, key_scale = r.cols[h, :, 0:1], r.cols[h, :, 1:2]
        query_scale = r.cols[h, 0:count, 2:3]
        go = r.go[:, h * size : (h + 1) * size]
        solved, fresh = r.solved[h], r.fresh[h].astype(BF16)
        keys = key.astype(BF16)
        state, adjoint = states[h], adjoints[h]
        rest = r.vr[h] - dg(keys, state, NT)
        d_scores = jnp.where(smask, dg(go, fresh, NT), 0.0).astype(BF16)
        d_system = jnp.where(strict, -mm1(solved, fresh, NT), 0.0)
        gram = dg(keys, keys, NT)
        d_beta = jnp.sum(solved * rest, axis=-1, keepdims=True) + jnp.sum(d_system * gram, axis=-1, keepdims=True)
        d_gram = (beta * d_system).astype(BF16)
        d_query = dg(go, state, NN) + dg(d_scores, keys, NN)
        d_key = (
            mm1(d_scores, query, TN)
            + dg(fresh, adjoint, NN)
            - mm1(beta * solved, state)
            + dg(d_gram, keys, NN)
            + dg(d_gram, keys, TN)
        )
        d_query = query_scale * (d_query - query * jnp.sum(query * d_query, axis=-1, keepdims=True))
        d_key = key_scale * (d_key - key * jnp.sum(key * d_key, axis=-1, keepdims=True))
        d_logit = d_beta * beta * (1.0 - 0.5 * beta)
        at = value_wide + h * head_wide
        r.g[:, at : at + size] = d_query.astype(BF16)
        for j in range(NH):
            at += size
            r.g[:, at : at + size] = d_key[j * count : (j + 1) * count].astype(BF16)
            logits.append(d_logit[j * count : (j + 1) * count])
        if h == 0:
            relay(0)
            offer(heads)
    pad = jnp.zeros((count, size - len(logits)), F32)
    r.g[:, logit_at:] = jnp.concatenate(logits + [pad], axis=1).astype(BF16)
    relay(1)
    offer(heads + 1)

    def input_term(d, side):
        lo = pl.multiple_of((lax.rem(y + d, yn) * 2 + side) * block, block)
        spot = pl.ds(lo, block)
        total = dg(r.g[:, :value_wide], r.wv[spot, :], NT)
        for h in range(heads):
            at = value_wide + h * head_wide
            total = total + dg(r.g[:, at : at + size], r.wq[spot, h * size : (h + 1) * size], NT)
            total = total + dg(r.g[:, at + size : at + head_wide], r.wk[spot, h * two : (h + 1) * two], NT)
        return total + dg(r.g[:, logit_at : logit_at + heads * NH], r.wb[:, spot], NN)

    def pair_copy(d):
        return remote(r.pair_put.at[d], r.pair_got.at[d], r.csend.at[d], r.crecv.at[d], (seq, partner))

    def y_copy(d):
        i = d - 1
        device = (seq, lax.rem(y + d, yn) * 2 + core)
        return remote(r.y_put.at[i], r.y_got.at[i], r.ysend.at[i], r.yrecv.at[i], device)

    order = list(range(1, yn)) + [0]

    def partner_terms():
        for d in order:
            r.pair_put[d] = input_term(d, 1 - core).astype(BF16)
            pair_copy(d).start()

    def own_terms():
        for d in order:
            term = input_term(d, core)
            pair_copy(d).wait_recv()
            term = term + r.pair_got[d].astype(F32)
            if d:
                r.y_put[d - 1] = term.astype(BF16)
                y_copy(d).start()
            else:
                r.kept[...] = term

    def hops(p):
        return (zn // 2, zn // 2 - 1) if p % 2 == 0 else (zn // 2 - 1, zn // 2)

    def ring_hop(p, way, step):
        lo, hi = cuts[p]
        device = ((below if way else above) * XN + x, head)
        put, got = r.ring_put.at[way, step, :, lo:hi], r.ring_got.at[way, step, :, lo:hi]
        return remote(put, got, r.rsend.at[p, way, step], r.rrecv.at[p, way, step], device)

    def ring_step(p, step):
        lo, hi = cuts[p]
        if step == 0:
            onward_copy(p).wait_recv()
            left_side = r.tt[...].reshape(zn * shard, XN * count)
            r.part[:, :, lo:hi] = dg(left_side, r.gbuf[:, lo:hi], NN).reshape(zn, shard, hi - lo)
        lengths = hops(p)
        for way in range(2):
            length = lengths[way]
            if step >= length:
                continue
            chunk = lax.rem(z + zn + (step - length if way else length - step), zn)
            value = r.part[chunk, :, lo:hi]
            if step > 0:
                ring_hop(p, way, step - 1).wait_recv()
                value = value + r.ring_got[way, step - 1, :, lo:hi].astype(F32)
            r.ring_put[way, step, :, lo:hi] = value.astype(BF16)
            ring_hop(p, way, step).start()
        if step == max(lengths):
            value = r.part[z, :, lo:hi]
            for way in range(2):
                ring_hop(p, way, lengths[way] - 1).wait_recv()
                value = value + r.ring_got[way, lengths[way] - 1, :, lo:hi].astype(F32)
            r.gw[:, lo:hi] = value

    for copy in tok_copies:
        copy.wait_recv()
    delay = (0, 1, 2, 3, 3)
    extra = {0: (partner_terms, lambda: relay(2), lambda: offer(4)), 1: (own_terms, lambda: relay(3)), 2: (lambda: relay(4),)}
    for turn in range(zn // 2 + 1 + max(delay)):
        for p in range(len(cuts)):
            step = turn - delay[p]
            if 0 <= step <= zn // 2:
                ring_step(p, step)
        for action in extra.get(turn, ()):
            action()

    total = r.kept[...]
    for d in range(1, yn):
        y_copy(d).wait_recv()
        total = total + r.y_got[d - 1].astype(F32)
    r.gx[...] = total.astype(BF16)

    for copy in started:
        copy.wait_send()

    @pl.when(z < zn - 1)
    def _():
        s_hop.wait_send()

    @pl.when(z > 0)
    def _():
        d_hop.wait_send()

    for i in range(XN - 1):
        hand_copy(r.s_put, r.s_got, 0, i).wait_send()
        hand_copy(r.d_put, r.d_got, 1, i).wait_send()
    for p in range(len(cuts)):
        own_copy(p, 0).wait_send()
        own_copy(p, 1).wait_send()
        onward_copy(p).wait_send()
        for way in range(2):
            for step in range(hops(p)[way]):
                ring_hop(p, way, step).wait_send()
    for d in range(yn):
        pair_copy(d).wait_send()
        if d:
            y_copy(d).wait_send()


def finish_kernel(heads, gx_in, gw_in, gx, gwq, gwk, gwv, gwb):
    two = NH * HEAD_SIZE
    gx[...] = gx_in[...]
    gwv[...] = gw_in[:, : heads * two]
    at = heads * two
    for h in range(heads):
        gwq[:, h * HEAD_SIZE : (h + 1) * HEAD_SIZE] = gw_in[:, at : at + HEAD_SIZE]
        at += HEAD_SIZE
        gwk[:, h * two : (h + 1) * two] = gw_in[:, at : at + two]
        at += two
    gwb[...] = gw_in[:, at : at + 128].T[: heads * NH, :]


def vmem(count):
    return [pl.BlockSpec(memory_space=pltpu.VMEM)] * count


def per_device(tokens, w_query, w_key, w_value, w_beta, grad_out):
    count, depth = tokens.shape
    size = HEAD_SIZE
    heads = w_query.shape[1] // size
    rows = NH * count
    quarter = size // XN
    devices = lax.axis_size("seq")
    zn, yn = devices // XN, lax.axis_size("head") // 2
    shard, block = depth // devices, depth // (2 * yn)
    width = heads * (1 + 2 * NH) * size + 128
    pieces, hops = heads + 3, zn // 2
    w_beta_t = w_beta.T
    shape = jax.ShapeDtypeStruct
    dma = pltpu.SemaphoreType.DMA
    scratch = dict(
        tok=(tokens.shape, BF16),
        wk=(w_key.shape, BF16),
        wb=(w_beta_t.shape, BF16),
        wv=(w_value.shape, BF16),
        wq=(w_query.shape, BF16),
        go=(grad_out.shape, BF16),
        tokt=((zn, XN, shard, count), BF16),
        tt=((zn, shard, XN * count), BF16),
        system=((heads, rows, rows), F32),
        kr=((heads, rows, size), F32),
        vr=((heads, rows, size), F32),
        qr=((heads, count, size), F32),
        ur=((heads, rows, size), F32),
        pg=((heads, rows, size), F32),
        cols=((heads, rows, 8), F32),
        x_hi=((heads, rows, rows), BF16),
        x_lo=((heads, rows, rows), BF16),
        w_hi=((heads, rows, size), BF16),
        w_lo=((heads, rows, size), BF16),
        fresh=((heads, rows, size), F32),
        solved=((heads, rows, size), F32),
        e_own=((heads, size, size), BF16),
        bl_own=((XN, heads, 2 * quarter, size), BF16),
        ebuf=((XN, heads, size, size), BF16),
        blbuf=((XN, heads, 2 * quarter, size), BF16),
        tot_hi=((heads, size, size), BF16),
        tot_lo=((heads, size, size), BF16),
        e_pre=((heads, 3 * size, size), BF16),
        e_suf=((heads, size, 3 * size), BF16),
        s_off=((XN, heads, quarter, size), F32),
        d_off=((XN, heads, quarter, size), F32),
        s_in=((heads, quarter, size), BF16),
        d_in=((heads, quarter, size), BF16),
        s_out=((heads, quarter, size), BF16),
        d_out=((heads, quarter, size), BF16),
        s_put=((XN, heads, quarter, size), BF16),
        d_put=((XN, heads, quarter, size), BF16),
        s_got=((XN, heads, quarter, size), BF16),
        d_got=((XN, heads, quarter, size), BF16),
        g=((count, width), BF16),
        gbuf=((XN * count, width), BF16),
        part=((zn, shard, width), F32),
        ring_put=((2, hops, shard, width), BF16),
        ring_got=((2, hops, shard, width), BF16),
        pair_put=((yn, count, block), BF16),
        pair_got=((yn, count, block), BF16),
        y_put=((yn - 1, count, block), BF16),
        y_got=((yn - 1, count, block), BF16),
        kept=((count, block), F32),
    )
    semaphores = dict(
        load_sem=(6,),
        tsend=(XN - 1,),
        trecv=(XN - 1,),
        esend=(4,),
        erecv=(4,),
        bsend=(XN - 1,),
        brecv=(XN - 1,),
        zsend=(2,),
        zrecv=(2,),
        psend=(XN - 1, 2),
        precv=(XN - 1, 2),
        gsend=(pieces, 3),
        grecv=(pieces, 3),
        rsend=(pieces, 2, hops),
        rrecv=(pieces, 2, hops),
        csend=(yn,),
        crecv=(yn,),
        ysend=(yn - 1,),
        yrecv=(yn - 1,),
    )
    inputs = ("tok", "wq", "wk", "wv", "wb", "go")
    names = tuple(name + "_hbm" for name in inputs) + ("gx", "gw") + tuple(scratch) + tuple(semaphores)
    gx, gw = pl.pallas_call(
        functools.partial(layer_kernel, zn, yn, heads, names),
        out_shape=(shape((count, block), BF16), shape((shard, width), F32)),
        in_specs=[pl.BlockSpec(memory_space=pl.ANY)] * 6,
        out_specs=tuple(vmem(2)),
        scratch_shapes=[pltpu.VMEM(*spec) for spec in scratch.values()] + [dma(dims) for dims in semaphores.values()],
        compiler_params=pltpu.CompilerParams(collective_id=0, has_side_effects=True, vmem_limit_bytes=60 << 20),
        name="layer",
    )(tokens, w_query, w_key, w_value, w_beta_t, grad_out)
    outs = (
        shape((count, block), BF16),
        shape((shard, w_query.shape[1]), F32),
        shape((shard, w_key.shape[1]), F32),
        shape((shard, w_value.shape[1]), F32),
        shape((w_beta.shape[1], shard), F32),
    )
    grad_tokens, gwq, gwk, gwv, gwb = pl.pallas_call(
        functools.partial(finish_kernel, heads),
        out_shape=outs,
        in_specs=vmem(2),
        out_specs=tuple(vmem(5)),
        name="finish",
    )(gx, gw)
    return (grad_tokens, gwq, gwk, gwv, gwb.T)


def solution(mesh):
    in_specs = (
        P("seq", None),
        P(None, "head"),
        P(None, "head"),
        P(None, "head"),
        P(None, "head"),
        P("seq", "head"),
    )
    return jax.shard_map(
        per_device, mesh=mesh, in_specs=in_specs, out_specs=(P("seq", "head"),) * 5, check_vma=False
    )
```

```python
import functools
from types import SimpleNamespace

import jax
import jax.numpy as jnp
from jax import lax
from jax.experimental import pallas as pl
from jax.experimental.pallas import tpu as pltpu
from jax.sharding import PartitionSpec as P

HEAD_SIZE = 128
NH = 2
XN = 4
EPS = 1e-6
MESH = pl.DeviceIdType.MESH
F32 = jnp.float32
BF16 = jnp.bfloat16

NN = ((1,), (0,))
NT = ((1,), (1,))
TN = ((0,), (0,))


def dg(left, right, dims):
    return lax.dot_general(left, right, (dims, ((), ())), preferred_element_type=F32)


def parts(array):
    if isinstance(array, tuple):
        return array
    if array.dtype == BF16:
        return (array,)
    high = array.astype(BF16)
    return (high, (array - high.astype(F32)).astype(BF16))


def mm(left, right, dims=NN):
    left, right = parts(left), parts(right)
    total = dg(left[0], right[0], dims)
    if len(right) > 1:
        total = total + dg(left[0], right[1], dims)
    if len(left) > 1:
        total = total + dg(left[1], right[0], dims)
    return total


def mm1(left, right, dims=NN):
    return dg(left.astype(BF16), right.astype(BF16), dims)


def order_masks(tokens):
    rows = NH * tokens
    row = lax.broadcasted_iota(jnp.int32, (rows, rows), 0)
    col = lax.broadcasted_iota(jnp.int32, (rows, rows), 1)
    row_token, col_token = row & (tokens - 1), col & (tokens - 1)
    row_step, col_step = row >= tokens, col >= tokens
    return row, col, row_token, col_token, row_step, col_step


def score_mask(tokens):
    row = lax.broadcasted_iota(jnp.int32, (tokens, NH * tokens), 0)
    col = lax.broadcasted_iota(jnp.int32, (tokens, NH * tokens), 1)
    return (col & (tokens - 1)) <= row


def unit(matrix):
    scale = lax.rsqrt(jnp.sum(matrix * matrix, axis=-1, keepdims=True) + EPS)
    return matrix * scale, scale


def layer_kernel(zn, yn, heads, names, *refs):
    r = SimpleNamespace(**dict(zip(names, refs)))
    size = HEAD_SIZE
    seq, head = lax.axis_index("seq"), lax.axis_index("head")
    z, x = lax.div(seq, XN), lax.rem(seq, XN)
    y, core = lax.div(head, 2), lax.rem(head, 2)
    above, below = lax.rem(z + 1, zn), lax.rem(z + zn - 1, zn)
    odd = lax.rem(z, 2)
    beside = z + 1 - 2 * odd
    above2, below2 = lax.rem(z + 2, zn), lax.rem(z + zn - 2, zn)
    right, left, across = lax.rem(x + 1, XN), lax.rem(x + XN - 1, XN), lax.rem(x + 2, XN)
    peers = (right, left, across)
    partner = head + 1 - 2 * core
    quarter = size // XN
    count, depth = r.tok.shape
    rows = NH * count
    shard = depth // (zn * XN)
    block = r.gx.shape[1]
    width = r.g.shape[1]

    def row_device(member):
        return (z * XN + member, head)

    def remote(src, dst, send, recv, device):
        return pltpu.make_async_remote_copy(
            src_ref=src, dst_ref=dst, send_sem=send, recv_sem=recv, device_id=device, device_id_type=MESH
        )

    loads = {}
    for i, name in enumerate(("tok", "wk", "wb", "wv", "wq", "go")):
        loads[name] = pltpu.make_async_copy(getattr(r, name + "_hbm"), getattr(r, name), r.load_sem.at[i])
        loads[name].start()

    barrier = pltpu.get_barrier_semaphore()
    greeted = [row_device(peer) for peer in peers]
    greeted += [(zz * XN + x, head) for zz in (above, below, above2, below2)] + [(seq, partner)]
    greeted += [(seq, lax.rem(y + d, yn) * 2 + core) for d in range(1, yn)]
    for device in greeted:
        pl.semaphore_signal(barrier, inc=1, device_id=device, device_id_type=MESH)

    loads["tok"].wait()
    for zz in range(zn):
        lanes = r.tok[:, zz * XN * shard : (zz + 1) * XN * shard]
        r.tokt[zz] = lanes.T.reshape(XN, shard, count)
    own_lanes = pl.ds(pl.multiple_of(x * count, count), count)
    started = []

    def start(copy):
        copy.start()
        started.append(copy)
        return copy

    row, col, row_token, col_token, row_step, col_step = order_masks(count)
    strict = (col_token < row_token) | ((col_token == row_token) & row_step & ~col_step)
    smask = score_mask(count)
    loads["wk"].wait()
    loads["wb"].wait()
    tok = r.tok[...]
    pk = dg(tok, r.wk[...], NN)
    beta_all = 2.0 * jax.nn.sigmoid(dg(tok, r.wb[...], NT))
    eye = jnp.where(row == col, 1.0, 0.0)
    inverses = []
    for h in range(heads):
        base = h * NH * size
        key, key_scale = unit(jnp.concatenate([pk[:, base : base + size], pk[:, base + size : base + 2 * size]], axis=0))
        beta = jnp.concatenate([beta_all[:, 2 * h : 2 * h + 1], beta_all[:, 2 * h + 1 : 2 * h + 2]], axis=0)
        r.kr[h] = key
        r.cols[h, :, 0:1] = beta
        r.cols[h, :, 1:2] = key_scale
        system = jnp.where(strict, beta * mm(key, key, NT), 0.0)
        r.system[h] = system
        inverses.append(eye - jnp.where(col_token == row_token, system, 0.0))
    loads["wv"].wait()
    loads["wq"].wait()
    loads["go"].wait()
    pv = dg(tok, r.wv[...], NN)
    pq = dg(tok, r.wq[...], NN)
    for h in range(heads):
        base = h * NH * size
        r.vr[h] = jnp.concatenate([pv[:, base : base + size], pv[:, base + size : base + 2 * size]], axis=0)
        query, query_scale = unit(pq[:, h * size : (h + 1) * size])
        r.qr[h] = query
        r.cols[h, 0:count, 2:3] = query_scale
    level = 1
    while level < count:
        span = 2 * level - 1
        pick = ((row_token & span) >= level) & ((col_token | span) == (row_token | span)) & ((col_token & span) < level)
        for h in range(heads):
            inverse = parts(inverses[h])
            inner = mm(jnp.where(pick, r.system[h], 0.0), inverse)
            inverses[h] = inverses[h] - mm(inverse, inner)
        level *= 2
    for h in range(heads):
        key, beta = r.kr[h], r.cols[h, :, 0:1]
        query, go = r.qr[h], r.go[:, h * size : (h + 1) * size]
        inverse = parts(inverses[h])
        r.x_hi[h], r.x_lo[h] = inverse
        solved = mm(inverse, jnp.concatenate([beta * key, beta * r.vr[h]], axis=1))
        w_rows, u_rows = parts(solved[:, :size]), solved[:, size:]
        r.w_hi[h], r.w_lo[h] = w_rows
        r.ur[h] = u_rows
        key = parts(key)
        scores = jnp.where(smask, mm(query, key, NT), 0.0)
        pulled = mm(scores, go, TN)
        r.pg[h] = pulled
        r.e_own[h] = mm(key, w_rows, TN).astype(BF16)
        offset = mm(u_rows, key, TN)
        adjoint = mm(go, query, TN) - mm(pulled, w_rows, TN)
        for j in range(XN):
            r.bl_own[j, h, :quarter, :] = offset[j * quarter : (j + 1) * quarter].astype(BF16)
            r.bl_own[j, h, quarter:, :] = adjoint[j * quarter : (j + 1) * quarter].astype(BF16)

    pl.semaphore_wait(barrier, len(greeted))
    e_right = start(remote(r.e_own, r.ebuf.at[x], r.esend.at[0], r.erecv.at[0], row_device(right)))
    e_left = start(remote(r.e_own, r.ebuf.at[x], r.esend.at[1], r.erecv.at[1], row_device(left)))
    bl_copies = [
        start(remote(r.bl_own.at[peer], r.blbuf.at[x], r.bsend.at[i], r.brecv.at[i], row_device(peer)))
        for i, peer in enumerate(peers)
    ]
    r.ebuf[x] = r.e_own[...]
    r.blbuf[x] = r.bl_own[x]

    @pl.when(z < 2)
    def _():
        r.s_in[...] = jnp.zeros_like(r.s_in)

    @pl.when(z >= zn - 2)
    def _():
        r.d_in[...] = jnp.zeros_like(r.d_in)

    half = heads // 2
    e_right.wait_recv()
    spot = r.ebuf.at[left, :half]
    e_on_right = start(remote(spot, spot, r.esend.at[2], r.erecv.at[2], row_device(right)))
    e_left.wait_recv()
    spot = r.ebuf.at[right, half:]
    e_on_left = start(remote(spot, spot, r.esend.at[3], r.erecv.at[3], row_device(left)))
    for copy in bl_copies:
        copy.wait_recv()
    e_on_right.wait_recv()
    e_on_left.wait_recv()
    tok_copies = [
        start(remote(r.tokt.at[:, peer], r.tt.at[:, :, own_lanes], r.tsend.at[i], r.trecv.at[i], row_device(peer)))
        for i, peer in enumerate(peers)
    ]
    r.tt[:, :, own_lanes] = r.tokt[:, x]

    for h in range(heads):
        maps = [r.ebuf[j, h] for j in range(XN)]
        wide = [m.astype(F32) for m in maps]
        e10 = wide[1] + wide[0] - dg(maps[1], maps[0], NN)
        e32 = wide[3] + wide[2] - dg(maps[3], maps[2], NN)
        e10s, e32s = parts(e10), parts(e32)
        e210 = wide[2] + e10 - mm(maps[2], e10s)
        e321 = e32 + wide[1] - mm(e32s, maps[1])
        r.fz[odd, h] = (e32 + e10 - mm(e32s, e10s)).astype(BF16)
        for i, m in enumerate((maps[0], e10s[0], e210.astype(BF16))):
            r.e_pre[h, i * size : (i + 1) * size, :] = m
        for i, m in enumerate((maps[3], e32s[0], e321.astype(BF16))):
            r.e_suf[h, :, i * size : (i + 1) * size] = m
        off = r.blbuf[0, h, :quarter, :].astype(F32)
        for j in range(1, XN):
            r.s_off[j, h] = off
            off = off - mm(off, maps[j], NT) + r.blbuf[j, h, :quarter, :].astype(F32)
        r.sz[odd, h] = off.astype(BF16)
        off = r.blbuf[XN - 1, h, quarter:, :].astype(F32)
        for j in range(XN - 2, -1, -1):
            r.d_off[j, h] = off
            off = off - mm(off, maps[j], NN) + r.blbuf[j, h, quarter:, :].astype(F32)
        r.dz[odd, h] = off.astype(BF16)

    pair_swaps = [
        start(remote(ref.at[odd], ref.at[odd], r.swap_send.at[i], r.swap_recv.at[i], (beside * XN + x, head)))
        for i, ref in enumerate((r.fz, r.sz, r.dz))
    ]
    for copy in pair_swaps:
        copy.wait_recv()
    for h in range(heads):
        low, high = r.fz[0, h], r.fz[1, h]
        both = high.astype(F32) + low.astype(F32) - dg(high, low, NN)
        r.pair[h] = both.astype(BF16)
        r.pair_t[h] = both.T.astype(BF16)
        s_low, d_high = r.sz[0, h], r.dz[1, h]
        r.s_off[0, h] = s_low.astype(F32) - dg(s_low, high, NT) + r.sz[1, h].astype(F32)
        r.d_off[XN - 1, h] = d_high.astype(F32) - dg(d_high, low, NN) + r.dz[0, h].astype(F32)

    s_hop = remote(r.s_out, r.s_in, r.zsend.at[0], r.zrecv.at[0], (above2 * XN + x, head))
    d_hop = remote(r.d_out, r.d_in, r.zsend.at[1], r.zrecv.at[1], (below2 * XN + x, head))

    def hand_copy(put, got, kind, i):
        return remote(put.at[peers[i]], got.at[x], r.psend.at[i, kind], r.precv.at[i, kind], row_device(peers[i]))

    def hand_out(put, got, kind):
        for i in range(XN - 1):
            hand_copy(put, got, kind, i).start()
        got[x] = put[x]

    def forward():
        @pl.when(z >= 2)
        def _():
            s_hop.wait_recv()

        @pl.when(z < zn - 2)
        def _():
            for h in range(heads):
                state = r.s_in[h]
                moved = dg(state, r.pair_t[h], NN)
                r.s_out[h] = (state.astype(F32) + r.s_off[0, h] - moved).astype(BF16)
            s_hop.start()

        @pl.when(odd == 0)
        def _():
            r.s_mine[...] = r.s_in[...]

        @pl.when(odd == 1)
        def _():
            for h in range(heads):
                state = r.s_in[h]
                moved = dg(state, r.fz[0, h], NT)
                r.s_mine[h] = (state.astype(F32) + r.sz[0, h].astype(F32) - moved).astype(BF16)

        for h in range(heads):
            state = r.s_mine[h]
            moved = dg(state, r.e_pre[h], NT)
            r.s_put[0, h] = state
            for j in range(1, XN):
                value = state.astype(F32) + r.s_off[j, h] - moved[:, (j - 1) * size : j * size]
                r.s_put[j, h] = value.astype(BF16)
        hand_out(r.s_put, r.s_got, 0)

    def backward():
        @pl.when(z < zn - 2)
        def _():
            d_hop.wait_recv()

        @pl.when(z >= 2)
        def _():
            for h in range(heads):
                state = r.d_in[h]
                moved = dg(state, r.pair[h], NN)
                r.d_out[h] = (state.astype(F32) + r.d_off[XN - 1, h] - moved).astype(BF16)
            d_hop.start()

        @pl.when(odd == 1)
        def _():
            r.d_mine[...] = r.d_in[...]

        @pl.when(odd == 0)
        def _():
            for h in range(heads):
                state = r.d_in[h]
                moved = dg(state, r.fz[1, h], NN)
                r.d_mine[h] = (state.astype(F32) + r.dz[1, h].astype(F32) - moved).astype(BF16)

        for h in range(heads):
            state = r.d_mine[h]
            moved = dg(state, r.e_suf[h], NN)
            r.d_put[XN - 1, h] = state
            for j in range(XN - 1):
                i = XN - 2 - j
                value = state.astype(F32) + r.d_off[j, h] - moved[:, i * size : (i + 1) * size]
                r.d_put[j, h] = value.astype(BF16)
        hand_out(r.d_put, r.d_got, 1)

    @pl.when(z < zn // 2)
    def _():
        forward()
        backward()

    @pl.when(z >= zn // 2)
    def _():
        backward()
        forward()

    for i in range(XN - 1):
        hand_copy(r.s_put, r.s_got, 0, i).wait_recv()
        hand_copy(r.d_put, r.d_got, 1, i).wait_recv()

    two = NH * size
    value_wide = heads * two
    head_wide = size + two
    logit_at = value_wide + heads * head_wide
    cuts = [0]
    for h in range(heads):
        cuts.append(cuts[-1] + two)
    cuts += [value_wide + head_wide, value_wide + head_wide + two, width]
    cuts = list(zip(cuts[:-1], cuts[1:]))
    to_right = (True, False, True, False, False)

    def member_rows(member):
        return pl.ds(pl.multiple_of(member * count, count), count)

    def own_copy(p, way):
        lo, hi = cuts[p]
        device = row_device(left if way else right)
        src = r.g.at[:, lo:hi]
        return remote(src, r.gbuf.at[member_rows(x), lo:hi], r.gsend.at[p, way], r.grecv.at[p, way], device)

    def onward_copy(p):
        lo, hi = cuts[p]
        spot = r.gbuf.at[member_rows(left if to_right[p] else right), lo:hi]
        return remote(spot, spot, r.gsend.at[p, 2], r.grecv.at[p, 2], row_device(right if to_right[p] else left))

    def offer(p):
        lo, hi = cuts[p]
        own_copy(p, 0).start()
        own_copy(p, 1).start()
        r.gbuf[member_rows(x), lo:hi] = r.g[:, lo:hi]

    def relay(p):
        own_copy(p, 0).wait_recv()
        own_copy(p, 1).wait_recv()
        onward_copy(p).start()

    states = [jnp.concatenate([r.s_got[j, h] for j in range(XN)], axis=0) for h in range(heads)]
    adjoints = [jnp.concatenate([r.d_got[j, h] for j in range(XN)], axis=0) for h in range(heads)]
    for h in range(heads):
        keys = parts(r.kr[h])
        r.fresh[h] = r.ur[h] - mm((r.w_hi[h], r.w_lo[h]), states[h], NT)
        solved = mm((r.x_hi[h], r.x_lo[h]), r.pg[h] + mm(keys, adjoints[h], NT), TN)
        r.solved[h] = solved
        d_value = r.cols[h, :, 0:1] * solved
        for j in range(NH):
            at = h * two + j * size
            r.g[:, at : at + size] = d_value[j * count : (j + 1) * count].astype(BF16)
        offer(h)

    logits = []
    for h in range(heads):
        query, key = r.qr[h], r.kr[h]
        beta, key_scale = r.cols[h, :, 0:1], r.cols[h, :, 1:2]
        query_scale = r.cols[h, 0:count, 2:3]
        go = r.go[:, h * size : (h + 1) * size]
        solved, fresh = r.solved[h], r.fresh[h].astype(BF16)
        keys = key.astype(BF16)
        state, adjoint = states[h], adjoints[h]
        rest = r.vr[h] - dg(keys, state, NT)
        d_scores = jnp.where(smask, dg(go, fresh, NT), 0.0).astype(BF16)
        d_system = jnp.where(strict, -mm1(solved, fresh, NT), 0.0)
        gram = dg(keys, keys, NT)
        d_beta = jnp.sum(solved * rest, axis=-1, keepdims=True) + jnp.sum(d_system * gram, axis=-1, keepdims=True)
        d_gram = (beta * d_system).astype(BF16)
        d_query = dg(go, state, NN) + dg(d_scores, keys, NN)
        d_key = (
            mm1(d_scores, query, TN)
            + dg(fresh, adjoint, NN)
            - mm1(beta * solved, state)
            + dg(d_gram, keys, NN)
            + dg(d_gram, keys, TN)
        )
        d_query = query_scale * (d_query - query * jnp.sum(query * d_query, axis=-1, keepdims=True))
        d_key = key_scale * (d_key - key * jnp.sum(key * d_key, axis=-1, keepdims=True))
        d_logit = d_beta * beta * (1.0 - 0.5 * beta)
        at = value_wide + h * head_wide
        r.g[:, at : at + size] = d_query.astype(BF16)
        for j in range(NH):
            at += size
            r.g[:, at : at + size] = d_key[j * count : (j + 1) * count].astype(BF16)
            logits.append(d_logit[j * count : (j + 1) * count])
        if h == 0:
            offer(heads)
    pad = jnp.zeros((count, size - len(logits)), F32)
    r.g[:, logit_at:] = jnp.concatenate(logits + [pad], axis=1).astype(BF16)

    def input_term(d, side):
        lo = pl.multiple_of((lax.rem(y + d, yn) * 2 + side) * block, block)
        spot = pl.ds(lo, block)
        total = dg(r.g[:, :value_wide], r.wv[spot, :], NT)
        for h in range(heads):
            at = value_wide + h * head_wide
            total = total + dg(r.g[:, at : at + size], r.wq[spot, h * size : (h + 1) * size], NT)
            total = total + dg(r.g[:, at + size : at + head_wide], r.wk[spot, h * two : (h + 1) * two], NT)
        return total + dg(r.g[:, logit_at : logit_at + heads * NH], r.wb[:, spot], NN)

    def pair_copy(d):
        return remote(r.pair_put.at[d], r.pair_got.at[d], r.csend.at[d], r.crecv.at[d], (seq, partner))

    def y_copy(d):
        i = d - 1
        device = (seq, lax.rem(y + d, yn) * 2 + core)
        return remote(r.y_put.at[i], r.y_got.at[i], r.ysend.at[i], r.yrecv.at[i], device)

    order = list(range(1, yn)) + [0]

    def partner_terms():
        for d in order:
            r.pair_put[d] = input_term(d, 1 - core).astype(BF16)
            pair_copy(d).start()

    def own_terms():
        for d in order:
            term = input_term(d, core)
            pair_copy(d).wait_recv()
            term = term + r.pair_got[d].astype(F32)
            if d:
                r.y_put[d - 1] = term.astype(BF16)
                y_copy(d).start()
            else:
                r.kept[...] = term

    def hops(p):
        return (zn // 2, zn // 2 - 1) if p % 2 == 0 else (zn // 2 - 1, zn // 2)

    def ring_hop(p, way, step):
        lo, hi = cuts[p]
        device = ((below if way else above) * XN + x, head)
        put, got = r.ring_put.at[way, step, :, lo:hi], r.ring_got.at[way, step, :, lo:hi]
        return remote(put, got, r.rsend.at[p, way, step], r.rrecv.at[p, way, step], device)

    def ring_step(p, step):
        lo, hi = cuts[p]
        if step == 0:
            onward_copy(p).wait_recv()
            left_side = r.tt[...].reshape(zn * shard, XN * count)
            r.part[:, :, lo:hi] = dg(left_side, r.gbuf[:, lo:hi], NN).reshape(zn, shard, hi - lo)
        lengths = hops(p)
        for way in range(2):
            length = lengths[way]
            if step >= length:
                continue
            chunk = lax.rem(z + zn + (step - length if way else length - step), zn)
            value = r.part[chunk, :, lo:hi]
            if step > 0:
                ring_hop(p, way, step - 1).wait_recv()
                value = value + r.ring_got[way, step - 1, :, lo:hi].astype(F32)
            r.ring_put[way, step, :, lo:hi] = value.astype(BF16)
            ring_hop(p, way, step).start()
        if step == max(lengths):
            value = r.part[z, :, lo:hi]
            for way in range(2):
                ring_hop(p, way, lengths[way] - 1).wait_recv()
                value = value + r.ring_got[way, lengths[way] - 1, :, lo:hi].astype(F32)
            r.gw[:, lo:hi] = value

    partner_terms()
    relay(0)
    relay(1)
    offer(3)
    offer(4)
    own_terms()
    relay(2)
    for copy in tok_copies:
        copy.wait_recv()
    ring_step(0, 0)
    ring_step(1, 0)
    relay(3)
    relay(4)
    ring_step(0, 1)
    ring_step(1, 1)
    for p in (3, 2, 4):
        ring_step(p, 0)
    for step in range(2, zn // 2 + 1):
        for p in (0, 1):
            ring_step(p, step)
        for p in (3, 2, 4):
            ring_step(p, step - 1)
    for p in (3, 2, 4):
        ring_step(p, zn // 2)

    total = r.kept[...]
    for d in range(1, yn):
        y_copy(d).wait_recv()
        total = total + r.y_got[d - 1].astype(F32)
    r.gx[...] = total.astype(BF16)

    for copy in started:
        copy.wait_send()

    @pl.when(z < zn - 2)
    def _():
        s_hop.wait_send()

    @pl.when(z >= 2)
    def _():
        d_hop.wait_send()

    for i in range(XN - 1):
        hand_copy(r.s_put, r.s_got, 0, i).wait_send()
        hand_copy(r.d_put, r.d_got, 1, i).wait_send()
    for p in range(len(cuts)):
        own_copy(p, 0).wait_send()
        own_copy(p, 1).wait_send()
        onward_copy(p).wait_send()
        for way in range(2):
            for step in range(hops(p)[way]):
                ring_hop(p, way, step).wait_send()
    for d in range(yn):
        pair_copy(d).wait_send()
        if d:
            y_copy(d).wait_send()


def finish_kernel(heads, gx_in, gw_in, gx, gwq, gwk, gwv, gwb):
    two = NH * HEAD_SIZE
    gx[...] = gx_in[...]
    gwv[...] = gw_in[:, : heads * two]
    at = heads * two
    for h in range(heads):
        gwq[:, h * HEAD_SIZE : (h + 1) * HEAD_SIZE] = gw_in[:, at : at + HEAD_SIZE]
        at += HEAD_SIZE
        gwk[:, h * two : (h + 1) * two] = gw_in[:, at : at + two]
        at += two
    gwb[...] = gw_in[:, at : at + 128].T[: heads * NH, :]


def vmem(count):
    return [pl.BlockSpec(memory_space=pltpu.VMEM)] * count


def per_device(tokens, w_query, w_key, w_value, w_beta, grad_out):
    count, depth = tokens.shape
    size = HEAD_SIZE
    heads = w_query.shape[1] // size
    rows = NH * count
    quarter = size // XN
    devices = lax.axis_size("seq")
    zn, yn = devices // XN, lax.axis_size("head") // 2
    shard, block = depth // devices, depth // (2 * yn)
    width = heads * (1 + 2 * NH) * size + 128
    pieces, hops = heads + 3, zn // 2
    w_beta_t = w_beta.T
    shape = jax.ShapeDtypeStruct
    dma = pltpu.SemaphoreType.DMA
    scratch = dict(
        tok=(tokens.shape, BF16),
        wk=(w_key.shape, BF16),
        wb=(w_beta_t.shape, BF16),
        wv=(w_value.shape, BF16),
        wq=(w_query.shape, BF16),
        go=(grad_out.shape, BF16),
        tokt=((zn, XN, shard, count), BF16),
        tt=((zn, shard, XN * count), BF16),
        system=((heads, rows, rows), F32),
        kr=((heads, rows, size), F32),
        vr=((heads, rows, size), F32),
        qr=((heads, count, size), F32),
        ur=((heads, rows, size), F32),
        pg=((heads, rows, size), F32),
        cols=((heads, rows, 8), F32),
        x_hi=((heads, rows, rows), BF16),
        x_lo=((heads, rows, rows), BF16),
        w_hi=((heads, rows, size), BF16),
        w_lo=((heads, rows, size), BF16),
        fresh=((heads, rows, size), F32),
        solved=((heads, rows, size), F32),
        e_own=((heads, size, size), BF16),
        bl_own=((XN, heads, 2 * quarter, size), BF16),
        ebuf=((XN, heads, size, size), BF16),
        blbuf=((XN, heads, 2 * quarter, size), BF16),
        fz=((2, heads, size, size), BF16),
        sz=((2, heads, quarter, size), BF16),
        dz=((2, heads, quarter, size), BF16),
        pair=((heads, size, size), BF16),
        pair_t=((heads, size, size), BF16),
        s_mine=((heads, quarter, size), BF16),
        d_mine=((heads, quarter, size), BF16),
        e_pre=((heads, 3 * size, size), BF16),
        e_suf=((heads, size, 3 * size), BF16),
        s_off=((XN, heads, quarter, size), F32),
        d_off=((XN, heads, quarter, size), F32),
        s_in=((heads, quarter, size), BF16),
        d_in=((heads, quarter, size), BF16),
        s_out=((heads, quarter, size), BF16),
        d_out=((heads, quarter, size), BF16),
        s_put=((XN, heads, quarter, size), BF16),
        d_put=((XN, heads, quarter, size), BF16),
        s_got=((XN, heads, quarter, size), BF16),
        d_got=((XN, heads, quarter, size), BF16),
        g=((count, width), BF16),
        gbuf=((XN * count, width), BF16),
        part=((zn, shard, width), F32),
        ring_put=((2, hops, shard, width), BF16),
        ring_got=((2, hops, shard, width), BF16),
        pair_put=((yn, count, block), BF16),
        pair_got=((yn, count, block), BF16),
        y_put=((yn - 1, count, block), BF16),
        y_got=((yn - 1, count, block), BF16),
        kept=((count, block), F32),
    )
    semaphores = dict(
        load_sem=(6,),
        tsend=(XN - 1,),
        trecv=(XN - 1,),
        esend=(4,),
        erecv=(4,),
        bsend=(XN - 1,),
        brecv=(XN - 1,),
        swap_send=(3,),
        swap_recv=(3,),
        zsend=(2,),
        zrecv=(2,),
        psend=(XN - 1, 2),
        precv=(XN - 1, 2),
        gsend=(pieces, 3),
        grecv=(pieces, 3),
        rsend=(pieces, 2, hops),
        rrecv=(pieces, 2, hops),
        csend=(yn,),
        crecv=(yn,),
        ysend=(yn - 1,),
        yrecv=(yn - 1,),
    )
    inputs = ("tok", "wq", "wk", "wv", "wb", "go")
    names = tuple(name + "_hbm" for name in inputs) + ("gx", "gw") + tuple(scratch) + tuple(semaphores)
    gx, gw = pl.pallas_call(
        functools.partial(layer_kernel, zn, yn, heads, names),
        out_shape=(shape((count, block), BF16), shape((shard, width), F32)),
        in_specs=[pl.BlockSpec(memory_space=pl.ANY)] * 6,
        out_specs=tuple(vmem(2)),
        scratch_shapes=[pltpu.VMEM(*spec) for spec in scratch.values()] + [dma(dims) for dims in semaphores.values()],
        compiler_params=pltpu.CompilerParams(collective_id=0, has_side_effects=True, vmem_limit_bytes=60 << 20),
        name="layer",
    )(tokens, w_query, w_key, w_value, w_beta_t, grad_out)
    outs = (
        shape((count, block), BF16),
        shape((shard, w_query.shape[1]), F32),
        shape((shard, w_key.shape[1]), F32),
        shape((shard, w_value.shape[1]), F32),
        shape((w_beta.shape[1], shard), F32),
    )
    grad_tokens, gwq, gwk, gwv, gwb = pl.pallas_call(
        functools.partial(finish_kernel, heads),
        out_shape=outs,
        in_specs=vmem(2),
        out_specs=tuple(vmem(5)),
        name="finish",
    )(gx, gw)
    return (grad_tokens, gwq, gwk, gwv, gwb.T)


def solution(mesh):
    in_specs = (
        P("seq", None),
        P(None, "head"),
        P(None, "head"),
        P(None, "head"),
        P(None, "head"),
        P("seq", "head"),
    )
    return jax.shard_map(
        per_device, mesh=mesh, in_specs=in_specs, out_specs=(P("seq", "head"),) * 5, check_vma=False
    )
```

```python
import functools
from types import SimpleNamespace

import jax
import jax.numpy as jnp
from jax import lax
from jax.experimental import pallas as pl
from jax.experimental.pallas import tpu as pltpu
from jax.sharding import PartitionSpec as P

HEAD_SIZE = 128
NH = 2
XN = 4
EPS = 1e-6
MESH = pl.DeviceIdType.MESH
F32 = jnp.float32
BF16 = jnp.bfloat16

NN = ((1,), (0,))
NT = ((1,), (1,))
TN = ((0,), (0,))


def dg(left, right, dims):
    return lax.dot_general(left, right, (dims, ((), ())), preferred_element_type=F32)


def parts(array):
    if isinstance(array, tuple):
        return array
    if array.dtype == BF16:
        return (array,)
    high = array.astype(BF16)
    return (high, (array - high.astype(F32)).astype(BF16))


def mm(left, right, dims=NN):
    left, right = parts(left), parts(right)
    total = dg(left[0], right[0], dims)
    if len(right) > 1:
        total = total + dg(left[0], right[1], dims)
    if len(left) > 1:
        total = total + dg(left[1], right[0], dims)
    return total


def mm1(left, right, dims=NN):
    return dg(left.astype(BF16), right.astype(BF16), dims)


def order_masks(tokens):
    rows = NH * tokens
    row = lax.broadcasted_iota(jnp.int32, (rows, rows), 0)
    col = lax.broadcasted_iota(jnp.int32, (rows, rows), 1)
    row_token, col_token = row & (tokens - 1), col & (tokens - 1)
    row_step, col_step = row >= tokens, col >= tokens
    return row, col, row_token, col_token, row_step, col_step


def score_mask(tokens):
    row = lax.broadcasted_iota(jnp.int32, (tokens, NH * tokens), 0)
    col = lax.broadcasted_iota(jnp.int32, (tokens, NH * tokens), 1)
    return (col & (tokens - 1)) <= row


def unit(matrix):
    scale = lax.rsqrt(jnp.sum(matrix * matrix, axis=-1, keepdims=True) + EPS)
    return matrix * scale, scale


def layer_kernel(zn, yn, heads, names, *refs):
    r = SimpleNamespace(**dict(zip(names, refs)))
    size = HEAD_SIZE
    seq, head = lax.axis_index("seq"), lax.axis_index("head")
    z, x = lax.div(seq, XN), lax.rem(seq, XN)
    y, core = lax.div(head, 2), lax.rem(head, 2)
    above, below = lax.rem(z + 1, zn), lax.rem(z + zn - 1, zn)
    odd = lax.rem(z, 2)
    beside = z + 1 - 2 * odd
    above2, below2 = lax.rem(z + 2, zn), lax.rem(z + zn - 2, zn)
    right, left, across = lax.rem(x + 1, XN), lax.rem(x + XN - 1, XN), lax.rem(x + 2, XN)
    peers = (right, left, across)
    partner = head + 1 - 2 * core
    quarter = size // XN
    count, depth = r.tok.shape
    rows = NH * count
    shard = depth // (zn * XN)
    block = r.gx.shape[1]
    width = r.g.shape[1]

    def row_device(member):
        return (z * XN + member, head)

    def remote(src, dst, send, recv, device):
        return pltpu.make_async_remote_copy(
            src_ref=src, dst_ref=dst, send_sem=send, recv_sem=recv, device_id=device, device_id_type=MESH
        )

    loads = {}
    for i, name in enumerate(("tok", "wk", "wb", "wv", "wq", "go")):
        loads[name] = pltpu.make_async_copy(getattr(r, name + "_hbm"), getattr(r, name), r.load_sem.at[i])
        loads[name].start()

    barrier = pltpu.get_barrier_semaphore()
    greeted = [row_device(peer) for peer in peers]
    greeted += [(zz * XN + x, head) for zz in (above, below, above2, below2)] + [(seq, partner)]
    greeted += [(seq, lax.rem(y + d, yn) * 2 + core) for d in range(1, yn)]
    for device in greeted:
        pl.semaphore_signal(barrier, inc=1, device_id=device, device_id_type=MESH)

    loads["tok"].wait()
    own_lanes = pl.ds(pl.multiple_of(x * count, count), count)
    started = []

    def start(copy):
        copy.start()
        started.append(copy)
        return copy

    row, col, row_token, col_token, row_step, col_step = order_masks(count)
    strict = (col_token < row_token) | ((col_token == row_token) & row_step & ~col_step)
    smask = score_mask(count)
    loads["wk"].wait()
    loads["wb"].wait()
    tok = r.tok[...]
    pk = dg(tok, r.wk[...], NN)
    beta_all = 2.0 * jax.nn.sigmoid(dg(tok, r.wb[...], NT))
    eye = jnp.where(row == col, 1.0, 0.0)
    inverses = []
    for h in range(heads):
        base = h * NH * size
        key, key_scale = unit(jnp.concatenate([pk[:, base : base + size], pk[:, base + size : base + 2 * size]], axis=0))
        beta = jnp.concatenate([beta_all[:, 2 * h : 2 * h + 1], beta_all[:, 2 * h + 1 : 2 * h + 2]], axis=0)
        r.kr[h] = key
        r.cols[h, :, 0:1] = beta
        r.cols[h, :, 1:2] = key_scale
        system = jnp.where(strict, beta * mm(key, key, NT), 0.0)
        r.system[h] = system
        inverses.append(eye - jnp.where(col_token == row_token, system, 0.0))
    loads["wv"].wait()
    loads["wq"].wait()
    loads["go"].wait()
    pv = dg(tok, r.wv[...], NN)
    pq = dg(tok, r.wq[...], NN)
    for h in range(heads):
        base = h * NH * size
        r.vr[h] = jnp.concatenate([pv[:, base : base + size], pv[:, base + size : base + 2 * size]], axis=0)
        query, query_scale = unit(pq[:, h * size : (h + 1) * size])
        r.qr[h] = query
        r.cols[h, 0:count, 2:3] = query_scale
    level = 1
    while level < count:
        span = 2 * level - 1
        pick = ((row_token & span) >= level) & ((col_token | span) == (row_token | span)) & ((col_token & span) < level)
        for h in range(heads):
            inverse = parts(inverses[h])
            inner = mm(jnp.where(pick, r.system[h], 0.0), inverse)
            inverses[h] = inverses[h] - mm(inverse, inner)
        level *= 2
    e_copies = {}
    for h in range(heads):
        key, beta = r.kr[h], r.cols[h, :, 0:1]
        inverse = parts(inverses[h])
        r.x_hi[h], r.x_lo[h] = inverse
        solved = mm(inverse, jnp.concatenate([beta * key, beta * r.vr[h]], axis=1))
        w_rows = parts(solved[:, :size])
        r.w_hi[h], r.w_lo[h] = w_rows
        r.ur[h] = solved[:, size:]
        r.e_own[h] = mm(key, w_rows, TN).astype(BF16)
        if h == 0:
            pl.semaphore_wait(barrier, len(greeted))
        for way, device in enumerate((right, left)):
            e_copies[h, way] = start(
                remote(r.e_own.at[h], r.ebuf.at[x, h], r.esend.at[h, way], r.erecv.at[h, way], row_device(device))
            )
    for h in range(heads):
        query, go = r.qr[h], r.go[:, h * size : (h + 1) * size]
        key = parts(r.kr[h])
        scores = jnp.where(smask, mm(query, key, NT), 0.0)
        pulled = mm(scores, go, TN)
        r.pg[h] = pulled
        offset = mm(r.ur[h], key, TN)
        adjoint = mm(go, query, TN) - mm(pulled, (r.w_hi[h], r.w_lo[h]), TN)
        for j in range(XN):
            r.bl_own[j, h, :quarter, :] = offset[j * quarter : (j + 1) * quarter].astype(BF16)
            r.bl_own[j, h, quarter:, :] = adjoint[j * quarter : (j + 1) * quarter].astype(BF16)
    bl_copies = [
        start(remote(r.bl_own.at[peer], r.blbuf.at[x], r.bsend.at[i], r.brecv.at[i], row_device(peer)))
        for i, peer in enumerate(peers)
    ]
    r.ebuf[x] = r.e_own[...]
    r.blbuf[x] = r.bl_own[x]

    @pl.when(z < 2)
    def _():
        r.s_in[...] = jnp.zeros_like(r.s_in)

    @pl.when(z >= zn - 2)
    def _():
        r.d_in[...] = jnp.zeros_like(r.d_in)

    e_onward = []
    for h in range(heads):
        for way in range(2):
            e_copies[h, way].wait_recv()
        to_right = h < heads // 2
        spot = r.ebuf.at[left if to_right else right, h]
        device = row_device(right if to_right else left)
        e_onward.append(start(remote(spot, spot, r.esend.at[h, 2], r.erecv.at[h, 2], device)))
    for zz in range(zn):
        lanes = r.tok[:, zz * XN * shard : (zz + 1) * XN * shard]
        r.tokt[zz] = lanes.T.reshape(XN, shard, count)
    for copy in bl_copies:
        copy.wait_recv()
    for copy in e_onward:
        copy.wait_recv()
    tok_copies = [
        start(remote(r.tokt.at[:, peer], r.tt.at[:, :, own_lanes], r.tsend.at[i], r.trecv.at[i], row_device(peer)))
        for i, peer in enumerate(peers)
    ]
    r.tt[:, :, own_lanes] = r.tokt[:, x]

    for h in range(heads):
        maps = [r.ebuf[j, h] for j in range(XN)]
        wide = [m.astype(F32) for m in maps]
        e10 = wide[1] + wide[0] - dg(maps[1], maps[0], NN)
        e32 = wide[3] + wide[2] - dg(maps[3], maps[2], NN)
        e10s, e32s = parts(e10), parts(e32)
        e210 = wide[2] + e10 - mm(maps[2], e10s)
        e321 = e32 + wide[1] - mm(e32s, maps[1])
        r.fz[odd, h] = (e32 + e10 - mm(e32s, e10s)).astype(BF16)
        for i, m in enumerate((maps[0], e10s[0], e210.astype(BF16))):
            r.e_pre[h, i * size : (i + 1) * size, :] = m
        for i, m in enumerate((maps[3], e32s[0], e321.astype(BF16))):
            r.e_suf[h, :, i * size : (i + 1) * size] = m
        off = r.blbuf[0, h, :quarter, :].astype(F32)
        for j in range(1, XN):
            r.s_off[j, h] = off
            off = off - mm(off, maps[j], NT) + r.blbuf[j, h, :quarter, :].astype(F32)
        r.sz[odd, h] = off.astype(BF16)
        off = r.blbuf[XN - 1, h, quarter:, :].astype(F32)
        for j in range(XN - 2, -1, -1):
            r.d_off[j, h] = off
            off = off - mm(off, maps[j], NN) + r.blbuf[j, h, quarter:, :].astype(F32)
        r.dz[odd, h] = off.astype(BF16)

    pair_swaps = [
        start(remote(ref.at[odd], ref.at[odd], r.swap_send.at[i], r.swap_recv.at[i], (beside * XN + x, head)))
        for i, ref in enumerate((r.fz, r.sz, r.dz))
    ]
    for copy in pair_swaps:
        copy.wait_recv()
    for h in range(heads):
        low, high = r.fz[0, h], r.fz[1, h]
        both = high.astype(F32) + low.astype(F32) - dg(high, low, NN)
        r.pair[h] = both.astype(BF16)
        r.pair_t[h] = both.T.astype(BF16)
        s_low, d_high = r.sz[0, h], r.dz[1, h]
        r.s_off[0, h] = s_low.astype(F32) - dg(s_low, high, NT) + r.sz[1, h].astype(F32)
        r.d_off[XN - 1, h] = d_high.astype(F32) - dg(d_high, low, NN) + r.dz[0, h].astype(F32)

    s_hop = remote(r.s_out, r.s_in, r.zsend.at[0], r.zrecv.at[0], (above2 * XN + x, head))
    d_hop = remote(r.d_out, r.d_in, r.zsend.at[1], r.zrecv.at[1], (below2 * XN + x, head))

    def hand_copy(put, got, kind, i):
        return remote(put.at[peers[i]], got.at[x], r.psend.at[i, kind], r.precv.at[i, kind], row_device(peers[i]))

    def hand_out(put, got, kind):
        for i in range(XN - 1):
            hand_copy(put, got, kind, i).start()
        got[x] = put[x]

    def forward():
        @pl.when(z >= 2)
        def _():
            s_hop.wait_recv()

        @pl.when(z < zn - 2)
        def _():
            for h in range(heads):
                state = r.s_in[h]
                moved = dg(state, r.pair_t[h], NN)
                r.s_out[h] = (state.astype(F32) + r.s_off[0, h] - moved).astype(BF16)
            s_hop.start()

        @pl.when(odd == 0)
        def _():
            r.s_mine[...] = r.s_in[...]

        @pl.when(odd == 1)
        def _():
            for h in range(heads):
                state = r.s_in[h]
                moved = dg(state, r.fz[0, h], NT)
                r.s_mine[h] = (state.astype(F32) + r.sz[0, h].astype(F32) - moved).astype(BF16)

        for h in range(heads):
            state = r.s_mine[h]
            moved = dg(state, r.e_pre[h], NT)
            r.s_put[0, h] = state
            for j in range(1, XN):
                value = state.astype(F32) + r.s_off[j, h] - moved[:, (j - 1) * size : j * size]
                r.s_put[j, h] = value.astype(BF16)
        hand_out(r.s_put, r.s_got, 0)

    def backward():
        @pl.when(z < zn - 2)
        def _():
            d_hop.wait_recv()

        @pl.when(z >= 2)
        def _():
            for h in range(heads):
                state = r.d_in[h]
                moved = dg(state, r.pair[h], NN)
                r.d_out[h] = (state.astype(F32) + r.d_off[XN - 1, h] - moved).astype(BF16)
            d_hop.start()

        @pl.when(odd == 1)
        def _():
            r.d_mine[...] = r.d_in[...]

        @pl.when(odd == 0)
        def _():
            for h in range(heads):
                state = r.d_in[h]
                moved = dg(state, r.fz[1, h], NN)
                r.d_mine[h] = (state.astype(F32) + r.dz[1, h].astype(F32) - moved).astype(BF16)

        for h in range(heads):
            state = r.d_mine[h]
            moved = dg(state, r.e_suf[h], NN)
            r.d_put[XN - 1, h] = state
            for j in range(XN - 1):
                i = XN - 2 - j
                value = state.astype(F32) + r.d_off[j, h] - moved[:, i * size : (i + 1) * size]
                r.d_put[j, h] = value.astype(BF16)
        hand_out(r.d_put, r.d_got, 1)

    two = NH * size
    value_at = heads * size
    key_at = value_at + heads * two
    logit_at = key_at + heads * two
    cuts = [0, value_at] + [value_at + (h + 1) * two for h in range(heads)] + [logit_at - size, width]
    cuts = list(zip(cuts[:-1], cuts[1:]))
    to_right = (True, False, True, False, True)

    def member_rows(member):
        return pl.ds(pl.multiple_of(member * count, count), count)

    def own_copy(p, way):
        lo, hi = cuts[p]
        device = row_device(left if way else right)
        src = r.g.at[:, lo:hi]
        return remote(src, r.gbuf.at[member_rows(x), lo:hi], r.gsend.at[p, way], r.grecv.at[p, way], device)

    def onward_copy(p):
        lo, hi = cuts[p]
        spot = r.gbuf.at[member_rows(left if to_right[p] else right), lo:hi]
        return remote(spot, spot, r.gsend.at[p, 2], r.grecv.at[p, 2], row_device(right if to_right[p] else left))

    def offer(p):
        lo, hi = cuts[p]
        own_copy(p, 0).start()
        own_copy(p, 1).start()
        r.gbuf[member_rows(x), lo:hi] = r.g[:, lo:hi]

    def relay(p):
        own_copy(p, 0).wait_recv()
        own_copy(p, 1).wait_recv()
        onward_copy(p).start()

    def joined(got, h):
        return jnp.concatenate([got[j, h] for j in range(XN)], axis=0)

    def query_grads():
        for i in range(XN - 1):
            hand_copy(r.s_put, r.s_got, 0, i).wait_recv()
        for h in range(heads):
            state = joined(r.s_got, h)
            keys, query = r.kr[h].astype(BF16), r.qr[h]
            go = r.go[:, h * size : (h + 1) * size]
            fresh = (r.ur[h] - mm((r.w_hi[h], r.w_lo[h]), state, NT)).astype(BF16)
            r.fresh[h] = fresh
            d_scores = jnp.where(smask, dg(go, fresh, NT), 0.0).astype(BF16)
            d_query = dg(go, state, NN) + dg(d_scores, keys, NN)
            d_query = r.cols[h, 0:count, 2:3] * (d_query - query * jnp.sum(query * d_query, axis=-1, keepdims=True))
            r.g[:, h * size : (h + 1) * size] = d_query.astype(BF16)
            if h == heads - 1:
                offer(0)
            r.rest[h] = r.vr[h] - dg(keys, state, NT)
            r.dk[h] = mm1(d_scores, query, TN)

    early = z < zn // 2

    @pl.when(early)
    def _():
        forward()
        query_grads()
        backward()
        relay(0)

    @pl.when(jnp.logical_not(early))
    def _():
        backward()
        forward()
        query_grads()

    for i in range(XN - 1):
        hand_copy(r.d_put, r.d_got, 1, i).wait_recv()
    adjoints = [joined(r.d_got, h) for h in range(heads)]
    for h in range(heads):
        keys = parts(r.kr[h])
        solved = mm((r.x_hi[h], r.x_lo[h]), r.pg[h] + mm(keys, adjoints[h], NT), TN)
        r.solved[h] = solved
        d_value = r.cols[h, :, 0:1] * solved
        for j in range(NH):
            at = value_at + h * two + j * size
            r.g[:, at : at + size] = d_value[j * count : (j + 1) * count].astype(BF16)
        offer(1 + h)

    logits = []
    for h in range(heads):
        key = r.kr[h]
        beta, key_scale = r.cols[h, :, 0:1], r.cols[h, :, 1:2]
        solved, fresh, keys = r.solved[h], r.fresh[h], key.astype(BF16)
        d_system = jnp.where(strict, -mm1(solved, fresh, NT), 0.0)
        gram = dg(keys, keys, NT)
        d_beta = jnp.sum(solved * r.rest[h], axis=-1, keepdims=True) + jnp.sum(d_system * gram, axis=-1, keepdims=True)
        d_gram = (beta * d_system).astype(BF16)
        d_key = (
            r.dk[h]
            + dg(fresh, adjoints[h], NN)
            - mm1(beta * solved, joined(r.s_got, h))
            + dg(d_gram, keys, NN)
            + dg(d_gram, keys, TN)
        )
        d_key = key_scale * (d_key - key * jnp.sum(key * d_key, axis=-1, keepdims=True))
        d_logit = d_beta * beta * (1.0 - 0.5 * beta)
        for j in range(NH):
            at = key_at + h * two + j * size
            r.g[:, at : at + size] = d_key[j * count : (j + 1) * count].astype(BF16)
            logits.append(d_logit[j * count : (j + 1) * count])
    pad = jnp.zeros((count, size - len(logits)), F32)
    r.g[:, logit_at:] = jnp.concatenate(logits + [pad], axis=1).astype(BF16)
    offer(3)

    def input_term(d, side):
        lo = pl.multiple_of((lax.rem(y + d, yn) * 2 + side) * block, block)
        spot = pl.ds(lo, block)
        total = dg(r.g[:, :value_at], r.wq[spot, :], NT)
        total = total + dg(r.g[:, value_at:key_at], r.wv[spot, :], NT)
        total = total + dg(r.g[:, key_at:logit_at], r.wk[spot, :], NT)
        return total + dg(r.g[:, logit_at : logit_at + heads * NH], r.wb[:, spot], NN)

    def pair_copy(d):
        return remote(r.pair_put.at[d], r.pair_got.at[d], r.csend.at[d], r.crecv.at[d], (seq, partner))

    def y_copy(d):
        i = d - 1
        device = (seq, lax.rem(y + d, yn) * 2 + core)
        return remote(r.y_put.at[i], r.y_got.at[i], r.ysend.at[i], r.yrecv.at[i], device)

    order = list(range(1, yn)) + [0]

    def partner_terms():
        for d in order:
            r.pair_put[d] = input_term(d, 1 - core).astype(BF16)
            pair_copy(d).start()

    def own_terms():
        for d in order:
            r.own_part[d] = input_term(d, core)

    def merge_terms():
        for d in order:
            pair_copy(d).wait_recv()
            term = r.own_part[d] + r.pair_got[d].astype(F32)
            if d:
                r.y_put[d - 1] = term.astype(BF16)
                y_copy(d).start()
            else:
                r.kept[...] = term

    def hops(p):
        return (zn // 2, zn // 2 - 1) if p % 2 == 0 else (zn // 2 - 1, zn // 2)

    def ring_hop(p, way, step):
        lo, hi = cuts[p]
        device = ((below if way else above) * XN + x, head)
        put, got = r.ring_put.at[way, step, :, lo:hi], r.ring_got.at[way, step, :, lo:hi]
        return remote(put, got, r.rsend.at[p, way, step], r.rrecv.at[p, way, step], device)

    def ring_step(p, step):
        lo, hi = cuts[p]
        if step == 0:
            onward_copy(p).wait_recv()
            left_side = r.tt[...].reshape(zn * shard, XN * count)
            r.part[:, :, lo:hi] = dg(left_side, r.gbuf[:, lo:hi], NN).reshape(zn, shard, hi - lo)
        lengths = hops(p)
        for way in range(2):
            length = lengths[way]
            if step >= length:
                continue
            chunk = lax.rem(z + zn + (step - length if way else length - step), zn)
            value = r.part[chunk, :, lo:hi]
            if step > 0:
                ring_hop(p, way, step - 1).wait_recv()
                value = value + r.ring_got[way, step - 1, :, lo:hi].astype(F32)
            r.ring_put[way, step, :, lo:hi] = value.astype(BF16)
            ring_hop(p, way, step).start()
        if step == max(lengths):
            value = r.part[z, :, lo:hi]
            for way in range(2):
                ring_hop(p, way, lengths[way] - 1).wait_recv()
                value = value + r.ring_got[way, lengths[way] - 1, :, lo:hi].astype(F32)
            r.gw[:, lo:hi] = value

    @pl.when(jnp.logical_not(early))
    def _():
        relay(0)

    partner_terms()
    relay(1)
    relay(2)
    offer(4)
    for copy in tok_copies:
        copy.wait_recv()
    ring_step(0, 0)
    own_terms()
    relay(3)
    ring_step(1, 0)
    ring_step(2, 0)
    relay(4)
    for p in (0, 1, 2):
        ring_step(p, 1)
    ring_step(3, 0)
    ring_step(4, 0)
    for step in range(2, zn // 2 + 1):
        for p in (0, 1, 2):
            ring_step(p, step)
        if step == zn // 2:
            merge_terms()
        for p in (3, 4):
            ring_step(p, step - 1)
    for p in (3, 4):
        ring_step(p, zn // 2)

    total = r.kept[...]
    for d in range(1, yn):
        y_copy(d).wait_recv()
        total = total + r.y_got[d - 1].astype(F32)
    r.gx[...] = total.astype(BF16)

    for copy in started:
        copy.wait_send()

    @pl.when(z < zn - 2)
    def _():
        s_hop.wait_send()

    @pl.when(z >= 2)
    def _():
        d_hop.wait_send()

    for i in range(XN - 1):
        hand_copy(r.s_put, r.s_got, 0, i).wait_send()
        hand_copy(r.d_put, r.d_got, 1, i).wait_send()
    for p in range(len(cuts)):
        own_copy(p, 0).wait_send()
        own_copy(p, 1).wait_send()
        onward_copy(p).wait_send()
        for way in range(2):
            for step in range(hops(p)[way]):
                ring_hop(p, way, step).wait_send()
    for d in range(yn):
        pair_copy(d).wait_send()
        if d:
            y_copy(d).wait_send()


def finish_kernel(heads, gx_in, gw_in, gx, gwq, gwk, gwv, gwb):
    queries, steps = heads * HEAD_SIZE, heads * NH * HEAD_SIZE
    gx[...] = gx_in[...]
    gwq[...] = gw_in[:, :queries]
    gwv[...] = gw_in[:, queries : queries + steps]
    gwk[...] = gw_in[:, queries + steps : queries + 2 * steps]
    at = queries + 2 * steps
    gwb[...] = gw_in[:, at : at + 128].T[: heads * NH, :]


def vmem(count):
    return [pl.BlockSpec(memory_space=pltpu.VMEM)] * count


def per_device(tokens, w_query, w_key, w_value, w_beta, grad_out):
    count, depth = tokens.shape
    size = HEAD_SIZE
    heads = w_query.shape[1] // size
    rows = NH * count
    quarter = size // XN
    devices = lax.axis_size("seq")
    zn, yn = devices // XN, lax.axis_size("head") // 2
    shard, block = depth // devices, depth // (2 * yn)
    width = heads * (1 + 2 * NH) * size + 128
    pieces, hops = heads + 3, zn // 2
    w_beta_t = w_beta.T
    shape = jax.ShapeDtypeStruct
    dma = pltpu.SemaphoreType.DMA
    scratch = dict(
        tok=(tokens.shape, BF16),
        wk=(w_key.shape, BF16),
        wb=(w_beta_t.shape, BF16),
        wv=(w_value.shape, BF16),
        wq=(w_query.shape, BF16),
        go=(grad_out.shape, BF16),
        tokt=((zn, XN, shard, count), BF16),
        tt=((zn, shard, XN * count), BF16),
        system=((heads, rows, rows), F32),
        kr=((heads, rows, size), F32),
        vr=((heads, rows, size), F32),
        qr=((heads, count, size), F32),
        ur=((heads, rows, size), F32),
        pg=((heads, rows, size), F32),
        cols=((heads, rows, 8), F32),
        x_hi=((heads, rows, rows), BF16),
        x_lo=((heads, rows, rows), BF16),
        w_hi=((heads, rows, size), BF16),
        w_lo=((heads, rows, size), BF16),
        fresh=((heads, rows, size), BF16),
        rest=((heads, rows, size), F32),
        dk=((heads, rows, size), F32),
        solved=((heads, rows, size), F32),
        e_own=((heads, size, size), BF16),
        bl_own=((XN, heads, 2 * quarter, size), BF16),
        ebuf=((XN, heads, size, size), BF16),
        blbuf=((XN, heads, 2 * quarter, size), BF16),
        fz=((2, heads, size, size), BF16),
        sz=((2, heads, quarter, size), BF16),
        dz=((2, heads, quarter, size), BF16),
        pair=((heads, size, size), BF16),
        pair_t=((heads, size, size), BF16),
        s_mine=((heads, quarter, size), BF16),
        d_mine=((heads, quarter, size), BF16),
        e_pre=((heads, 3 * size, size), BF16),
        e_suf=((heads, size, 3 * size), BF16),
        s_off=((XN, heads, quarter, size), F32),
        d_off=((XN, heads, quarter, size), F32),
        s_in=((heads, quarter, size), BF16),
        d_in=((heads, quarter, size), BF16),
        s_out=((heads, quarter, size), BF16),
        d_out=((heads, quarter, size), BF16),
        s_put=((XN, heads, quarter, size), BF16),
        d_put=((XN, heads, quarter, size), BF16),
        s_got=((XN, heads, quarter, size), BF16),
        d_got=((XN, heads, quarter, size), BF16),
        g=((count, width), BF16),
        gbuf=((XN * count, width), BF16),
        part=((zn, shard, width), F32),
        ring_put=((2, hops, shard, width), BF16),
        ring_got=((2, hops, shard, width), BF16),
        pair_put=((yn, count, block), BF16),
        pair_got=((yn, count, block), BF16),
        y_put=((yn - 1, count, block), BF16),
        y_got=((yn - 1, count, block), BF16),
        own_part=((yn, count, block), F32),
        kept=((count, block), F32),
    )
    semaphores = dict(
        load_sem=(6,),
        tsend=(XN - 1,),
        trecv=(XN - 1,),
        esend=(heads, 3),
        erecv=(heads, 3),
        bsend=(XN - 1,),
        brecv=(XN - 1,),
        swap_send=(3,),
        swap_recv=(3,),
        zsend=(2,),
        zrecv=(2,),
        psend=(XN - 1, 2),
        precv=(XN - 1, 2),
        gsend=(pieces, 3),
        grecv=(pieces, 3),
        rsend=(pieces, 2, hops),
        rrecv=(pieces, 2, hops),
        csend=(yn,),
        crecv=(yn,),
        ysend=(yn - 1,),
        yrecv=(yn - 1,),
    )
    inputs = ("tok", "wq", "wk", "wv", "wb", "go")
    names = tuple(name + "_hbm" for name in inputs) + ("gx", "gw") + tuple(scratch) + tuple(semaphores)
    gx, gw = pl.pallas_call(
        functools.partial(layer_kernel, zn, yn, heads, names),
        out_shape=(shape((count, block), BF16), shape((shard, width), F32)),
        in_specs=[pl.BlockSpec(memory_space=pl.ANY)] * 6,
        out_specs=tuple(vmem(2)),
        scratch_shapes=[pltpu.VMEM(*spec) for spec in scratch.values()] + [dma(dims) for dims in semaphores.values()],
        compiler_params=pltpu.CompilerParams(collective_id=0, has_side_effects=True, vmem_limit_bytes=60 << 20),
        name="layer",
    )(tokens, w_query, w_key, w_value, w_beta_t, grad_out)
    outs = (
        shape((count, block), BF16),
        shape((shard, w_query.shape[1]), F32),
        shape((shard, w_key.shape[1]), F32),
        shape((shard, w_value.shape[1]), F32),
        shape((w_beta.shape[1], shard), F32),
    )
    grad_tokens, gwq, gwk, gwv, gwb = pl.pallas_call(
        functools.partial(finish_kernel, heads),
        out_shape=outs,
        in_specs=vmem(2),
        out_specs=tuple(vmem(5)),
        name="finish",
    )(gx, gw)
    return (grad_tokens, gwq, gwk, gwv, gwb.T)


def solution(mesh):
    in_specs = (
        P("seq", None),
        P(None, "head"),
        P(None, "head"),
        P(None, "head"),
        P(None, "head"),
        P("seq", "head"),
    )
    return jax.shard_map(
        per_device, mesh=mesh, in_specs=in_specs, out_specs=(P("seq", "head"),) * 5, check_vma=False
    )
```

```python
import functools
from types import SimpleNamespace

import jax
import jax.numpy as jnp
from jax import lax
from jax.experimental import pallas as pl
from jax.experimental.pallas import tpu as pltpu
from jax.sharding import PartitionSpec as P

HEAD_SIZE = 128
NH = 2
XN = 4
EPS = 1e-6
MESH = pl.DeviceIdType.MESH
F32 = jnp.float32
BF16 = jnp.bfloat16

NN = ((1,), (0,))
NT = ((1,), (1,))
TN = ((0,), (0,))


def dg(left, right, dims):
    return lax.dot_general(left, right, (dims, ((), ())), preferred_element_type=F32)


def parts(array):
    if isinstance(array, tuple):
        return array
    if array.dtype == BF16:
        return (array,)
    high = array.astype(BF16)
    return (high, (array - high.astype(F32)).astype(BF16))


def mm(left, right, dims=NN):
    left, right = parts(left), parts(right)
    total = dg(left[0], right[0], dims)
    if len(right) > 1:
        total = total + dg(left[0], right[1], dims)
    if len(left) > 1:
        total = total + dg(left[1], right[0], dims)
    return total


def mm1(left, right, dims=NN):
    return dg(left.astype(BF16), right.astype(BF16), dims)


def order_masks(tokens):
    rows = NH * tokens
    row = lax.broadcasted_iota(jnp.int32, (rows, rows), 0)
    col = lax.broadcasted_iota(jnp.int32, (rows, rows), 1)
    row_token, col_token = row & (tokens - 1), col & (tokens - 1)
    row_step, col_step = row >= tokens, col >= tokens
    return row, col, row_token, col_token, row_step, col_step


def score_mask(tokens):
    row = lax.broadcasted_iota(jnp.int32, (tokens, NH * tokens), 0)
    col = lax.broadcasted_iota(jnp.int32, (tokens, NH * tokens), 1)
    return (col & (tokens - 1)) <= row


def unit(matrix):
    scale = lax.rsqrt(jnp.sum(matrix * matrix, axis=-1, keepdims=True) + EPS)
    return matrix * scale, scale


def layer_kernel(zn, yn, heads, names, *refs):
    r = SimpleNamespace(**dict(zip(names, refs)))
    size = HEAD_SIZE
    seq, head = lax.axis_index("seq"), lax.axis_index("head")
    z, x = lax.div(seq, XN), lax.rem(seq, XN)
    y, core = lax.div(head, 2), lax.rem(head, 2)
    above, below = lax.rem(z + 1, zn), lax.rem(z + zn - 1, zn)
    odd = lax.rem(z, 2)
    beside = z + 1 - 2 * odd
    above2, below2 = lax.rem(z + 2, zn), lax.rem(z + zn - 2, zn)
    right, left, across = lax.rem(x + 1, XN), lax.rem(x + XN - 1, XN), lax.rem(x + 2, XN)
    peers = (right, left, across)
    partner = head + 1 - 2 * core
    quarter = size // XN
    count, depth = r.tok.shape
    rows = NH * count
    shard = depth // (zn * XN)
    block = r.gx.shape[1]
    width = r.g.shape[1]

    def row_device(member):
        return (z * XN + member, head)

    def remote(src, dst, send, recv, device):
        return pltpu.make_async_remote_copy(
            src_ref=src, dst_ref=dst, send_sem=send, recv_sem=recv, device_id=device, device_id_type=MESH
        )

    loads = {}
    for i, name in enumerate(("tok", "wk", "wb", "wv", "wq", "go")):
        loads[name] = pltpu.make_async_copy(getattr(r, name + "_hbm"), getattr(r, name), r.load_sem.at[i])
        loads[name].start()

    barrier = pltpu.get_barrier_semaphore()
    greeted = [row_device(peer) for peer in peers]
    greeted += [(zz * XN + x, head) for zz in (above, below, above2, below2)] + [(seq, partner)]
    greeted += [(seq, lax.rem(y + d, yn) * 2 + core) for d in range(1, yn)]
    for device in greeted:
        pl.semaphore_signal(barrier, inc=1, device_id=device, device_id_type=MESH)

    loads["tok"].wait()
    own_lanes = pl.ds(pl.multiple_of(x * count, count), count)
    started = []

    def start(copy):
        copy.start()
        started.append(copy)
        return copy

    row, col, row_token, col_token, row_step, col_step = order_masks(count)
    strict = (col_token < row_token) | ((col_token == row_token) & row_step & ~col_step)
    smask = score_mask(count)
    loads["wk"].wait()
    loads["wb"].wait()
    tok = r.tok[...]
    pk = dg(tok, r.wk[...], NN)
    beta_all = 2.0 * jax.nn.sigmoid(dg(tok, r.wb[...], NT))
    eye = jnp.where(row == col, 1.0, 0.0)
    inverses = []
    for h in range(heads):
        base = h * NH * size
        key, key_scale = unit(jnp.concatenate([pk[:, base : base + size], pk[:, base + size : base + 2 * size]], axis=0))
        beta = jnp.concatenate([beta_all[:, 2 * h : 2 * h + 1], beta_all[:, 2 * h + 1 : 2 * h + 2]], axis=0)
        r.kr[h] = key
        r.cols[h, :, 0:1] = beta
        r.cols[h, :, 1:2] = key_scale
        system = jnp.where(strict, beta * mm(key, key, NT), 0.0)
        r.system[h] = system
        inverses.append(eye - jnp.where(col_token == row_token, system, 0.0))
    loads["wv"].wait()
    loads["wq"].wait()
    loads["go"].wait()
    pv = dg(tok, r.wv[...], NN)
    pq = dg(tok, r.wq[...], NN)
    for h in range(heads):
        base = h * NH * size
        r.vr[h] = jnp.concatenate([pv[:, base : base + size], pv[:, base + size : base + 2 * size]], axis=0)
        query, query_scale = unit(pq[:, h * size : (h + 1) * size])
        r.qr[h] = query
        r.cols[h, 0:count, 2:3] = query_scale
    level = 1
    while level < count:
        span = 2 * level - 1
        pick = ((row_token & span) >= level) & ((col_token | span) == (row_token | span)) & ((col_token & span) < level)
        for h in range(heads):
            inverse = parts(inverses[h])
            inner = mm(jnp.where(pick, r.system[h], 0.0), inverse)
            inverses[h] = inverses[h] - mm(inverse, inner)
        level *= 2
    e_copies = {}
    for h in range(heads):
        key, beta = r.kr[h], r.cols[h, :, 0:1]
        inverse = parts(inverses[h])
        r.x_hi[h], r.x_lo[h] = inverse
        solved = mm(inverse, jnp.concatenate([beta * key, beta * r.vr[h]], axis=1))
        w_rows = parts(solved[:, :size])
        r.w_hi[h], r.w_lo[h] = w_rows
        r.ur[h] = solved[:, size:]
        r.e_own[h] = mm(key, w_rows, TN).astype(BF16)
        if h == 0:
            pl.semaphore_wait(barrier, len(greeted))
        for way, device in enumerate((right, left)):
            e_copies[h, way] = start(
                remote(r.e_own.at[h], r.ebuf.at[x, h], r.esend.at[h, way], r.erecv.at[h, way], row_device(device))
            )
    for h in range(heads):
        query, go = r.qr[h], r.go[:, h * size : (h + 1) * size]
        key = parts(r.kr[h])
        scores = jnp.where(smask, mm(query, key, NT), 0.0)
        pulled = mm(scores, go, TN)
        r.pg[h] = pulled
        offset = mm(r.ur[h], key, TN)
        adjoint = mm(go, query, TN) - mm(pulled, (r.w_hi[h], r.w_lo[h]), TN)
        for j in range(XN):
            r.bl_own[j, h, :quarter, :] = offset[j * quarter : (j + 1) * quarter].astype(BF16)
            r.bl_own[j, h, quarter:, :] = adjoint[j * quarter : (j + 1) * quarter].astype(BF16)
    bl_copies = [
        start(remote(r.bl_own.at[peer], r.blbuf.at[x], r.bsend.at[i], r.brecv.at[i], row_device(peer)))
        for i, peer in enumerate(peers)
    ]
    r.ebuf[x] = r.e_own[...]
    r.blbuf[x] = r.bl_own[x]

    @pl.when(z < 2)
    def _():
        r.s_in[...] = jnp.zeros_like(r.s_in)

    @pl.when(z >= zn - 2)
    def _():
        r.d_in[...] = jnp.zeros_like(r.d_in)

    e_onward = []
    for h in range(heads):
        for way in range(2):
            e_copies[h, way].wait_recv()
        to_right = h < heads // 2
        spot = r.ebuf.at[left if to_right else right, h]
        device = row_device(right if to_right else left)
        e_onward.append(start(remote(spot, spot, r.esend.at[h, 2], r.erecv.at[h, 2], device)))
    for zz in range(zn):
        lanes = r.tok[:, zz * XN * shard : (zz + 1) * XN * shard]
        r.tokt[zz] = lanes.T.reshape(XN, shard, count)
    for copy in bl_copies:
        copy.wait_recv()
    for copy in e_onward:
        copy.wait_recv()
    tok_copies = [
        start(remote(r.tokt.at[:, peer], r.tt.at[:, :, own_lanes], r.tsend.at[i], r.trecv.at[i], row_device(peer)))
        for i, peer in enumerate(peers)
    ]
    r.tt[:, :, own_lanes] = r.tokt[:, x]

    pair_swaps = []
    for h in range(heads):
        maps = [r.ebuf[j, h] for j in range(XN)]
        wide = [m.astype(F32) for m in maps]
        e10 = wide[1] + wide[0] - dg(maps[1], maps[0], NN)
        e32 = wide[3] + wide[2] - dg(maps[3], maps[2], NN)
        e10s, e32s = parts(e10), parts(e32)
        e210 = wide[2] + e10 - mm(maps[2], e10s)
        e321 = e32 + wide[1] - mm(e32s, maps[1])
        r.fz[odd, h] = (e32 + e10 - mm(e32s, e10s)).astype(BF16)
        for i, m in enumerate((maps[0], e10s[0], e210.astype(BF16))):
            r.e_pre[h, i * size : (i + 1) * size, :] = m
        for i, m in enumerate((maps[3], e32s[0], e321.astype(BF16))):
            r.e_suf[h, :, i * size : (i + 1) * size] = m
        off = r.blbuf[0, h, :quarter, :].astype(F32)
        for j in range(1, XN):
            r.s_off[j, h] = off
            off = off - mm(off, maps[j], NT) + r.blbuf[j, h, :quarter, :].astype(F32)
        r.sz[odd, h] = off.astype(BF16)
        off = r.blbuf[XN - 1, h, quarter:, :].astype(F32)
        for j in range(XN - 2, -1, -1):
            r.d_off[j, h] = off
            off = off - mm(off, maps[j], NN) + r.blbuf[j, h, quarter:, :].astype(F32)
        r.dz[odd, h] = off.astype(BF16)
        pair_swaps.append(
            [
                start(
                    remote(
                        ref.at[odd, h],
                        ref.at[odd, h],
                        r.swap_send.at[h, i],
                        r.swap_recv.at[h, i],
                        (beside * XN + x, head),
                    )
                )
                for i, ref in enumerate((r.fz, r.sz, r.dz))
            ]
        )

    for h in range(heads):
        for copy in pair_swaps[h]:
            copy.wait_recv()
        low, high = r.fz[0, h], r.fz[1, h]
        both = high.astype(F32) + low.astype(F32) - dg(high, low, NN)
        r.pair[h] = both.astype(BF16)
        r.pair_t[h] = both.T.astype(BF16)
        s_low, d_high = r.sz[0, h], r.dz[1, h]
        r.s_off[0, h] = s_low.astype(F32) - dg(s_low, high, NT) + r.sz[1, h].astype(F32)
        r.d_off[XN - 1, h] = d_high.astype(F32) - dg(d_high, low, NN) + r.dz[0, h].astype(F32)

    s_hop = remote(r.s_out, r.s_in, r.zsend.at[0], r.zrecv.at[0], (above2 * XN + x, head))
    d_hop = remote(r.d_out, r.d_in, r.zsend.at[1], r.zrecv.at[1], (below2 * XN + x, head))

    def hand_copy(put, got, kind, i):
        return remote(put.at[peers[i]], got.at[x], r.psend.at[i, kind], r.precv.at[i, kind], row_device(peers[i]))

    def hand_out(put, got, kind):
        for i in reversed(range(XN - 1)):
            hand_copy(put, got, kind, i).start()
        got[x] = put[x]

    def forward():
        @pl.when(z >= 2)
        def _():
            s_hop.wait_recv()

        @pl.when(z < zn - 2)
        def _():
            for h in range(heads):
                state = r.s_in[h]
                moved = dg(state, r.pair_t[h], NN)
                r.s_out[h] = (state.astype(F32) + r.s_off[0, h] - moved).astype(BF16)
            s_hop.start()

        @pl.when(odd == 0)
        def _():
            r.s_mine[...] = r.s_in[...]

        @pl.when(odd == 1)
        def _():
            for h in range(heads):
                state = r.s_in[h]
                moved = dg(state, r.fz[0, h], NT)
                r.s_mine[h] = (state.astype(F32) + r.sz[0, h].astype(F32) - moved).astype(BF16)

        for h in range(heads):
            state = r.s_mine[h]
            moved = dg(state, r.e_pre[h], NT)
            r.s_put[0, h] = state
            for j in range(1, XN):
                value = state.astype(F32) + r.s_off[j, h] - moved[:, (j - 1) * size : j * size]
                r.s_put[j, h] = value.astype(BF16)
        hand_out(r.s_put, r.s_got, 0)

    def backward():
        @pl.when(z < zn - 2)
        def _():
            d_hop.wait_recv()

        @pl.when(z >= 2)
        def _():
            for h in range(heads):
                state = r.d_in[h]
                moved = dg(state, r.pair[h], NN)
                r.d_out[h] = (state.astype(F32) + r.d_off[XN - 1, h] - moved).astype(BF16)
            d_hop.start()

        @pl.when(odd == 1)
        def _():
            r.d_mine[...] = r.d_in[...]

        @pl.when(odd == 0)
        def _():
            for h in range(heads):
                state = r.d_in[h]
                moved = dg(state, r.fz[1, h], NN)
                r.d_mine[h] = (state.astype(F32) + r.dz[1, h].astype(F32) - moved).astype(BF16)

        for h in range(heads):
            state = r.d_mine[h]
            moved = dg(state, r.e_suf[h], NN)
            r.d_put[XN - 1, h] = state
            for j in range(XN - 1):
                i = XN - 2 - j
                value = state.astype(F32) + r.d_off[j, h] - moved[:, i * size : (i + 1) * size]
                r.d_put[j, h] = value.astype(BF16)
        hand_out(r.d_put, r.d_got, 1)

    two = NH * size
    value_at = heads * size
    key_at = value_at + heads * two
    logit_at = key_at + heads * two
    cuts = [0, value_at] + [value_at + (h + 1) * two for h in range(heads)] + [logit_at - size, width]
    cuts = list(zip(cuts[:-1], cuts[1:]))
    to_right = (True, False, True, False, True)

    def member_rows(member):
        return pl.ds(pl.multiple_of(member * count, count), count)

    def own_copy(p, way):
        lo, hi = cuts[p]
        device = row_device(left if way else right)
        src = r.g.at[:, lo:hi]
        return remote(src, r.gbuf.at[member_rows(x), lo:hi], r.gsend.at[p, way], r.grecv.at[p, way], device)

    def onward_copy(p):
        lo, hi = cuts[p]
        spot = r.gbuf.at[member_rows(left if to_right[p] else right), lo:hi]
        return remote(spot, spot, r.gsend.at[p, 2], r.grecv.at[p, 2], row_device(right if to_right[p] else left))

    def offer(p):
        lo, hi = cuts[p]
        own_copy(p, 0).start()
        own_copy(p, 1).start()
        r.gbuf[member_rows(x), lo:hi] = r.g[:, lo:hi]

    def relay(p):
        own_copy(p, 0).wait_recv()
        own_copy(p, 1).wait_recv()
        onward_copy(p).start()

    def joined(got, h):
        return jnp.concatenate([got[j, h] for j in range(XN)], axis=0)

    def query_grads():
        for i in range(XN - 1):
            hand_copy(r.s_put, r.s_got, 0, i).wait_recv()
        for h in range(heads):
            state = joined(r.s_got, h)
            keys, query = r.kr[h].astype(BF16), r.qr[h]
            go = r.go[:, h * size : (h + 1) * size]
            fresh = (r.ur[h] - mm((r.w_hi[h], r.w_lo[h]), state, NT)).astype(BF16)
            r.fresh[h] = fresh
            d_scores = jnp.where(smask, dg(go, fresh, NT), 0.0).astype(BF16)
            d_query = dg(go, state, NN) + dg(d_scores, keys, NN)
            d_query = r.cols[h, 0:count, 2:3] * (d_query - query * jnp.sum(query * d_query, axis=-1, keepdims=True))
            r.g[:, h * size : (h + 1) * size] = d_query.astype(BF16)
            if h == heads - 1:
                offer(0)
            r.rest[h] = r.vr[h] - dg(keys, state, NT)
            r.dk[h] = mm1(d_scores, query, TN)

    early = z < zn // 2

    @pl.when(early)
    def _():
        forward()
        query_grads()
        backward()
        relay(0)

    @pl.when(jnp.logical_not(early))
    def _():
        backward()
        forward()
        query_grads()

    for i in range(XN - 1):
        hand_copy(r.d_put, r.d_got, 1, i).wait_recv()
    adjoints = [joined(r.d_got, h) for h in range(heads)]
    for h in range(heads):
        keys = parts(r.kr[h])
        solved = mm((r.x_hi[h], r.x_lo[h]), r.pg[h] + mm(keys, adjoints[h], NT), TN)
        r.solved[h] = solved
        d_value = r.cols[h, :, 0:1] * solved
        for j in range(NH):
            at = value_at + h * two + j * size
            r.g[:, at : at + size] = d_value[j * count : (j + 1) * count].astype(BF16)
        offer(1 + h)

    logits = []
    for h in range(heads):
        key = r.kr[h]
        beta, key_scale = r.cols[h, :, 0:1], r.cols[h, :, 1:2]
        solved, fresh, keys = r.solved[h], r.fresh[h], key.astype(BF16)
        d_system = jnp.where(strict, -mm1(solved, fresh, NT), 0.0)
        gram = dg(keys, keys, NT)
        d_beta = jnp.sum(solved * r.rest[h], axis=-1, keepdims=True) + jnp.sum(d_system * gram, axis=-1, keepdims=True)
        d_gram = (beta * d_system).astype(BF16)
        d_key = (
            r.dk[h]
            + dg(fresh, adjoints[h], NN)
            - mm1(beta * solved, joined(r.s_got, h))
            + dg(d_gram, keys, NN)
            + dg(d_gram, keys, TN)
        )
        d_key = key_scale * (d_key - key * jnp.sum(key * d_key, axis=-1, keepdims=True))
        d_logit = d_beta * beta * (1.0 - 0.5 * beta)
        for j in range(NH):
            at = key_at + h * two + j * size
            r.g[:, at : at + size] = d_key[j * count : (j + 1) * count].astype(BF16)
            logits.append(d_logit[j * count : (j + 1) * count])
    pad = jnp.zeros((count, size - len(logits)), F32)
    r.g[:, logit_at:] = jnp.concatenate(logits + [pad], axis=1).astype(BF16)
    offer(3)
    offer(4)

    def input_term(d, side):
        lo = pl.multiple_of((lax.rem(y + d, yn) * 2 + side) * block, block)
        spot = pl.ds(lo, block)
        total = dg(r.g[:, :value_at], r.wq[spot, :], NT)
        total = total + dg(r.g[:, value_at:key_at], r.wv[spot, :], NT)
        total = total + dg(r.g[:, key_at:logit_at], r.wk[spot, :], NT)
        return total + dg(r.g[:, logit_at : logit_at + heads * NH], r.wb[:, spot], NN)

    def pair_copy(d):
        return remote(r.pair_put.at[d], r.pair_got.at[d], r.csend.at[d], r.crecv.at[d], (seq, partner))

    def y_copy(d):
        i = d - 1
        device = (seq, lax.rem(y + d, yn) * 2 + core)
        return remote(r.y_put.at[i], r.y_got.at[i], r.ysend.at[i], r.yrecv.at[i], device)

    order = list(range(1, yn)) + [0]

    def partner_terms():
        for d in order:
            r.pair_put[d] = input_term(d, 1 - core).astype(BF16)
            pair_copy(d).start()

    def own_terms():
        for d in order:
            r.own_part[d] = input_term(d, core)

    def merge_terms():
        for d in order:
            pair_copy(d).wait_recv()
            term = r.own_part[d] + r.pair_got[d].astype(F32)
            if d:
                r.y_put[d - 1] = term.astype(BF16)
                y_copy(d).start()
            else:
                r.kept[...] = term

    def hops(p):
        return (zn // 2, zn // 2 - 1) if p % 2 == 0 else (zn // 2 - 1, zn // 2)

    def ring_hop(p, way, step):
        lo, hi = cuts[p]
        device = ((below if way else above) * XN + x, head)
        put, got = r.ring_put.at[way, step, :, lo:hi], r.ring_got.at[way, step, :, lo:hi]
        return remote(put, got, r.rsend.at[p, way, step], r.rrecv.at[p, way, step], device)

    def ring_step(p, step):
        lo, hi = cuts[p]
        if step == 0:
            onward_copy(p).wait_recv()
            left_side = r.tt[...].reshape(zn * shard, XN * count)
            r.part[:, :, lo:hi] = dg(left_side, r.gbuf[:, lo:hi], NN).reshape(zn, shard, hi - lo)
        lengths = hops(p)
        for way in range(2):
            length = lengths[way]
            if step >= length:
                continue
            chunk = lax.rem(z + zn + (step - length if way else length - step), zn)
            value = r.part[chunk, :, lo:hi]
            if step > 0:
                ring_hop(p, way, step - 1).wait_recv()
                value = value + r.ring_got[way, step - 1, :, lo:hi].astype(F32)
            r.ring_put[way, step, :, lo:hi] = value.astype(BF16)
            ring_hop(p, way, step).start()
        if step == max(lengths):
            value = r.part[z, :, lo:hi]
            for way in range(2):
                ring_hop(p, way, lengths[way] - 1).wait_recv()
                value = value + r.ring_got[way, lengths[way] - 1, :, lo:hi].astype(F32)
            r.gw[:, lo:hi] = value

    @pl.when(jnp.logical_not(early))
    def _():
        relay(0)

    partner_terms()
    relay(1)
    relay(2)
    for copy in tok_copies:
        copy.wait_recv()
    ring_step(0, 0)
    own_terms()
    relay(3)
    ring_step(1, 0)
    ring_step(2, 0)
    relay(4)
    for p in (0, 1, 2):
        ring_step(p, 1)
    ring_step(3, 0)
    ring_step(4, 0)
    for step in range(2, zn // 2 + 1):
        for p in (0, 1, 2):
            ring_step(p, step)
        if step == zn // 2:
            merge_terms()
        for p in (3, 4):
            ring_step(p, step - 1)
    for p in (3, 4):
        ring_step(p, zn // 2)

    total = r.kept[...]
    for d in range(1, yn):
        y_copy(d).wait_recv()
        total = total + r.y_got[d - 1].astype(F32)
    r.gx[...] = total.astype(BF16)

    for copy in started:
        copy.wait_send()

    @pl.when(z < zn - 2)
    def _():
        s_hop.wait_send()

    @pl.when(z >= 2)
    def _():
        d_hop.wait_send()

    for i in range(XN - 1):
        hand_copy(r.s_put, r.s_got, 0, i).wait_send()
        hand_copy(r.d_put, r.d_got, 1, i).wait_send()
    for p in range(len(cuts)):
        own_copy(p, 0).wait_send()
        own_copy(p, 1).wait_send()
        onward_copy(p).wait_send()
        for way in range(2):
            for step in range(hops(p)[way]):
                ring_hop(p, way, step).wait_send()
    for d in range(yn):
        pair_copy(d).wait_send()
        if d:
            y_copy(d).wait_send()


def finish_kernel(heads, gx_in, gw_in, gx, gwq, gwk, gwv, gwb):
    queries, steps = heads * HEAD_SIZE, heads * NH * HEAD_SIZE
    gx[...] = gx_in[...]
    gwq[...] = gw_in[:, :queries]
    gwv[...] = gw_in[:, queries : queries + steps]
    gwk[...] = gw_in[:, queries + steps : queries + 2 * steps]
    at = queries + 2 * steps
    gwb[...] = gw_in[:, at : at + 128].T[: heads * NH, :]


def vmem(count):
    return [pl.BlockSpec(memory_space=pltpu.VMEM)] * count


def per_device(tokens, w_query, w_key, w_value, w_beta, grad_out):
    count, depth = tokens.shape
    size = HEAD_SIZE
    heads = w_query.shape[1] // size
    rows = NH * count
    quarter = size // XN
    devices = lax.axis_size("seq")
    zn, yn = devices // XN, lax.axis_size("head") // 2
    shard, block = depth // devices, depth // (2 * yn)
    width = heads * (1 + 2 * NH) * size + 128
    pieces, hops = heads + 3, zn // 2
    w_beta_t = w_beta.T
    shape = jax.ShapeDtypeStruct
    dma = pltpu.SemaphoreType.DMA
    scratch = dict(
        tok=(tokens.shape, BF16),
        wk=(w_key.shape, BF16),
        wb=(w_beta_t.shape, BF16),
        wv=(w_value.shape, BF16),
        wq=(w_query.shape, BF16),
        go=(grad_out.shape, BF16),
        tokt=((zn, XN, shard, count), BF16),
        tt=((zn, shard, XN * count), BF16),
        system=((heads, rows, rows), F32),
        kr=((heads, rows, size), F32),
        vr=((heads, rows, size), F32),
        qr=((heads, count, size), F32),
        ur=((heads, rows, size), F32),
        pg=((heads, rows, size), F32),
        cols=((heads, rows, 8), F32),
        x_hi=((heads, rows, rows), BF16),
        x_lo=((heads, rows, rows), BF16),
        w_hi=((heads, rows, size), BF16),
        w_lo=((heads, rows, size), BF16),
        fresh=((heads, rows, size), BF16),
        rest=((heads, rows, size), F32),
        dk=((heads, rows, size), F32),
        solved=((heads, rows, size), F32),
        e_own=((heads, size, size), BF16),
        bl_own=((XN, heads, 2 * quarter, size), BF16),
        ebuf=((XN, heads, size, size), BF16),
        blbuf=((XN, heads, 2 * quarter, size), BF16),
        fz=((2, heads, size, size), BF16),
        sz=((2, heads, quarter, size), BF16),
        dz=((2, heads, quarter, size), BF16),
        pair=((heads, size, size), BF16),
        pair_t=((heads, size, size), BF16),
        s_mine=((heads, quarter, size), BF16),
        d_mine=((heads, quarter, size), BF16),
        e_pre=((heads, 3 * size, size), BF16),
        e_suf=((heads, size, 3 * size), BF16),
        s_off=((XN, heads, quarter, size), F32),
        d_off=((XN, heads, quarter, size), F32),
        s_in=((heads, quarter, size), BF16),
        d_in=((heads, quarter, size), BF16),
        s_out=((heads, quarter, size), BF16),
        d_out=((heads, quarter, size), BF16),
        s_put=((XN, heads, quarter, size), BF16),
        d_put=((XN, heads, quarter, size), BF16),
        s_got=((XN, heads, quarter, size), BF16),
        d_got=((XN, heads, quarter, size), BF16),
        g=((count, width), BF16),
        gbuf=((XN * count, width), BF16),
        part=((zn, shard, width), F32),
        ring_put=((2, hops, shard, width), BF16),
        ring_got=((2, hops, shard, width), BF16),
        pair_put=((yn, count, block), BF16),
        pair_got=((yn, count, block), BF16),
        y_put=((yn - 1, count, block), BF16),
        y_got=((yn - 1, count, block), BF16),
        own_part=((yn, count, block), F32),
        kept=((count, block), F32),
    )
    semaphores = dict(
        load_sem=(6,),
        tsend=(XN - 1,),
        trecv=(XN - 1,),
        esend=(heads, 3),
        erecv=(heads, 3),
        bsend=(XN - 1,),
        brecv=(XN - 1,),
        swap_send=(heads, 3),
        swap_recv=(heads, 3),
        zsend=(2,),
        zrecv=(2,),
        psend=(XN - 1, 2),
        precv=(XN - 1, 2),
        gsend=(pieces, 3),
        grecv=(pieces, 3),
        rsend=(pieces, 2, hops),
        rrecv=(pieces, 2, hops),
        csend=(yn,),
        crecv=(yn,),
        ysend=(yn - 1,),
        yrecv=(yn - 1,),
    )
    inputs = ("tok", "wq", "wk", "wv", "wb", "go")
    names = tuple(name + "_hbm" for name in inputs) + ("gx", "gw") + tuple(scratch) + tuple(semaphores)
    gx, gw = pl.pallas_call(
        functools.partial(layer_kernel, zn, yn, heads, names),
        out_shape=(shape((count, block), BF16), shape((shard, width), F32)),
        in_specs=[pl.BlockSpec(memory_space=pl.ANY)] * 6,
        out_specs=tuple(vmem(2)),
        scratch_shapes=[pltpu.VMEM(*spec) for spec in scratch.values()] + [dma(dims) for dims in semaphores.values()],
        compiler_params=pltpu.CompilerParams(collective_id=0, has_side_effects=True, vmem_limit_bytes=60 << 20),
        name="layer",
    )(tokens, w_query, w_key, w_value, w_beta_t, grad_out)
    outs = (
        shape((count, block), BF16),
        shape((shard, w_query.shape[1]), F32),
        shape((shard, w_key.shape[1]), F32),
        shape((shard, w_value.shape[1]), F32),
        shape((w_beta.shape[1], shard), F32),
    )
    grad_tokens, gwq, gwk, gwv, gwb = pl.pallas_call(
        functools.partial(finish_kernel, heads),
        out_shape=outs,
        in_specs=vmem(2),
        out_specs=tuple(vmem(5)),
        name="finish",
    )(gx, gw)
    return (grad_tokens, gwq, gwk, gwv, gwb.T)


def solution(mesh):
    in_specs = (
        P("seq", None),
        P(None, "head"),
        P(None, "head"),
        P(None, "head"),
        P(None, "head"),
        P("seq", "head"),
    )
    return jax.shard_map(
        per_device, mesh=mesh, in_specs=in_specs, out_specs=(P("seq", "head"),) * 5, check_vma=False
    )
```

```python
import functools
from types import SimpleNamespace

import jax
import jax.numpy as jnp
from jax import lax
from jax.experimental import pallas as pl
from jax.experimental.pallas import tpu as pltpu
from jax.sharding import PartitionSpec as P

HEAD_SIZE = 128
NH = 2
XN = 4
EPS = 1e-6
MESH = pl.DeviceIdType.MESH
F32 = jnp.float32
BF16 = jnp.bfloat16

NN = ((1,), (0,))
NT = ((1,), (1,))
TN = ((0,), (0,))


def dg(left, right, dims):
    return lax.dot_general(left, right, (dims, ((), ())), preferred_element_type=F32)


def parts(array):
    if isinstance(array, tuple):
        return array
    if array.dtype == BF16:
        return (array,)
    high = array.astype(BF16)
    return (high, (array - high.astype(F32)).astype(BF16))


def mm(left, right, dims=NN):
    left, right = parts(left), parts(right)
    total = dg(left[0], right[0], dims)
    if len(right) > 1:
        total = total + dg(left[0], right[1], dims)
    if len(left) > 1:
        total = total + dg(left[1], right[0], dims)
    return total


def mm1(left, right, dims=NN):
    return dg(left.astype(BF16), right.astype(BF16), dims)


def order_masks(tokens):
    rows = NH * tokens
    row = lax.broadcasted_iota(jnp.int32, (rows, rows), 0)
    col = lax.broadcasted_iota(jnp.int32, (rows, rows), 1)
    row_token, col_token = row & (tokens - 1), col & (tokens - 1)
    row_step, col_step = row >= tokens, col >= tokens
    return row, col, row_token, col_token, row_step, col_step


def score_mask(tokens):
    row = lax.broadcasted_iota(jnp.int32, (tokens, NH * tokens), 0)
    col = lax.broadcasted_iota(jnp.int32, (tokens, NH * tokens), 1)
    return (col & (tokens - 1)) <= row


def unit(matrix):
    scale = lax.rsqrt(jnp.sum(matrix * matrix, axis=-1, keepdims=True) + EPS)
    return matrix * scale, scale


def layer_kernel(zn, yn, heads, names, *refs):
    r = SimpleNamespace(**dict(zip(names, refs)))
    size = HEAD_SIZE
    seq, head = lax.axis_index("seq"), lax.axis_index("head")
    z, x = lax.div(seq, XN), lax.rem(seq, XN)
    y, core = lax.div(head, 2), lax.rem(head, 2)
    above, below = lax.rem(z + 1, zn), lax.rem(z + zn - 1, zn)
    odd = lax.rem(z, 2)
    beside = z + 1 - 2 * odd
    above2, below2 = lax.rem(z + 2, zn), lax.rem(z + zn - 2, zn)
    right, left, across = lax.rem(x + 1, XN), lax.rem(x + XN - 1, XN), lax.rem(x + 2, XN)
    peers = (right, left, across)
    partner = head + 1 - 2 * core
    quarter = size // XN
    count, depth = r.tok.shape
    rows = NH * count
    shard = depth // (zn * XN)
    block = r.gx.shape[1]
    width = r.g.shape[1]

    def row_device(member):
        return (z * XN + member, head)

    def remote(src, dst, send, recv, device):
        return pltpu.make_async_remote_copy(
            src_ref=src, dst_ref=dst, send_sem=send, recv_sem=recv, device_id=device, device_id_type=MESH
        )

    loads = {}
    for i, name in enumerate(("tok", "wk", "wb", "wv", "wq", "go")):
        loads[name] = pltpu.make_async_copy(getattr(r, name + "_hbm"), getattr(r, name), r.load_sem.at[i])
        loads[name].start()

    barrier = pltpu.get_barrier_semaphore()
    greeted = [row_device(peer) for peer in peers]
    greeted += [(zz * XN + x, head) for zz in (above, below, above2, below2)] + [(seq, partner)]
    greeted += [(seq, lax.rem(y + d, yn) * 2 + core) for d in range(1, yn)]
    for device in greeted:
        pl.semaphore_signal(barrier, inc=1, device_id=device, device_id_type=MESH)

    loads["tok"].wait()
    own_lanes = pl.ds(pl.multiple_of(x * count, count), count)
    started = []

    def start(copy):
        copy.start()
        started.append(copy)
        return copy

    row, col, row_token, col_token, row_step, col_step = order_masks(count)
    strict = (col_token < row_token) | ((col_token == row_token) & row_step & ~col_step)
    smask = score_mask(count)
    loads["wk"].wait()
    loads["wb"].wait()
    tok = r.tok[...]
    pk = dg(tok, r.wk[...], NN)
    beta_all = 2.0 * jax.nn.sigmoid(dg(tok, r.wb[...], NT))
    eye = jnp.where(row == col, 1.0, 0.0)
    inverses = []
    for h in range(heads):
        base = h * NH * size
        key, key_scale = unit(jnp.concatenate([pk[:, base : base + size], pk[:, base + size : base + 2 * size]], axis=0))
        beta = jnp.concatenate([beta_all[:, 2 * h : 2 * h + 1], beta_all[:, 2 * h + 1 : 2 * h + 2]], axis=0)
        r.kr[h] = key
        r.cols[h, :, 0:1] = beta
        r.cols[h, :, 1:2] = key_scale
        system = jnp.where(strict, beta * mm(key, key, NT), 0.0)
        r.system[h] = system
        inverses.append(eye - jnp.where(col_token == row_token, system, 0.0))
    loads["wv"].wait()
    loads["wq"].wait()
    loads["go"].wait()
    pv = dg(tok, r.wv[...], NN)
    pq = dg(tok, r.wq[...], NN)
    for h in range(heads):
        base = h * NH * size
        r.vr[h] = jnp.concatenate([pv[:, base : base + size], pv[:, base + size : base + 2 * size]], axis=0)
        query, query_scale = unit(pq[:, h * size : (h + 1) * size])
        r.qr[h] = query
        r.cols[h, 0:count, 2:3] = query_scale
    level = 1
    while level < count:
        span = 2 * level - 1
        pick = ((row_token & span) >= level) & ((col_token | span) == (row_token | span)) & ((col_token & span) < level)
        for h in range(heads):
            inverse = parts(inverses[h])
            inner = mm(jnp.where(pick, r.system[h], 0.0), inverse)
            inverses[h] = inverses[h] - mm(inverse, inner)
        level *= 2
    e_copies = {}
    for h in range(heads):
        key, beta = r.kr[h], r.cols[h, :, 0:1]
        inverse = parts(inverses[h])
        r.x_hi[h], r.x_lo[h] = inverse
        solved = mm(inverse, jnp.concatenate([beta * key, beta * r.vr[h]], axis=1))
        w_rows = parts(solved[:, :size])
        r.w_hi[h], r.w_lo[h] = w_rows
        r.ur[h] = solved[:, size:]
        r.e_own[h] = mm(key, w_rows, TN).astype(BF16)
        if h == 0:
            pl.semaphore_wait(barrier, len(greeted))
        for way, device in enumerate((right, left)):
            e_copies[h, way] = start(
                remote(r.e_own.at[h], r.ebuf.at[x, h], r.esend.at[h, way], r.erecv.at[h, way], row_device(device))
            )
    for h in range(heads):
        query, go = r.qr[h], r.go[:, h * size : (h + 1) * size]
        key = parts(r.kr[h])
        scores = jnp.where(smask, mm(query, key, NT), 0.0)
        pulled = mm(scores, go, TN)
        r.pg[h] = pulled
        offset = mm(r.ur[h], key, TN)
        adjoint = mm(go, query, TN) - mm(pulled, (r.w_hi[h], r.w_lo[h]), TN)
        for j in range(XN):
            r.bl_own[j, h, :quarter, :] = offset[j * quarter : (j + 1) * quarter].astype(BF16)
            r.bl_own[j, h, quarter:, :] = adjoint[j * quarter : (j + 1) * quarter].astype(BF16)
    bl_copies = [
        start(remote(r.bl_own.at[peer], r.blbuf.at[x], r.bsend.at[i], r.brecv.at[i], row_device(peer)))
        for i, peer in enumerate(peers)
    ]
    r.ebuf[x] = r.e_own[...]
    r.blbuf[x] = r.bl_own[x]

    @pl.when(z < 2)
    def _():
        r.s_in[...] = jnp.zeros_like(r.s_in)

    @pl.when(z >= zn - 2)
    def _():
        r.d_in[...] = jnp.zeros_like(r.d_in)

    e_onward = []
    for h in range(heads):
        for way in range(2):
            e_copies[h, way].wait_recv()
        to_right = h < heads // 2
        spot = r.ebuf.at[left if to_right else right, h]
        device = row_device(right if to_right else left)
        e_onward.append(start(remote(spot, spot, r.esend.at[h, 2], r.erecv.at[h, 2], device)))
    for zz in range(zn):
        lanes = r.tok[:, zz * XN * shard : (zz + 1) * XN * shard]
        r.tokt[zz] = lanes.T.reshape(XN, shard, count)
    for copy in bl_copies:
        copy.wait_recv()
    for copy in e_onward:
        copy.wait_recv()
    tok_copies = [
        start(remote(r.tokt.at[:, peer], r.tt.at[:, :, own_lanes], r.tsend.at[i], r.trecv.at[i], row_device(peer)))
        for i, peer in enumerate(peers)
    ]
    r.tt[:, :, own_lanes] = r.tokt[:, x]

    pair_swaps = []
    for h in range(heads):
        maps = [r.ebuf[j, h] for j in range(XN)]
        wide = [m.astype(F32) for m in maps]
        e10 = wide[1] + wide[0] - dg(maps[1], maps[0], NN)
        e32 = wide[3] + wide[2] - dg(maps[3], maps[2], NN)
        e10s, e32s = parts(e10), parts(e32)
        e210 = wide[2] + e10 - mm(maps[2], e10s)
        e321 = e32 + wide[1] - mm(e32s, maps[1])
        r.fz[odd, h] = (e32 + e10 - mm(e32s, e10s)).astype(BF16)
        for i, m in enumerate((maps[0], e10s[0], e210.astype(BF16))):
            r.e_pre[h, i * size : (i + 1) * size, :] = m
        for i, m in enumerate((maps[3], e32s[0], e321.astype(BF16))):
            r.e_suf[h, :, i * size : (i + 1) * size] = m
        off = r.blbuf[0, h, :quarter, :].astype(F32)
        for j in range(1, XN):
            r.s_off[j, h] = off
            off = off - mm(off, maps[j], NT) + r.blbuf[j, h, :quarter, :].astype(F32)
        r.sz[odd, h] = off.astype(BF16)
        off = r.blbuf[XN - 1, h, quarter:, :].astype(F32)
        for j in range(XN - 2, -1, -1):
            r.d_off[j, h] = off
            off = off - mm(off, maps[j], NN) + r.blbuf[j, h, quarter:, :].astype(F32)
        r.dz[odd, h] = off.astype(BF16)
        pair_swaps.append(
            [
                start(
                    remote(
                        ref.at[odd, h],
                        ref.at[odd, h],
                        r.swap_send.at[h, i],
                        r.swap_recv.at[h, i],
                        (beside * XN + x, head),
                    )
                )
                for i, ref in enumerate((r.fz, r.sz, r.dz))
            ]
        )

    for h in range(heads):
        for copy in pair_swaps[h]:
            copy.wait_recv()
        low, high = r.fz[0, h], r.fz[1, h]
        both = high.astype(F32) + low.astype(F32) - dg(high, low, NN)
        r.pair[h] = both.astype(BF16)
        r.pair_t[h] = both.T.astype(BF16)
        s_low, d_high = r.sz[0, h], r.dz[1, h]
        r.s_off[0, h] = s_low.astype(F32) - dg(s_low, high, NT) + r.sz[1, h].astype(F32)
        r.d_off[XN - 1, h] = d_high.astype(F32) - dg(d_high, low, NN) + r.dz[0, h].astype(F32)

    s_hop = remote(r.s_out, r.s_in, r.zsend.at[0], r.zrecv.at[0], (above2 * XN + x, head))
    d_hop = remote(r.d_out, r.d_in, r.zsend.at[1], r.zrecv.at[1], (below2 * XN + x, head))

    def hand_copy(put, got, kind, i):
        return remote(put.at[peers[i]], got.at[x], r.psend.at[i, kind], r.precv.at[i, kind], row_device(peers[i]))

    def hand_out(put, got, kind):
        for i in reversed(range(XN - 1)):
            hand_copy(put, got, kind, i).start()
        got[x] = put[x]

    def forward():
        @pl.when(z >= 2)
        def _():
            s_hop.wait_recv()

        @pl.when(z < zn - 2)
        def _():
            for h in range(heads):
                state = r.s_in[h]
                moved = dg(state, r.pair_t[h], NN)
                r.s_out[h] = (state.astype(F32) + r.s_off[0, h] - moved).astype(BF16)
            s_hop.start()

        @pl.when(odd == 0)
        def _():
            r.s_mine[...] = r.s_in[...]

        @pl.when(odd == 1)
        def _():
            for h in range(heads):
                state = r.s_in[h]
                moved = dg(state, r.fz[0, h], NT)
                r.s_mine[h] = (state.astype(F32) + r.sz[0, h].astype(F32) - moved).astype(BF16)

        for h in range(heads):
            state = r.s_mine[h]
            moved = dg(state, r.e_pre[h], NT)
            r.s_put[0, h] = state
            for j in range(1, XN):
                value = state.astype(F32) + r.s_off[j, h] - moved[:, (j - 1) * size : j * size]
                r.s_put[j, h] = value.astype(BF16)
        hand_out(r.s_put, r.s_got, 0)

    def backward():
        @pl.when(z < zn - 2)
        def _():
            d_hop.wait_recv()

        @pl.when(z >= 2)
        def _():
            for h in range(heads):
                state = r.d_in[h]
                moved = dg(state, r.pair[h], NN)
                r.d_out[h] = (state.astype(F32) + r.d_off[XN - 1, h] - moved).astype(BF16)
            d_hop.start()

        @pl.when(odd == 1)
        def _():
            r.d_mine[...] = r.d_in[...]

        @pl.when(odd == 0)
        def _():
            for h in range(heads):
                state = r.d_in[h]
                moved = dg(state, r.fz[1, h], NN)
                r.d_mine[h] = (state.astype(F32) + r.dz[1, h].astype(F32) - moved).astype(BF16)

        for h in range(heads):
            state = r.d_mine[h]
            moved = dg(state, r.e_suf[h], NN)
            r.d_put[XN - 1, h] = state
            for j in range(XN - 1):
                i = XN - 2 - j
                value = state.astype(F32) + r.d_off[j, h] - moved[:, i * size : (i + 1) * size]
                r.d_put[j, h] = value.astype(BF16)
        hand_out(r.d_put, r.d_got, 1)

    two = NH * size
    value_at = heads * size
    key_at = value_at + heads * two
    logit_at = key_at + heads * two
    cuts = [0, value_at] + [value_at + (h + 1) * two for h in range(heads)] + [logit_at - size, width]
    cuts = list(zip(cuts[:-1], cuts[1:]))
    to_right = (True, False, True, False, True)

    def member_rows(member):
        return pl.ds(pl.multiple_of(member * count, count), count)

    def own_copy(p, way):
        lo, hi = cuts[p]
        device = row_device(left if way else right)
        src = r.g.at[:, lo:hi]
        return remote(src, r.gbuf.at[member_rows(x), lo:hi], r.gsend.at[p, way], r.grecv.at[p, way], device)

    def onward_copy(p):
        lo, hi = cuts[p]
        spot = r.gbuf.at[member_rows(left if to_right[p] else right), lo:hi]
        return remote(spot, spot, r.gsend.at[p, 2], r.grecv.at[p, 2], row_device(right if to_right[p] else left))

    def offer(p):
        lo, hi = cuts[p]
        own_copy(p, 0).start()
        own_copy(p, 1).start()
        r.gbuf[member_rows(x), lo:hi] = r.g[:, lo:hi]

    def relay(p):
        own_copy(p, 0).wait_recv()
        own_copy(p, 1).wait_recv()
        onward_copy(p).start()

    def joined(got, h):
        return jnp.concatenate([got[j, h] for j in range(XN)], axis=0)

    def query_grads():
        for i in range(XN - 1):
            hand_copy(r.s_put, r.s_got, 0, i).wait_recv()
        for h in range(heads):
            state = joined(r.s_got, h)
            keys, query = r.kr[h].astype(BF16), r.qr[h]
            go = r.go[:, h * size : (h + 1) * size]
            fresh = (r.ur[h] - mm((r.w_hi[h], r.w_lo[h]), state, NT)).astype(BF16)
            r.fresh[h] = fresh
            d_scores = jnp.where(smask, dg(go, fresh, NT), 0.0).astype(BF16)
            d_query = dg(go, state, NN) + dg(d_scores, keys, NN)
            d_query = r.cols[h, 0:count, 2:3] * (d_query - query * jnp.sum(query * d_query, axis=-1, keepdims=True))
            r.g[:, h * size : (h + 1) * size] = d_query.astype(BF16)
            if h == heads - 1:
                offer(0)
            r.rest[h] = r.vr[h] - dg(keys, state, NT)
            r.dk[h] = mm1(d_scores, query, TN)

    early = z < zn // 2

    @pl.when(early)
    def _():
        forward()
        query_grads()
        backward()
        relay(0)

    @pl.when(jnp.logical_not(early))
    def _():
        backward()
        forward()
        query_grads()

    for i in range(XN - 1):
        hand_copy(r.d_put, r.d_got, 1, i).wait_recv()
    adjoints = [joined(r.d_got, h) for h in range(heads)]
    for h in range(heads):
        keys = parts(r.kr[h])
        solved = mm((r.x_hi[h], r.x_lo[h]), r.pg[h] + mm(keys, adjoints[h], NT), TN)
        r.solved[h] = solved
        d_value = r.cols[h, :, 0:1] * solved
        for j in range(NH):
            at = value_at + h * two + j * size
            r.g[:, at : at + size] = d_value[j * count : (j + 1) * count].astype(BF16)
        offer(1 + h)

    logits = []
    for h in range(heads):
        key = r.kr[h]
        beta, key_scale = r.cols[h, :, 0:1], r.cols[h, :, 1:2]
        solved, fresh, keys = r.solved[h], r.fresh[h], key.astype(BF16)
        d_system = jnp.where(strict, -mm1(solved, fresh, NT), 0.0)
        gram = dg(keys, keys, NT)
        d_beta = jnp.sum(solved * r.rest[h], axis=-1, keepdims=True) + jnp.sum(d_system * gram, axis=-1, keepdims=True)
        d_gram = (beta * d_system).astype(BF16)
        d_key = (
            r.dk[h]
            + dg(fresh, adjoints[h], NN)
            - mm1(beta * solved, joined(r.s_got, h))
            + dg(d_gram, keys, NN)
            + dg(d_gram, keys, TN)
        )
        d_key = key_scale * (d_key - key * jnp.sum(key * d_key, axis=-1, keepdims=True))
        d_logit = d_beta * beta * (1.0 - 0.5 * beta)
        for j in range(NH):
            at = key_at + h * two + j * size
            r.g[:, at : at + size] = d_key[j * count : (j + 1) * count].astype(BF16)
            logits.append(d_logit[j * count : (j + 1) * count])
    pad = jnp.zeros((count, size - len(logits)), F32)
    r.g[:, logit_at:] = jnp.concatenate(logits + [pad], axis=1).astype(BF16)
    offer(3)
    offer(4)

    def input_term(d, side):
        lo = pl.multiple_of((lax.rem(y + d, yn) * 2 + side) * block, block)
        spot = pl.ds(lo, block)
        total = dg(r.g[:, :value_at], r.wq[spot, :], NT)
        total = total + dg(r.g[:, value_at:key_at], r.wv[spot, :], NT)
        total = total + dg(r.g[:, key_at:logit_at], r.wk[spot, :], NT)
        return total + dg(r.g[:, logit_at : logit_at + heads * NH], r.wb[:, spot], NN)

    def pair_copy(d):
        return remote(r.pair_put.at[d], r.pair_got.at[d], r.csend.at[d], r.crecv.at[d], (seq, partner))

    def y_copy(d):
        i = d - 1
        device = (seq, lax.rem(y + d, yn) * 2 + core)
        return remote(r.y_put.at[i], r.y_got.at[i], r.ysend.at[i], r.yrecv.at[i], device)

    order = list(range(1, yn)) + [0]

    def partner_terms():
        for d in order:
            r.pair_put[d] = input_term(d, 1 - core).astype(BF16)
            pair_copy(d).start()

    def own_terms():
        for d in order:
            r.own_part[d] = input_term(d, core)

    def merge_terms():
        for d in order:
            pair_copy(d).wait_recv()
            term = r.own_part[d] + r.pair_got[d].astype(F32)
            if d:
                r.y_put[d - 1] = term.astype(BF16)
                y_copy(d).start()
            else:
                r.kept[...] = term

    def hops(p):
        return (zn // 2, zn // 2 - 1) if p % 2 == 0 else (zn // 2 - 1, zn // 2)

    def ring_hop(p, way, step):
        lo, hi = cuts[p]
        device = ((below if way else above) * XN + x, head)
        put, got = r.ring_put.at[way, step, :, lo:hi], r.ring_got.at[way, step, :, lo:hi]
        return remote(put, got, r.rsend.at[p, way, step], r.rrecv.at[p, way, step], device)

    def ring_step(p, step):
        lo, hi = cuts[p]
        if step == 0:
            onward_copy(p).wait_recv()
            left_side = r.tt[...].reshape(zn * shard, XN * count)
            r.part[:, :, lo:hi] = dg(left_side, r.gbuf[:, lo:hi], NN).reshape(zn, shard, hi - lo)
        lengths = hops(p)
        for way in range(2):
            length = lengths[way]
            if step >= length:
                continue
            chunk = lax.rem(z + zn + (step - length if way else length - step), zn)
            value = r.part[chunk, :, lo:hi]
            if step > 0:
                ring_hop(p, way, step - 1).wait_recv()
                value = value + r.ring_got[way, step - 1, :, lo:hi].astype(F32)
            r.ring_put[way, step, :, lo:hi] = value.astype(BF16)
            ring_hop(p, way, step).start()
        if step == max(lengths):
            value = r.part[z, :, lo:hi]
            for way in range(2):
                ring_hop(p, way, lengths[way] - 1).wait_recv()
                value = value + r.ring_got[way, lengths[way] - 1, :, lo:hi].astype(F32)
            r.gw[:, lo:hi] = value

    @pl.when(jnp.logical_not(early))
    def _():
        relay(0)

    partner_terms()
    relay(1)
    relay(2)
    for copy in tok_copies:
        copy.wait_recv()
    ring_step(0, 0)
    relay(3)
    ring_step(1, 0)
    ring_step(2, 0)
    relay(4)
    own_terms()
    for p in (0, 1, 2):
        ring_step(p, 1)
    ring_step(3, 0)
    ring_step(4, 0)
    for step in range(2, zn // 2 + 1):
        for p in (0, 1, 2):
            ring_step(p, step)
        if step == zn // 2:
            merge_terms()
        for p in (3, 4):
            ring_step(p, step - 1)
    for p in (3, 4):
        ring_step(p, zn // 2)

    total = r.kept[...]
    for d in range(1, yn):
        y_copy(d).wait_recv()
        total = total + r.y_got[d - 1].astype(F32)
    r.gx[...] = total.astype(BF16)

    for copy in started:
        copy.wait_send()

    @pl.when(z < zn - 2)
    def _():
        s_hop.wait_send()

    @pl.when(z >= 2)
    def _():
        d_hop.wait_send()

    for i in range(XN - 1):
        hand_copy(r.s_put, r.s_got, 0, i).wait_send()
        hand_copy(r.d_put, r.d_got, 1, i).wait_send()
    for p in range(len(cuts)):
        own_copy(p, 0).wait_send()
        own_copy(p, 1).wait_send()
        onward_copy(p).wait_send()
        for way in range(2):
            for step in range(hops(p)[way]):
                ring_hop(p, way, step).wait_send()
    for d in range(yn):
        pair_copy(d).wait_send()
        if d:
            y_copy(d).wait_send()


def finish_kernel(heads, gx_in, gw_in, gx, gwq, gwk, gwv, gwb):
    queries, steps = heads * HEAD_SIZE, heads * NH * HEAD_SIZE
    gx[...] = gx_in[...]
    gwq[...] = gw_in[:, :queries]
    gwv[...] = gw_in[:, queries : queries + steps]
    gwk[...] = gw_in[:, queries + steps : queries + 2 * steps]
    at = queries + 2 * steps
    gwb[...] = gw_in[:, at : at + 128].T[: heads * NH, :]


def vmem(count):
    return [pl.BlockSpec(memory_space=pltpu.VMEM)] * count


def per_device(tokens, w_query, w_key, w_value, w_beta, grad_out):
    count, depth = tokens.shape
    size = HEAD_SIZE
    heads = w_query.shape[1] // size
    rows = NH * count
    quarter = size // XN
    devices = lax.axis_size("seq")
    zn, yn = devices // XN, lax.axis_size("head") // 2
    shard, block = depth // devices, depth // (2 * yn)
    width = heads * (1 + 2 * NH) * size + 128
    pieces, hops = heads + 3, zn // 2
    w_beta_t = w_beta.T
    shape = jax.ShapeDtypeStruct
    dma = pltpu.SemaphoreType.DMA
    scratch = dict(
        tok=(tokens.shape, BF16),
        wk=(w_key.shape, BF16),
        wb=(w_beta_t.shape, BF16),
        wv=(w_value.shape, BF16),
        wq=(w_query.shape, BF16),
        go=(grad_out.shape, BF16),
        tokt=((zn, XN, shard, count), BF16),
        tt=((zn, shard, XN * count), BF16),
        system=((heads, rows, rows), F32),
        kr=((heads, rows, size), F32),
        vr=((heads, rows, size), F32),
        qr=((heads, count, size), F32),
        ur=((heads, rows, size), F32),
        pg=((heads, rows, size), F32),
        cols=((heads, rows, 8), F32),
        x_hi=((heads, rows, rows), BF16),
        x_lo=((heads, rows, rows), BF16),
        w_hi=((heads, rows, size), BF16),
        w_lo=((heads, rows, size), BF16),
        fresh=((heads, rows, size), BF16),
        rest=((heads, rows, size), F32),
        dk=((heads, rows, size), F32),
        solved=((heads, rows, size), F32),
        e_own=((heads, size, size), BF16),
        bl_own=((XN, heads, 2 * quarter, size), BF16),
        ebuf=((XN, heads, size, size), BF16),
        blbuf=((XN, heads, 2 * quarter, size), BF16),
        fz=((2, heads, size, size), BF16),
        sz=((2, heads, quarter, size), BF16),
        dz=((2, heads, quarter, size), BF16),
        pair=((heads, size, size), BF16),
        pair_t=((heads, size, size), BF16),
        s_mine=((heads, quarter, size), BF16),
        d_mine=((heads, quarter, size), BF16),
        e_pre=((heads, 3 * size, size), BF16),
        e_suf=((heads, size, 3 * size), BF16),
        s_off=((XN, heads, quarter, size), F32),
        d_off=((XN, heads, quarter, size), F32),
        s_in=((heads, quarter, size), BF16),
        d_in=((heads, quarter, size), BF16),
        s_out=((heads, quarter, size), BF16),
        d_out=((heads, quarter, size), BF16),
        s_put=((XN, heads, quarter, size), BF16),
        d_put=((XN, heads, quarter, size), BF16),
        s_got=((XN, heads, quarter, size), BF16),
        d_got=((XN, heads, quarter, size), BF16),
        g=((count, width), BF16),
        gbuf=((XN * count, width), BF16),
        part=((zn, shard, width), F32),
        ring_put=((2, hops, shard, width), BF16),
        ring_got=((2, hops, shard, width), BF16),
        pair_put=((yn, count, block), BF16),
        pair_got=((yn, count, block), BF16),
        y_put=((yn - 1, count, block), BF16),
        y_got=((yn - 1, count, block), BF16),
        own_part=((yn, count, block), F32),
        kept=((count, block), F32),
    )
    semaphores = dict(
        load_sem=(6,),
        tsend=(XN - 1,),
        trecv=(XN - 1,),
        esend=(heads, 3),
        erecv=(heads, 3),
        bsend=(XN - 1,),
        brecv=(XN - 1,),
        swap_send=(heads, 3),
        swap_recv=(heads, 3),
        zsend=(2,),
        zrecv=(2,),
        psend=(XN - 1, 2),
        precv=(XN - 1, 2),
        gsend=(pieces, 3),
        grecv=(pieces, 3),
        rsend=(pieces, 2, hops),
        rrecv=(pieces, 2, hops),
        csend=(yn,),
        crecv=(yn,),
        ysend=(yn - 1,),
        yrecv=(yn - 1,),
    )
    inputs = ("tok", "wq", "wk", "wv", "wb", "go")
    names = tuple(name + "_hbm" for name in inputs) + ("gx", "gw") + tuple(scratch) + tuple(semaphores)
    gx, gw = pl.pallas_call(
        functools.partial(layer_kernel, zn, yn, heads, names),
        out_shape=(shape((count, block), BF16), shape((shard, width), F32)),
        in_specs=[pl.BlockSpec(memory_space=pl.ANY)] * 6,
        out_specs=tuple(vmem(2)),
        scratch_shapes=[pltpu.VMEM(*spec) for spec in scratch.values()] + [dma(dims) for dims in semaphores.values()],
        compiler_params=pltpu.CompilerParams(collective_id=0, has_side_effects=True, vmem_limit_bytes=60 << 20),
        name="layer",
    )(tokens, w_query, w_key, w_value, w_beta_t, grad_out)
    outs = (
        shape((count, block), BF16),
        shape((shard, w_query.shape[1]), F32),
        shape((shard, w_key.shape[1]), F32),
        shape((shard, w_value.shape[1]), F32),
        shape((w_beta.shape[1], shard), F32),
    )
    grad_tokens, gwq, gwk, gwv, gwb = pl.pallas_call(
        functools.partial(finish_kernel, heads),
        out_shape=outs,
        in_specs=vmem(2),
        out_specs=tuple(vmem(5)),
        name="finish",
    )(gx, gw)
    return (grad_tokens, gwq, gwk, gwv, gwb.T)


def solution(mesh):
    in_specs = (
        P("seq", None),
        P(None, "head"),
        P(None, "head"),
        P(None, "head"),
        P(None, "head"),
        P("seq", "head"),
    )
    return jax.shard_map(
        per_device, mesh=mesh, in_specs=in_specs, out_specs=(P("seq", "head"),) * 5, check_vma=False
    )
```

```python
import functools
from types import SimpleNamespace

import jax
import jax.numpy as jnp
from jax import lax
from jax.experimental import pallas as pl
from jax.experimental.pallas import tpu as pltpu
from jax.sharding import PartitionSpec as P

HEAD_SIZE = 128
NH = 2
XN = 4
EPS = 1e-6
MESH = pl.DeviceIdType.MESH
F32 = jnp.float32
BF16 = jnp.bfloat16

NN = ((1,), (0,))
NT = ((1,), (1,))
TN = ((0,), (0,))


def dg(left, right, dims):
    return lax.dot_general(left, right, (dims, ((), ())), preferred_element_type=F32)


def parts(array):
    if isinstance(array, tuple):
        return array
    if array.dtype == BF16:
        return (array,)
    high = array.astype(BF16)
    return (high, (array - high.astype(F32)).astype(BF16))


def mm(left, right, dims=NN):
    left, right = parts(left), parts(right)
    total = dg(left[0], right[0], dims)
    if len(right) > 1:
        total = total + dg(left[0], right[1], dims)
    if len(left) > 1:
        total = total + dg(left[1], right[0], dims)
    return total


def mm1(left, right, dims=NN):
    return dg(left.astype(BF16), right.astype(BF16), dims)


def order_masks(tokens):
    rows = NH * tokens
    row = lax.broadcasted_iota(jnp.int32, (rows, rows), 0)
    col = lax.broadcasted_iota(jnp.int32, (rows, rows), 1)
    row_token, col_token = row & (tokens - 1), col & (tokens - 1)
    row_step, col_step = row >= tokens, col >= tokens
    return row, col, row_token, col_token, row_step, col_step


def score_mask(tokens):
    row = lax.broadcasted_iota(jnp.int32, (tokens, NH * tokens), 0)
    col = lax.broadcasted_iota(jnp.int32, (tokens, NH * tokens), 1)
    return (col & (tokens - 1)) <= row


def unit(matrix):
    scale = lax.rsqrt(jnp.sum(matrix * matrix, axis=-1, keepdims=True) + EPS)
    return matrix * scale, scale


def layer_kernel(zn, yn, heads, names, *refs):
    r = SimpleNamespace(**dict(zip(names, refs)))
    size = HEAD_SIZE
    seq, head = lax.axis_index("seq"), lax.axis_index("head")
    z, x = lax.div(seq, XN), lax.rem(seq, XN)
    y, core = lax.div(head, 2), lax.rem(head, 2)
    above, below = lax.rem(z + 1, zn), lax.rem(z + zn - 1, zn)
    odd = lax.rem(z, 2)
    beside = z + 1 - 2 * odd
    above2, below2 = lax.rem(z + 2, zn), lax.rem(z + zn - 2, zn)
    right, left, across = lax.rem(x + 1, XN), lax.rem(x + XN - 1, XN), lax.rem(x + 2, XN)
    peers = (right, left, across)
    partner = head + 1 - 2 * core
    quarter = size // XN
    count, depth = r.tok.shape
    rows = NH * count
    shard = depth // (zn * XN)
    block = r.gx.shape[1]
    width = r.g.shape[1]

    def row_device(member):
        return (z * XN + member, head)

    def remote(src, dst, send, recv, device):
        return pltpu.make_async_remote_copy(
            src_ref=src, dst_ref=dst, send_sem=send, recv_sem=recv, device_id=device, device_id_type=MESH
        )

    loads = {}
    for i, name in enumerate(("tok", "wk", "wb", "wv", "wq", "go")):
        loads[name] = pltpu.make_async_copy(getattr(r, name + "_hbm"), getattr(r, name), r.load_sem.at[i])
        loads[name].start()

    barrier = pltpu.get_barrier_semaphore()
    greeted = [row_device(peer) for peer in peers]
    greeted += [(zz * XN + x, head) for zz in (above, below, above2, below2)] + [(seq, partner)]
    greeted += [(seq, lax.rem(y + d, yn) * 2 + core) for d in range(1, yn)]
    for device in greeted:
        pl.semaphore_signal(barrier, inc=1, device_id=device, device_id_type=MESH)

    loads["tok"].wait()
    own_lanes = pl.ds(pl.multiple_of(x * count, count), count)
    started = []

    def start(copy):
        copy.start()
        started.append(copy)
        return copy

    row, col, row_token, col_token, row_step, col_step = order_masks(count)
    strict = (col_token < row_token) | ((col_token == row_token) & row_step & ~col_step)
    smask = score_mask(count)
    loads["wk"].wait()
    loads["wb"].wait()
    tok = r.tok[...]
    pk = dg(tok, r.wk[...], NN)
    beta_all = 2.0 * jax.nn.sigmoid(dg(tok, r.wb[...], NT))
    eye = jnp.where(row == col, 1.0, 0.0)
    inverses = []
    for h in range(heads):
        base = h * NH * size
        key, key_scale = unit(jnp.concatenate([pk[:, base : base + size], pk[:, base + size : base + 2 * size]], axis=0))
        beta = jnp.concatenate([beta_all[:, 2 * h : 2 * h + 1], beta_all[:, 2 * h + 1 : 2 * h + 2]], axis=0)
        r.kr[h] = key
        r.cols[h, :, 0:1] = beta
        r.cols[h, :, 1:2] = key_scale
        system = jnp.where(strict, beta * mm(key, key, NT), 0.0)
        r.system[h] = system
        inverses.append(eye - jnp.where(col_token == row_token, system, 0.0))
    loads["wv"].wait()
    loads["wq"].wait()
    loads["go"].wait()
    pv = dg(tok, r.wv[...], NN)
    pq = dg(tok, r.wq[...], NN)
    for h in range(heads):
        base = h * NH * size
        r.vr[h] = jnp.concatenate([pv[:, base : base + size], pv[:, base + size : base + 2 * size]], axis=0)
        query, query_scale = unit(pq[:, h * size : (h + 1) * size])
        r.qr[h] = query
        r.cols[h, 0:count, 2:3] = query_scale
    level = 1
    while level < count:
        span = 2 * level - 1
        pick = ((row_token & span) >= level) & ((col_token | span) == (row_token | span)) & ((col_token & span) < level)
        for h in range(heads):
            inverse = parts(inverses[h])
            inner = mm(jnp.where(pick, r.system[h], 0.0), inverse)
            inverses[h] = inverses[h] - mm(inverse, inner)
        level *= 2
    e_copies = {}
    for h in range(heads):
        key, beta = r.kr[h], r.cols[h, :, 0:1]
        inverse = parts(inverses[h])
        r.x_hi[h], r.x_lo[h] = inverse
        solved = mm(inverse, jnp.concatenate([beta * key, beta * r.vr[h]], axis=1))
        w_rows = parts(solved[:, :size])
        r.w_hi[h], r.w_lo[h] = w_rows
        r.ur[h] = solved[:, size:]
        r.e_own[h] = mm(key, w_rows, TN).astype(BF16)
        if h == 0:
            pl.semaphore_wait(barrier, len(greeted))
        for way, device in enumerate((right, left)):
            e_copies[h, way] = start(
                remote(r.e_own.at[h], r.ebuf.at[x, h], r.esend.at[h, way], r.erecv.at[h, way], row_device(device))
            )
    for h in range(heads):
        query, go = r.qr[h], r.go[:, h * size : (h + 1) * size]
        key = parts(r.kr[h])
        scores = jnp.where(smask, mm(query, key, NT), 0.0)
        pulled = mm(scores, go, TN)
        r.pg[h] = pulled
        offset = mm(r.ur[h], key, TN)
        adjoint = mm(go, query, TN) - mm(pulled, (r.w_hi[h], r.w_lo[h]), TN)
        for j in range(XN):
            r.bl_own[j, h, :quarter, :] = offset[j * quarter : (j + 1) * quarter].astype(BF16)
            r.bl_own[j, h, quarter:, :] = adjoint[j * quarter : (j + 1) * quarter].astype(BF16)
    bl_copies = [
        start(remote(r.bl_own.at[peer], r.blbuf.at[x], r.bsend.at[i], r.brecv.at[i], row_device(peer)))
        for i, peer in reversed(list(enumerate(peers)))
    ]
    r.ebuf[x] = r.e_own[...]
    r.blbuf[x] = r.bl_own[x]

    @pl.when(z < 2)
    def _():
        r.s_in[...] = jnp.zeros_like(r.s_in)

    @pl.when(z >= zn - 2)
    def _():
        r.d_in[...] = jnp.zeros_like(r.d_in)

    e_onward = []
    for h in range(heads):
        for way in range(2):
            e_copies[h, way].wait_recv()
        to_right = h < heads // 2
        spot = r.ebuf.at[left if to_right else right, h]
        device = row_device(right if to_right else left)
        e_onward.append(start(remote(spot, spot, r.esend.at[h, 2], r.erecv.at[h, 2], device)))
    for zz in range(zn):
        lanes = r.tok[:, zz * XN * shard : (zz + 1) * XN * shard]
        r.tokt[zz] = lanes.T.reshape(XN, shard, count)
    for copy in bl_copies:
        copy.wait_recv()
    for copy in e_onward:
        copy.wait_recv()
    tok_copies = [
        start(remote(r.tokt.at[:, peer], r.tt.at[:, :, own_lanes], r.tsend.at[i], r.trecv.at[i], row_device(peer)))
        for i, peer in enumerate(peers)
    ]
    r.tt[:, :, own_lanes] = r.tokt[:, x]

    pair_swaps = []
    for h in range(heads):
        maps = [r.ebuf[j, h] for j in range(XN)]
        wide = [m.astype(F32) for m in maps]
        e10 = wide[1] + wide[0] - dg(maps[1], maps[0], NN)
        e32 = wide[3] + wide[2] - dg(maps[3], maps[2], NN)
        e10s, e32s = parts(e10), parts(e32)
        e210 = wide[2] + e10 - mm(maps[2], e10s)
        e321 = e32 + wide[1] - mm(e32s, maps[1])
        r.fz[odd, h] = (e32 + e10 - mm(e32s, e10s)).astype(BF16)
        for i, m in enumerate((maps[0], e10s[0], e210.astype(BF16))):
            r.e_pre[h, i * size : (i + 1) * size, :] = m
        for i, m in enumerate((maps[3], e32s[0], e321.astype(BF16))):
            r.e_suf[h, :, i * size : (i + 1) * size] = m
        off = r.blbuf[0, h, :quarter, :].astype(F32)
        for j in range(1, XN):
            r.s_off[j, h] = off
            off = off - mm(off, maps[j], NT) + r.blbuf[j, h, :quarter, :].astype(F32)
        r.sz[odd, h] = off.astype(BF16)
        off = r.blbuf[XN - 1, h, quarter:, :].astype(F32)
        for j in range(XN - 2, -1, -1):
            r.d_off[j, h] = off
            off = off - mm(off, maps[j], NN) + r.blbuf[j, h, quarter:, :].astype(F32)
        r.dz[odd, h] = off.astype(BF16)
        pair_swaps.append(
            [
                start(
                    remote(
                        ref.at[odd, h],
                        ref.at[odd, h],
                        r.swap_send.at[h, i],
                        r.swap_recv.at[h, i],
                        (beside * XN + x, head),
                    )
                )
                for i, ref in enumerate((r.fz, r.sz, r.dz))
            ]
        )

    for h in range(heads):
        for copy in pair_swaps[h]:
            copy.wait_recv()
        low, high = r.fz[0, h], r.fz[1, h]
        both = high.astype(F32) + low.astype(F32) - dg(high, low, NN)
        r.pair[h] = both.astype(BF16)
        r.pair_t[h] = both.T.astype(BF16)
        s_low, d_high = r.sz[0, h], r.dz[1, h]
        r.s_off[0, h] = s_low.astype(F32) - dg(s_low, high, NT) + r.sz[1, h].astype(F32)
        r.d_off[XN - 1, h] = d_high.astype(F32) - dg(d_high, low, NN) + r.dz[0, h].astype(F32)

    s_hop = remote(r.s_out, r.s_in, r.zsend.at[0], r.zrecv.at[0], (above2 * XN + x, head))
    d_hop = remote(r.d_out, r.d_in, r.zsend.at[1], r.zrecv.at[1], (below2 * XN + x, head))

    def hand_copy(put, got, kind, i):
        return remote(put.at[peers[i]], got.at[x], r.psend.at[i, kind], r.precv.at[i, kind], row_device(peers[i]))

    def hand_out(put, got, kind):
        for i in reversed(range(XN - 1)):
            hand_copy(put, got, kind, i).start()
        got[x] = put[x]

    def forward():
        @pl.when(z >= 2)
        def _():
            s_hop.wait_recv()

        @pl.when(z < zn - 2)
        def _():
            for h in range(heads):
                state = r.s_in[h]
                moved = dg(state, r.pair_t[h], NN)
                r.s_out[h] = (state.astype(F32) + r.s_off[0, h] - moved).astype(BF16)
            s_hop.start()

        @pl.when(odd == 0)
        def _():
            r.s_mine[...] = r.s_in[...]

        @pl.when(odd == 1)
        def _():
            for h in range(heads):
                state = r.s_in[h]
                moved = dg(state, r.fz[0, h], NT)
                r.s_mine[h] = (state.astype(F32) + r.sz[0, h].astype(F32) - moved).astype(BF16)

        for h in range(heads):
            state = r.s_mine[h]
            moved = dg(state, r.e_pre[h], NT)
            r.s_put[0, h] = state
            for j in range(1, XN):
                value = state.astype(F32) + r.s_off[j, h] - moved[:, (j - 1) * size : j * size]
                r.s_put[j, h] = value.astype(BF16)
        hand_out(r.s_put, r.s_got, 0)

    def backward():
        @pl.when(z < zn - 2)
        def _():
            d_hop.wait_recv()

        @pl.when(z >= 2)
        def _():
            for h in range(heads):
                state = r.d_in[h]
                moved = dg(state, r.pair[h], NN)
                r.d_out[h] = (state.astype(F32) + r.d_off[XN - 1, h] - moved).astype(BF16)
            d_hop.start()

        @pl.when(odd == 1)
        def _():
            r.d_mine[...] = r.d_in[...]

        @pl.when(odd == 0)
        def _():
            for h in range(heads):
                state = r.d_in[h]
                moved = dg(state, r.fz[1, h], NN)
                r.d_mine[h] = (state.astype(F32) + r.dz[1, h].astype(F32) - moved).astype(BF16)

        for h in range(heads):
            state = r.d_mine[h]
            moved = dg(state, r.e_suf[h], NN)
            r.d_put[XN - 1, h] = state
            for j in range(XN - 1):
                i = XN - 2 - j
                value = state.astype(F32) + r.d_off[j, h] - moved[:, i * size : (i + 1) * size]
                r.d_put[j, h] = value.astype(BF16)
        hand_out(r.d_put, r.d_got, 1)

    two = NH * size
    value_at = heads * size
    key_at = value_at + heads * two
    logit_at = key_at + heads * two
    cuts = [0, value_at] + [value_at + (h + 1) * two for h in range(heads)] + [logit_at - size, width]
    cuts = list(zip(cuts[:-1], cuts[1:]))
    to_right = (True, False, True, False, True)

    def member_rows(member):
        return pl.ds(pl.multiple_of(member * count, count), count)

    def own_copy(p, way):
        lo, hi = cuts[p]
        device = row_device(left if way else right)
        src = r.g.at[:, lo:hi]
        return remote(src, r.gbuf.at[member_rows(x), lo:hi], r.gsend.at[p, way], r.grecv.at[p, way], device)

    def onward_copy(p):
        lo, hi = cuts[p]
        spot = r.gbuf.at[member_rows(left if to_right[p] else right), lo:hi]
        return remote(spot, spot, r.gsend.at[p, 2], r.grecv.at[p, 2], row_device(right if to_right[p] else left))

    def offer(p):
        lo, hi = cuts[p]
        own_copy(p, 0).start()
        own_copy(p, 1).start()
        r.gbuf[member_rows(x), lo:hi] = r.g[:, lo:hi]

    def relay(p):
        own_copy(p, 0).wait_recv()
        own_copy(p, 1).wait_recv()
        onward_copy(p).start()

    def joined(got, h):
        return jnp.concatenate([got[j, h] for j in range(XN)], axis=0)

    def query_grads():
        for i in range(XN - 1):
            hand_copy(r.s_put, r.s_got, 0, i).wait_recv()
        for h in range(heads):
            state = joined(r.s_got, h)
            keys, query = r.kr[h].astype(BF16), r.qr[h]
            go = r.go[:, h * size : (h + 1) * size]
            fresh = (r.ur[h] - mm((r.w_hi[h], r.w_lo[h]), state, NT)).astype(BF16)
            r.fresh[h] = fresh
            d_scores = jnp.where(smask, dg(go, fresh, NT), 0.0).astype(BF16)
            d_query = dg(go, state, NN) + dg(d_scores, keys, NN)
            d_query = r.cols[h, 0:count, 2:3] * (d_query - query * jnp.sum(query * d_query, axis=-1, keepdims=True))
            r.g[:, h * size : (h + 1) * size] = d_query.astype(BF16)
            if h == heads - 1:
                offer(0)
            r.rest[h] = r.vr[h] - dg(keys, state, NT)
            r.dk[h] = mm1(d_scores, query, TN)

    early = z < zn // 2

    @pl.when(early)
    def _():
        forward()
        query_grads()
        backward()
        relay(0)

    @pl.when(jnp.logical_not(early))
    def _():
        backward()
        forward()
        query_grads()

    for i in range(XN - 1):
        hand_copy(r.d_put, r.d_got, 1, i).wait_recv()
    adjoints = [joined(r.d_got, h) for h in range(heads)]
    for h in range(heads):
        keys = parts(r.kr[h])
        solved = mm((r.x_hi[h], r.x_lo[h]), r.pg[h] + mm(keys, adjoints[h], NT), TN)
        r.solved[h] = solved
        d_value = r.cols[h, :, 0:1] * solved
        for j in range(NH):
            at = value_at + h * two + j * size
            r.g[:, at : at + size] = d_value[j * count : (j + 1) * count].astype(BF16)
        offer(1 + h)

    logits = []
    for h in range(heads):
        key = r.kr[h]
        beta, key_scale = r.cols[h, :, 0:1], r.cols[h, :, 1:2]
        solved, fresh, keys = r.solved[h], r.fresh[h], key.astype(BF16)
        d_system = jnp.where(strict, -mm1(solved, fresh, NT), 0.0)
        gram = dg(keys, keys, NT)
        d_beta = jnp.sum(solved * r.rest[h], axis=-1, keepdims=True) + jnp.sum(d_system * gram, axis=-1, keepdims=True)
        d_gram = (beta * d_system).astype(BF16)
        d_key = (
            r.dk[h]
            + dg(fresh, adjoints[h], NN)
            - mm1(beta * solved, joined(r.s_got, h))
            + dg(d_gram, keys, NN)
            + dg(d_gram, keys, TN)
        )
        d_key = key_scale * (d_key - key * jnp.sum(key * d_key, axis=-1, keepdims=True))
        d_logit = d_beta * beta * (1.0 - 0.5 * beta)
        for j in range(NH):
            at = key_at + h * two + j * size
            r.g[:, at : at + size] = d_key[j * count : (j + 1) * count].astype(BF16)
            logits.append(d_logit[j * count : (j + 1) * count])
    pad = jnp.zeros((count, size - len(logits)), F32)
    r.g[:, logit_at:] = jnp.concatenate(logits + [pad], axis=1).astype(BF16)
    offer(3)
    offer(4)

    def input_term(d, side):
        lo = pl.multiple_of((lax.rem(y + d, yn) * 2 + side) * block, block)
        spot = pl.ds(lo, block)
        total = dg(r.g[:, :value_at], r.wq[spot, :], NT)
        total = total + dg(r.g[:, value_at:key_at], r.wv[spot, :], NT)
        total = total + dg(r.g[:, key_at:logit_at], r.wk[spot, :], NT)
        return total + dg(r.g[:, logit_at : logit_at + heads * NH], r.wb[:, spot], NN)

    def pair_copy(d):
        return remote(r.pair_put.at[d], r.pair_got.at[d], r.csend.at[d], r.crecv.at[d], (seq, partner))

    def y_copy(d):
        i = d - 1
        device = (seq, lax.rem(y + d, yn) * 2 + core)
        return remote(r.y_put.at[i], r.y_got.at[i], r.ysend.at[i], r.yrecv.at[i], device)

    order = list(range(1, yn)) + [0]

    def partner_terms():
        for d in order:
            r.pair_put[d] = input_term(d, 1 - core).astype(BF16)
            pair_copy(d).start()

    def own_terms():
        for d in order:
            r.own_part[d] = input_term(d, core)

    def merge_terms():
        for d in order:
            pair_copy(d).wait_recv()
            term = r.own_part[d] + r.pair_got[d].astype(F32)
            if d:
                r.y_put[d - 1] = term.astype(BF16)
                y_copy(d).start()
            else:
                r.kept[...] = term

    def hops(p):
        return (zn // 2, zn // 2 - 1) if p % 2 == 0 else (zn // 2 - 1, zn // 2)

    def ring_hop(p, way, step):
        lo, hi = cuts[p]
        device = ((below if way else above) * XN + x, head)
        put, got = r.ring_put.at[way, step, :, lo:hi], r.ring_got.at[way, step, :, lo:hi]
        return remote(put, got, r.rsend.at[p, way, step], r.rrecv.at[p, way, step], device)

    def ring_step(p, step):
        lo, hi = cuts[p]
        if step == 0:
            onward_copy(p).wait_recv()
            left_side = r.tt[...].reshape(zn * shard, XN * count)
            r.part[:, :, lo:hi] = dg(left_side, r.gbuf[:, lo:hi], NN).reshape(zn, shard, hi - lo)
        lengths = hops(p)
        for way in range(2):
            length = lengths[way]
            if step >= length:
                continue
            chunk = lax.rem(z + zn + (step - length if way else length - step), zn)
            value = r.part[chunk, :, lo:hi]
            if step > 0:
                ring_hop(p, way, step - 1).wait_recv()
                value = value + r.ring_got[way, step - 1, :, lo:hi].astype(F32)
            r.ring_put[way, step, :, lo:hi] = value.astype(BF16)
            ring_hop(p, way, step).start()
        if step == max(lengths):
            value = r.part[z, :, lo:hi]
            for way in range(2):
                ring_hop(p, way, lengths[way] - 1).wait_recv()
                value = value + r.ring_got[way, lengths[way] - 1, :, lo:hi].astype(F32)
            r.gw[:, lo:hi] = value

    @pl.when(jnp.logical_not(early))
    def _():
        relay(0)

    partner_terms()
    relay(1)
    relay(2)
    for copy in tok_copies:
        copy.wait_recv()
    ring_step(0, 0)
    relay(3)
    ring_step(1, 0)
    ring_step(2, 0)
    relay(4)
    own_terms()
    for p in (0, 1, 2):
        ring_step(p, 1)
    ring_step(3, 0)
    ring_step(4, 0)
    for step in range(2, zn // 2 + 1):
        for p in (0, 1, 2):
            ring_step(p, step)
        if step == zn // 2:
            merge_terms()
        for p in (3, 4):
            ring_step(p, step - 1)
    for p in (3, 4):
        ring_step(p, zn // 2)

    total = r.kept[...]
    for d in range(1, yn):
        y_copy(d).wait_recv()
        total = total + r.y_got[d - 1].astype(F32)
    r.gx[...] = total.astype(BF16)

    for copy in started:
        copy.wait_send()

    @pl.when(z < zn - 2)
    def _():
        s_hop.wait_send()

    @pl.when(z >= 2)
    def _():
        d_hop.wait_send()

    for i in range(XN - 1):
        hand_copy(r.s_put, r.s_got, 0, i).wait_send()
        hand_copy(r.d_put, r.d_got, 1, i).wait_send()
    for p in range(len(cuts)):
        own_copy(p, 0).wait_send()
        own_copy(p, 1).wait_send()
        onward_copy(p).wait_send()
        for way in range(2):
            for step in range(hops(p)[way]):
                ring_hop(p, way, step).wait_send()
    for d in range(yn):
        pair_copy(d).wait_send()
        if d:
            y_copy(d).wait_send()


def finish_kernel(heads, gx_in, gw_in, gx, gwq, gwk, gwv, gwb):
    queries, steps = heads * HEAD_SIZE, heads * NH * HEAD_SIZE
    gx[...] = gx_in[...]
    gwq[...] = gw_in[:, :queries]
    gwv[...] = gw_in[:, queries : queries + steps]
    gwk[...] = gw_in[:, queries + steps : queries + 2 * steps]
    at = queries + 2 * steps
    gwb[...] = gw_in[:, at : at + 128].T[: heads * NH, :]


def vmem(count):
    return [pl.BlockSpec(memory_space=pltpu.VMEM)] * count


def per_device(tokens, w_query, w_key, w_value, w_beta, grad_out):
    count, depth = tokens.shape
    size = HEAD_SIZE
    heads = w_query.shape[1] // size
    rows = NH * count
    quarter = size // XN
    devices = lax.axis_size("seq")
    zn, yn = devices // XN, lax.axis_size("head") // 2
    shard, block = depth // devices, depth // (2 * yn)
    width = heads * (1 + 2 * NH) * size + 128
    pieces, hops = heads + 3, zn // 2
    w_beta_t = w_beta.T
    shape = jax.ShapeDtypeStruct
    dma = pltpu.SemaphoreType.DMA
    scratch = dict(
        tok=(tokens.shape, BF16),
        wk=(w_key.shape, BF16),
        wb=(w_beta_t.shape, BF16),
        wv=(w_value.shape, BF16),
        wq=(w_query.shape, BF16),
        go=(grad_out.shape, BF16),
        tokt=((zn, XN, shard, count), BF16),
        tt=((zn, shard, XN * count), BF16),
        system=((heads, rows, rows), F32),
        kr=((heads, rows, size), F32),
        vr=((heads, rows, size), F32),
        qr=((heads, count, size), F32),
        ur=((heads, rows, size), F32),
        pg=((heads, rows, size), F32),
        cols=((heads, rows, 8), F32),
        x_hi=((heads, rows, rows), BF16),
        x_lo=((heads, rows, rows), BF16),
        w_hi=((heads, rows, size), BF16),
        w_lo=((heads, rows, size), BF16),
        fresh=((heads, rows, size), BF16),
        rest=((heads, rows, size), F32),
        dk=((heads, rows, size), F32),
        solved=((heads, rows, size), F32),
        e_own=((heads, size, size), BF16),
        bl_own=((XN, heads, 2 * quarter, size), BF16),
        ebuf=((XN, heads, size, size), BF16),
        blbuf=((XN, heads, 2 * quarter, size), BF16),
        fz=((2, heads, size, size), BF16),
        sz=((2, heads, quarter, size), BF16),
        dz=((2, heads, quarter, size), BF16),
        pair=((heads, size, size), BF16),
        pair_t=((heads, size, size), BF16),
        s_mine=((heads, quarter, size), BF16),
        d_mine=((heads, quarter, size), BF16),
        e_pre=((heads, 3 * size, size), BF16),
        e_suf=((heads, size, 3 * size), BF16),
        s_off=((XN, heads, quarter, size), F32),
        d_off=((XN, heads, quarter, size), F32),
        s_in=((heads, quarter, size), BF16),
        d_in=((heads, quarter, size), BF16),
        s_out=((heads, quarter, size), BF16),
        d_out=((heads, quarter, size), BF16),
        s_put=((XN, heads, quarter, size), BF16),
        d_put=((XN, heads, quarter, size), BF16),
        s_got=((XN, heads, quarter, size), BF16),
        d_got=((XN, heads, quarter, size), BF16),
        g=((count, width), BF16),
        gbuf=((XN * count, width), BF16),
        part=((zn, shard, width), F32),
        ring_put=((2, hops, shard, width), BF16),
        ring_got=((2, hops, shard, width), BF16),
        pair_put=((yn, count, block), BF16),
        pair_got=((yn, count, block), BF16),
        y_put=((yn - 1, count, block), BF16),
        y_got=((yn - 1, count, block), BF16),
        own_part=((yn, count, block), F32),
        kept=((count, block), F32),
    )
    semaphores = dict(
        load_sem=(6,),
        tsend=(XN - 1,),
        trecv=(XN - 1,),
        esend=(heads, 3),
        erecv=(heads, 3),
        bsend=(XN - 1,),
        brecv=(XN - 1,),
        swap_send=(heads, 3),
        swap_recv=(heads, 3),
        zsend=(2,),
        zrecv=(2,),
        psend=(XN - 1, 2),
        precv=(XN - 1, 2),
        gsend=(pieces, 3),
        grecv=(pieces, 3),
        rsend=(pieces, 2, hops),
        rrecv=(pieces, 2, hops),
        csend=(yn,),
        crecv=(yn,),
        ysend=(yn - 1,),
        yrecv=(yn - 1,),
    )
    inputs = ("tok", "wq", "wk", "wv", "wb", "go")
    names = tuple(name + "_hbm" for name in inputs) + ("gx", "gw") + tuple(scratch) + tuple(semaphores)
    gx, gw = pl.pallas_call(
        functools.partial(layer_kernel, zn, yn, heads, names),
        out_shape=(shape((count, block), BF16), shape((shard, width), F32)),
        in_specs=[pl.BlockSpec(memory_space=pl.ANY)] * 6,
        out_specs=tuple(vmem(2)),
        scratch_shapes=[pltpu.VMEM(*spec) for spec in scratch.values()] + [dma(dims) for dims in semaphores.values()],
        compiler_params=pltpu.CompilerParams(collective_id=0, has_side_effects=True, vmem_limit_bytes=60 << 20),
        name="layer",
    )(tokens, w_query, w_key, w_value, w_beta_t, grad_out)
    outs = (
        shape((count, block), BF16),
        shape((shard, w_query.shape[1]), F32),
        shape((shard, w_key.shape[1]), F32),
        shape((shard, w_value.shape[1]), F32),
        shape((w_beta.shape[1], shard), F32),
    )
    grad_tokens, gwq, gwk, gwv, gwb = pl.pallas_call(
        functools.partial(finish_kernel, heads),
        out_shape=outs,
        in_specs=vmem(2),
        out_specs=tuple(vmem(5)),
        name="finish",
    )(gx, gw)
    return (grad_tokens, gwq, gwk, gwv, gwb.T)


def solution(mesh):
    in_specs = (
        P("seq", None),
        P(None, "head"),
        P(None, "head"),
        P(None, "head"),
        P(None, "head"),
        P("seq", "head"),
    )
    return jax.shard_map(
        per_device, mesh=mesh, in_specs=in_specs, out_specs=(P("seq", "head"),) * 5, check_vma=False
    )
```
